256 devices in a mesh: dp: 8 (over z), expert: 32 (over x, y, core).
Axes of the slice: x: 4, y: 4, z: 8, core: 2. Of those that a mesh axis runs over, the one named last changes fastest.
Arguments:
- tokens: bfloat16 [256, 212, 1024], P(('dp', 'expert')), may hold values from -6 to 6
- expert_ids: int32 [256, 212, 1], P(('dp', 'expert')), may hold values from 0 to 31; in each aligned block of 212 rows (0 to 211, 212 to 423, ..., all dimensions but the last counted through in order) at most 9 rows name the same one
- caption_lengths: int32 [256], P(('dp', 'expert')), may hold values from 1 to 16, as said below
- layer_norm_gain: float32 [1024], replicated, may hold values from 0.5 to 1.5
- router: float32 [1024, 32], replicated, may hold values from -0.1875 to 0.1875
- w_up: bfloat16 [32, 1024, 4096], P('expert', None, 'dp'), may hold values from -0.1875 to 0.1875
- w_down: bfloat16 [32, 4096, 1024], P('expert', 'dp'), may hold values from -0.09375 to 0.09375
- logit_scale: float32 [1], replicated, may hold values from 5 to 20
- logit_bias: float32 [1], replicated, may hold values from -4 to -1.5
Outputs:
- loss: float32 [1], replicated
- grad_tokens: bfloat16 [256, 212, 1024], P(('dp', 'expert'))
- grad_up: float32 [32, 1024, 4096], P('expert', None, 'dp')
- grad_down: float32 [32, 4096, 1024], P('expert', 'dp')
- grad_router: float32 [1024, 32], replicated
- layer_gain_gradient: float32 [1024], replicated
The draws below stay inside these ranges and needn't reach their ends.
Inputs may be any that keep to these rules, and one draw needn't show every extreme that they name: `expert_ids`: among the rows of one device (aligned blocks of 212 rows, devices ordered by dp then expert) no expert is named more than 9 times, a bound that some block reaches. `caption_lengths`: some caption has all 16 tokens.
All inputs are finite; a program needn't handle non-finite values.
Results may differ from the reference program's by a relative error of at most 0.009.
Values may be sent and summed in bfloat16 or wider, within the bound.
No kernel may reach another device: no remote copies, remote signals or barrier semaphores. Data moves between devices by JAX's collectives and lax.ppermute only.
A program may use at most 128 MiB of HBM per device.

```python
import math
import jax
import jax.numpy as jnp
import numpy as np
from jax import lax

D = 1024
FF = 4096
EXPERTS = 32
PATCH = 196
CAPLEN = 16
SEQ = 212
PAIR_DEV = 1
PAIRS = 256
CAP = 9
N_DP = 8
N_EXPERT = 32


def draw_caption_lengths(key, part):
    drawn = jax.random.randint(jax.random.fold_in(key, 17), (PAIRS,), 1, CAPLEN + 1).astype(jnp.int32)
    return drawn.at[0].set(CAPLEN)


def draw_tokens(key, part):
    groups = max(PAIRS // 8, 1)
    key_member = jax.random.fold_in(key, 101)
    key_center = jax.random.fold_in(key, 102)
    key_private = jax.random.fold_in(key, 103)
    key_noise = jax.random.fold_in(key, 104)
    member = jax.random.randint(key_member, (PAIRS,), 0, groups).astype(jnp.int32)
    member_table = (member[:, None] == jnp.arange(groups, dtype=jnp.int32)[None, :]).astype(jnp.float32)
    centers = jax.random.normal(key_center, (groups, D), jnp.float32)
    center_rows = jnp.dot(member_table, centers)
    private_part = jax.random.normal(key_private, (PAIRS, D), jnp.float32)
    shared_part = 0.6 * center_rows + 0.8 * private_part
    noise_part = jax.random.normal(key_noise, (PAIRS, SEQ, D), jnp.float32)
    result_rows = 0.6 * shared_part[:, None, :] + 0.8 * noise_part
    return jnp.clip(result_rows, -6.0, 6.0).astype(jnp.bfloat16)


def level_of(own_key, dims, pieces, least, largest):
    loudness, own = 1.0, jax.random.fold_in(own_key, 6)
    for dim, blocks in pieces:
        draws = jnp.exp(jax.random.uniform(jax.random.fold_in(own, dim), (blocks,), jnp.float32, least / len(pieces), largest / len(pieces)))
        loudness = loudness * jnp.repeat(draws, dims[dim] // blocks).reshape([-1 if axis == dim else 1 for axis in range(len(dims))])
    return loudness


def deal_out(stream_key, own, number, rows, count, top, most, lean):
    order = jax.random.permutation(stream_key, count)
    packed, ordinary = shares(count, rows * top, most, lean, True), shares(count, rows * top, most, lean, False)
    places = jnp.arange(count)

    def named(sizes, turn):
        used = int((sizes > 0).sum())
        fixed = max(1, used // 4)
        moved = fixed + (places - fixed + turn * (used - fixed)) % max(1, count - fixed)
        return jnp.zeros((count,), jnp.int32).at[order[jnp.where(places < fixed, places, moved)]].set(jnp.asarray(sizes, jnp.int32))

    sizes = jnp.where(number % 4 == 0, named(packed, number // 4), named(ordinary, number - number // 4 - 1))
    mixed = jax.random.permutation(jax.random.fold_in(own, 3), count)
    donor, receiver = mixed[0:count // 2 * 2:2], mixed[1:count // 2 * 2:2]
    slack = jnp.minimum(sizes[donor] - 1, most - sizes[receiver]) // 2
    slack = jnp.where((donor == order[0]) | (receiver == order[0]) | (sizes[receiver] == 0), 0, jnp.maximum(slack, 0))
    moved = jax.random.randint(jax.random.fold_in(own, 4), (count // 2,), 0, 1 << 20) % (slack + 1)
    sizes = sizes.at[donor].add(-moved).at[receiver].add(moved)
    members = jnp.searchsorted(jnp.cumsum(sizes), jnp.arange(rows * top), side="right").astype(jnp.int32)
    table = members.reshape(top, rows).T
    table = table[jax.random.permutation(jax.random.fold_in(own, 1), rows)]
    turn = jax.random.randint(jax.random.fold_in(own, 2), (rows, 1), 0, top)
    return jnp.take_along_axis(table, (jnp.arange(top)[None, :] + turn) % top, axis=1)


def shares(number_of, total, most, lean, full):
    weights = [(1 << 20) // math.isqrt(rank ** lean) + 1 for rank in range(1, number_of + 1)]
    largest = most if full else min(most, max(-(-total // number_of), total * weights[0] // sum(weights)))
    least = 1 if total - largest >= number_of - 1 else 0
    counts, surplus = [largest] + [least] * (number_of - 1), total - largest - least * (number_of - 1)
    while surplus > 0:
        free = [i for i in range(1, number_of) if counts[i] < largest] or [i for i in range(1, number_of) if counts[i] < most]
        mass, remaining = sum([weights[i] for i in free]), surplus
        for i in free:
            more = min(most - counts[i], max(1, remaining * weights[i] // mass), surplus)
            counts[i] = counts[i] + more
            surplus = surplus - more
    return np.array(counts)


def bell_draw(stream_key, shape, spread, reach, split=(), held_as=jnp.bfloat16):
    entries = jax.random.normal(stream_key, shape, jnp.float32) * spread
    if len(split) > 0:
        entries = level_of(stream_key, shape, split, -0.22, 0.18) * entries
    return jnp.clip(entries, min=-reach, max=reach).astype(held_as)


def setup_inputs(seed: int = 0) -> dict:
    key_of = jax.random.split(jax.random.key(seed), 10)
    tokens = draw_tokens(jax.random.fold_in(key_of[9], 71), 0)
    expert_ids_keys = jax.random.split(jax.random.fold_in(key_of[1], 1), PAIRS * SEQ // (PAIR_DEV * SEQ))
    expert_ids_turns = jax.random.permutation(jax.random.fold_in(key_of[1], 3), PAIRS * SEQ // (PAIR_DEV * SEQ))
    expert_ids = jax.vmap(lambda own, number: deal_out(jax.random.fold_in(key_of[1], 2), own, number, PAIR_DEV * SEQ, EXPERTS, 1, CAP, 2))(expert_ids_keys, expert_ids_turns).reshape((PAIRS, SEQ, 1))
    caption_lengths = draw_caption_lengths(jax.random.fold_in(key_of[9], 71), 0)
    layer_norm_gain = jnp.clip(1.0 + 0.1 * jax.random.normal(key_of[3], (D,), jnp.float32), 0.5, 1.5)
    router = bell_draw(key_of[4], (D, EXPERTS), D ** -0.5, 0.1875, (), jnp.float32)
    w_up = bell_draw(key_of[5], (EXPERTS, D, FF), D ** -0.5, 0.1875, ((0, 32), (2, 8)))
    w_down = bell_draw(key_of[6], (EXPERTS, FF, D), FF ** -0.5, 0.09375, ((0, 32), (1, 8)))
    logit_scale = jnp.clip(jnp.exp(jax.random.uniform(key_of[7], (1,), jnp.float32, math.log(5.0), math.log(20.0))), 5.0, 20.0)
    logit_bias = jnp.clip(jax.random.uniform(key_of[8], (1,), jnp.float32, -4.0, -1.5), -4.0, -1.5)
    return {"tokens": tokens, "expert_ids": expert_ids, "caption_lengths": caption_lengths, "layer_norm_gain": layer_norm_gain, "router": router, "w_up": w_up, "w_down": w_down, "logit_scale": logit_scale, "logit_bias": logit_bias}


eps = 1e-06
loss_scale = 1024.0

def gelu_slope(pre):
    return 0.5 * (1.0 + lax.erf(pre * 0.7071067811865476)) + pre * jnp.exp(-0.5 * pre * pre) * 0.3989422804014327

def group_sum(parts):
    rounded = lax.optimization_barrier(parts.astype(jnp.bfloat16))
    return lax.optimization_barrier(jnp.sum(rounded.astype(jnp.float32), axis=0)).astype(jnp.bfloat16)

def reference(tokens, expert_ids, caption_lengths, layer_norm_gain, router, w_up, w_down, logit_scale, logit_bias):
    devices = N_DP * N_EXPERT
    rows_dev = PAIR_DEV * SEQ
    total = PAIRS * SEQ
    ffd = FF // N_DP
    input_rows = tokens.reshape(total, D).astype(jnp.float32)
    input_mean = lax.optimization_barrier(jnp.mean(input_rows, axis=1, keepdims=True))
    var_x = lax.optimization_barrier(jnp.mean((input_rows - input_mean) ** 2, axis=1, keepdims=True))
    inverse_deviation = 1.0 / jnp.sqrt(var_x + eps)
    centered_scaled_input = (input_rows - input_mean) * inverse_deviation
    normalized_input = (centered_scaled_input * layer_norm_gain).astype(jnp.bfloat16)
    ids = expert_ids.reshape(total).astype(jnp.int32)
    onehot = (ids[:, None] == jnp.arange(EXPERTS, dtype=jnp.int32)[None, :]).astype(jnp.int32)
    blocks = onehot.reshape(devices, rows_dev, EXPERTS)
    slot = lax.optimization_barrier(jnp.sum((jnp.cumsum(blocks, axis=1) - 1) * blocks, axis=2)).reshape(total)
    owner = jnp.arange(total, dtype=jnp.int32) // rows_dev
    dest = ids * (devices * CAP) + owner * CAP + slot
    xe = jnp.zeros((EXPERTS * devices * CAP, D), jnp.bfloat16).at[dest].set(normalized_input).reshape(EXPERTS, devices * CAP, D)

    def forward_one(operands):
        rows, wu, wd = operands
        pre = jnp.dot(rows, wu, preferred_element_type=jnp.float32)
        act = jax.nn.gelu(pre, approximate=False).astype(jnp.bfloat16)
        parts = jnp.einsum('rqf,qfd->qrd', act.astype(jnp.float32).reshape(-1, N_DP, ffd), wd.astype(jnp.float32).reshape(N_DP, ffd, D))
        return group_sum(parts)
    out_e = lax.map(forward_one, (xe, w_up, w_down))
    moe = out_e.reshape(-1, D)[dest].astype(jnp.float32)
    xnf = normalized_input.astype(jnp.float32)
    router_logits = jnp.dot(xnf, router, precision=lax.Precision.HIGHEST)
    gate = jax.nn.sigmoid(lax.optimization_barrier(jnp.sum(router_logits * onehot.astype(jnp.float32), axis=1)))
    y = (input_rows + gate[:, None] * moe).reshape(PAIRS, SEQ, D)
    img = lax.optimization_barrier(jnp.mean(y[:, :PATCH], axis=1))
    lengths = caption_lengths.astype(jnp.float32)
    mask = (jnp.arange(CAPLEN, dtype=jnp.int32)[None, :] < caption_lengths[:, None]).astype(jnp.float32)
    txt = lax.optimization_barrier(jnp.sum(y[:, PATCH:] * mask[:, :, None], axis=1)) / lengths[:, None]
    ru = jnp.sqrt(lax.optimization_barrier(jnp.mean(img * img, axis=1, keepdims=True)) + eps)
    rv = jnp.sqrt(lax.optimization_barrier(jnp.mean(txt * txt, axis=1, keepdims=True)) + eps)
    u = img / ru
    v = txt / rv
    scale = logit_scale[0]
    logits = scale * jnp.dot(u, v.T, precision=lax.Precision.HIGHEST) / D + logit_bias[0]
    sign = 2.0 * jnp.eye(PAIRS, dtype=jnp.float32) - 1.0
    loss = -jnp.sum(jax.nn.log_sigmoid(sign * logits)) / PAIRS
    coef = -(loss_scale / PAIRS) * sign * jax.nn.sigmoid(-sign * logits)
    du = scale / D * jnp.dot(coef, v, precision=lax.Precision.HIGHEST)
    dv = scale / D * jnp.dot(coef.T, u, precision=lax.Precision.HIGHEST)
    dimg = (du - u * lax.optimization_barrier(jnp.mean(du * u, axis=1, keepdims=True))) / ru
    dtxt = (dv - v * lax.optimization_barrier(jnp.mean(dv * v, axis=1, keepdims=True))) / rv
    dy_img = jnp.broadcast_to(dimg[:, None, :] / PATCH, (PAIRS, PATCH, D))
    dy_txt = (dtxt / lengths[:, None])[:, None, :] * mask[:, :, None]
    dy = jnp.concatenate([dy_img, dy_txt], axis=1).reshape(total, D)
    dmoe = (gate[:, None] * dy).astype(jnp.bfloat16)
    dgl = lax.optimization_barrier(jnp.sum(dy * moe, axis=1)) * gate * (1.0 - gate)
    grad_router = jnp.dot(xnf.T, onehot.astype(jnp.float32) * dgl[:, None], precision=lax.Precision.HIGHEST)
    dme = jnp.zeros((EXPERTS * devices * CAP, D), jnp.bfloat16).at[dest].set(dmoe).reshape(EXPERTS, devices * CAP, D)

    def backward_one(operands):
        rows, grads, wu, wd = operands
        pre = jnp.dot(rows, wu, preferred_element_type=jnp.float32)
        act = jax.nn.gelu(pre, approximate=False).astype(jnp.bfloat16)
        dact = jnp.dot(grads, wd.T, preferred_element_type=jnp.float32)
        dpre = (dact * gelu_slope(pre)).astype(jnp.bfloat16)
        g_down = jnp.dot(act.T, grads, preferred_element_type=jnp.float32)
        g_up = jnp.dot(rows.T, dpre, preferred_element_type=jnp.float32)
        parts = jnp.einsum('rqf,dqf->qrd', dpre.astype(jnp.float32).reshape(-1, N_DP, ffd), wu.astype(jnp.float32).reshape(D, N_DP, ffd))
        return (g_up, g_down, group_sum(parts))
    grad_up, grad_down, dxe = lax.map(backward_one, (xe, dme, w_up, w_down))
    router_rows = jnp.dot(onehot.astype(jnp.float32), router.T, precision=lax.Precision.HIGHEST)
    gradient_normalized_input = dxe.reshape(-1, D)[dest].astype(jnp.float32) + dgl[:, None] * router_rows
    layer_gain_gradient = lax.optimization_barrier(jnp.sum(gradient_normalized_input * centered_scaled_input, axis=0))
    scaled_output_gradient = gradient_normalized_input * layer_norm_gain
    normed_input_gradient = (scaled_output_gradient - lax.optimization_barrier(jnp.mean(scaled_output_gradient, axis=1, keepdims=True)) - centered_scaled_input * lax.optimization_barrier(jnp.mean(scaled_output_gradient * centered_scaled_input, axis=1, keepdims=True))) * inverse_deviation
    grad_tokens = (dy + normed_input_gradient).astype(jnp.bfloat16).reshape(PAIRS, SEQ, D)
    return (loss.reshape(1), grad_tokens, grad_up, grad_down, grad_router, layer_gain_gradient)
```

```python
import jax
import jax.numpy as jnp
from jax import lax
from jax.sharding import PartitionSpec as P

D = 1024
PATCH = 196
CAPLEN = 16
SEQ = 212
SLOTS = 9
META = 8

EPS = 1e-06
LOSS_SCALE = 1024.0
BF = jnp.bfloat16
F32 = jnp.float32


def mm(a, b, dims=((1,), (0,))):
    return lax.dot_general(a, b, (dims, ((), ())), preferred_element_type=F32)


def front(x, ids, length, gain, experts):
    mean = jnp.mean(x, axis=1, keepdims=True)
    var = jnp.mean((x - mean) ** 2, axis=1, keepdims=True)
    rstd = 1.0 / jnp.sqrt(var + EPS)
    xhat = (x - mean) * rstd
    xn = (xhat * gain).astype(BF)
    pos = jnp.arange(SEQ, dtype=jnp.int32)
    real = pos < PATCH + length
    onehot = ((ids[:, None] == jnp.arange(experts, dtype=jnp.int32)[None, :]) & real[:, None]).astype(BF)
    before = (pos[None, :] < pos[:, None]).astype(BF)
    slot = jnp.sum(mm(before, onehot) * onehot.astype(F32), axis=1).astype(jnp.int32)
    target = jnp.where(real, ids * SLOTS + slot, -1)
    place = (jnp.arange(experts * SLOTS, dtype=jnp.int32)[:, None] == target[None, :]).astype(BF)
    images = jnp.sum(onehot[:PATCH].astype(F32), axis=0)
    return xhat, rstd, xn, place, images


def body(tokens, expert_ids, caption_lengths, gain, router, w_up, w_down, logit_scale, logit_bias):
    n_dp = lax.axis_size("dp")
    n_ex = lax.axis_size("expert")
    experts = router.shape[1]
    pairs = n_dp * n_ex
    me_dp = lax.axis_index("dp")
    me_ex = lax.axis_index("expert")
    rows = n_ex * SLOTS
    wu = w_up[0]
    wd = w_down[0]
    x = tokens[0].astype(F32)
    length = caption_lengths[0]
    xhat, rstd, xn, place, images = front(x, expert_ids.reshape(SEQ), length, gain, experts)
    cap_w = jnp.where(jnp.arange(CAPLEN) < length, 1.0 / length.astype(F32), 0.0)
    x_means = jnp.stack([jnp.mean(x[:PATCH], axis=0), jnp.sum(x[PATCH:] * cap_w[:, None], axis=0)])

    buffer = mm(place, xn).astype(BF).reshape(experts, SLOTS, D)
    col = jnp.arange(D, dtype=jnp.int32)[None, :]
    meta = jnp.where(col == 0, images[:, None], jnp.where(col == 1, length.astype(F32), 0.0)).astype(BF)
    buffer = jnp.concatenate([buffer, meta[:, None, :]], axis=1)
    got = lax.all_to_all(buffer, "expert", split_axis=0, concat_axis=0, tiled=True)
    own_rows = got[:, :SLOTS].reshape(rows, D)
    own_meta = jnp.concatenate([got[:, SLOTS, 0], got[:, SLOTS, 1]])
    own_meta = jnp.pad(own_meta[None, :], ((0, META - 1), (0, D - 2 * n_ex)))
    own = jnp.concatenate([own_rows, own_meta], axis=0)
    height = rows + META

    right = [(i, (i + 1) % n_dp) for i in range(n_dp)]
    left = [(i, (i - 1) % n_dp) for i in range(n_dp)]
    half = n_dp // 2
    cut = rows // 2
    r, l = own, own
    blocks = [own]
    offsets = [0]
    for k in range(1, half):
        r = lax.ppermute(r, "dp", right)
        l = lax.ppermute(l, "dp", left)
        blocks += [r, l]
        offsets += [-k, k]
    r = lax.ppermute(r[:cut], "dp", right)
    l = lax.ppermute(l[cut:], "dp", left)
    blocks.append(jnp.concatenate([r, l], axis=0))
    offsets.append(half)

    mine = jnp.arange(experts, dtype=jnp.int32) == me_ex
    router_col = jnp.sum(jnp.where(mine[None, :], router, 0.0), axis=1)

    row = jnp.arange(height, dtype=jnp.int32)
    row_ex = row // SLOTS
    row_slot = row % SLOTS
    glob = jnp.arange(2 * pairs, dtype=jnp.int32)
    saved = []
    pooled = 0.0
    len_glob = 0.0
    for xb, off in zip(blocks, offsets):
        src = (me_dp + off) % n_dp
        n_img = xb[rows, :n_ex].astype(F32)
        lens = xb[rows, n_ex : 2 * n_ex].astype(F32)
        pick = (row_ex[:, None] == jnp.arange(n_ex, dtype=jnp.int32)[None, :]).astype(F32)
        row_img = jnp.sum(pick * n_img[None, :], axis=1)
        kind = jnp.where(row_slot.astype(F32) < row_img, 0, 1)
        pt = jnp.where(row < rows, (row_ex * n_dp + src) * 2 + kind, -1)
        sel = (glob[:, None] == pt[None, :]).astype(BF)
        pick_len = (glob[:, None] // 2 == (jnp.arange(n_ex, dtype=jnp.int32) * n_dp + src)[None, :]).astype(F32)
        len_glob = len_glob + jnp.sum(pick_len * lens[None, :], axis=1)
        pre = mm(xb, wu)
        phi = 0.5 * (1.0 + lax.erf(pre * 0.7071067811865476))
        act = (pre * phi).astype(BF)
        slope = phi + pre * jnp.exp(-0.5 * pre * pre) * 0.3989422804014327
        gate = jax.nn.sigmoid(jnp.sum(xb.astype(F32) * router_col[None, :], axis=1, keepdims=True))
        pooled = pooled + mm(sel, (gate * act.astype(F32)).astype(BF))
        saved.append((xb, sel, act, slope, gate))
    weight = jnp.where(glob % 2 == 0, 1.0 / PATCH, 1.0 / len_glob)[:, None]
    part = mm((pooled * weight).astype(BF), wd).astype(BF)

    part = lax.all_to_all(part.reshape(n_ex, 2 * n_dp, D), "expert", split_axis=0, concat_axis=0, tiled=True)
    col_sum = jnp.sum(part.astype(F32), axis=0)
    which = jnp.arange(n_dp, dtype=jnp.int32) == me_dp
    col_sum = col_sum + jnp.where(which[:, None, None], x_means[None], 0.0).reshape(2 * n_dp, D)
    col_all = jnp.broadcast_to(col_sum.astype(BF)[None], (n_dp, 2 * n_dp, D))
    col_all = lax.all_to_all(col_all, "dp", split_axis=0, concat_axis=0, tiled=True)
    col_done = jnp.sum(col_all.astype(F32), axis=0).astype(BF)
    emb = lax.all_to_all(
        jnp.broadcast_to(col_done[None], (n_ex, 2 * n_dp, D)), "expert", split_axis=0, concat_axis=0, tiled=True
    ).reshape(2 * pairs, D)

    scale = logit_scale[0]
    embf = emb.astype(F32)
    inv = 1.0 / jnp.sqrt(jnp.mean(embf * embf, axis=1, keepdims=True) + EPS)
    logits = scale / D * mm(emb, emb, ((1,), (1,))) * inv * inv.reshape(1, -1) + logit_bias[0]
    same = (glob[:, None] // 2) == (glob[None, :] // 2)
    cross = (glob[:, None] % 2) != (glob[None, :] % 2)
    sign = jnp.where(same, 1.0, -1.0)
    signed = sign * logits
    upper = cross & (glob[:, None] % 2 == 0)
    loss = -jnp.sum(jnp.where(upper, jax.nn.log_sigmoid(signed), 0.0)) / pairs
    coef = jnp.where(cross, -(LOSS_SCALE / pairs) * sign * jax.nn.sigmoid(-signed), 0.0)
    coef = coef * inv.reshape(1, -1) * (scale / D)
    high = lax.reduce_precision(coef, 8, 7)
    low = coef - high
    d_emb = mm(high.astype(BF), emb) + mm(low.astype(BF), emb)
    unit = embf * inv
    dy_glob = (d_emb - unit * jnp.mean(d_emb * unit, axis=1, keepdims=True)) * inv * weight
    dy_own = lax.dynamic_slice(dy_glob, ((me_ex * n_dp + me_dp) * 2, 0), (2, D))
    dyb = dy_glob.astype(BF)
    q = mm(dyb, wd, ((1,), (1,))).astype(BF)
    grad_down = mm(pooled.astype(BF), dyb, ((0,), (0,)))

    backs = {}
    grad_up = 0.0
    g_router = 0.0
    for (xb, sel, act, slope, gate), off in reversed(list(zip(saved, offsets))):
        dact = mm(sel, q, ((0,), (0,))) * gate
        dpre = (dact * slope).astype(BF)
        dgl = (1.0 - gate) * jnp.sum(dact * act.astype(F32), axis=1, keepdims=True)
        back = mm(dpre, wu, ((1,), (1,))) + dgl * router_col[None, :]
        backs[off] = back[:rows]
        grad_up = grad_up + mm(xb, dpre, ((0,), (0,)))
        g_router = g_router + jnp.sum(xb.astype(F32) * dgl, axis=0)
    g_gain = jnp.sum(grad_up * wu.astype(F32), axis=1) + g_router * router_col

    r = backs[half][:cut].astype(BF)
    l = backs[half][cut:].astype(BF)
    for k in range(half - 1, -1, -1):
        r = lax.ppermute(r, "dp", right)
        l = lax.ppermute(l, "dp", left)
        if k == half - 1:
            r = jnp.concatenate([r.astype(F32) + backs[k][:cut], backs[k][cut:]], axis=0).astype(BF)
            l = jnp.concatenate([backs[-k][:cut], l.astype(F32) + backs[-k][cut:]], axis=0).astype(BF)
        elif k > 0:
            r = (r.astype(F32) + backs[k]).astype(BF)
            l = (l.astype(F32) + backs[-k]).astype(BF)
    dxe = (r.astype(F32) + l.astype(F32) + backs[0]).astype(BF)

    small = jnp.broadcast_to(jnp.stack([g_router, g_gain])[None], (n_dp, 2, D))
    small = jnp.sum(lax.all_to_all(small, "dp", split_axis=0, concat_axis=0, tiled=True), axis=0).astype(BF)
    send = jnp.concatenate([dxe.reshape(n_ex, SLOTS, D), jnp.broadcast_to(small[None], (n_ex, 2, D))], axis=1)
    ret = lax.all_to_all(send, "expert", split_axis=0, concat_axis=0, tiled=True)
    grad_router = ret[:, SLOTS].astype(F32).T
    gain_grad = jnp.sum(ret[:, SLOTS + 1].astype(F32), axis=0) / gain
    dxn = mm(place, ret[:, :SLOTS].reshape(experts * SLOTS, D), ((0,), (0,)))

    pos = jnp.arange(SEQ, dtype=jnp.int32)[:, None]
    dy = jnp.where(pos < PATCH, dy_own[:1], jnp.where(pos < PATCH + length, dy_own[1:], 0.0))
    g = dxn * gain
    dx = (g - jnp.mean(g, axis=1, keepdims=True) - xhat * jnp.mean(g * xhat, axis=1, keepdims=True)) * rstd
    grad_tokens = (dy + dx).astype(BF)[None]
    return (loss.reshape(1), grad_tokens, grad_up[None], grad_down[None], grad_router, gain_grad)


def solution(mesh):
    return jax.shard_map(
        body,
        mesh=mesh,
        in_specs=(
            P(("dp", "expert"), None, None),
            P(("dp", "expert"), None, None),
            P(("dp", "expert")),
            P(),
            P(),
            P("expert", None, "dp"),
            P("expert", "dp", None),
            P(),
            P(),
        ),
        out_specs=(
            P(),
            P(("dp", "expert"), None, None),
            P("expert", None, "dp"),
            P("expert", "dp", None),
            P(),
            P(),
        ),
        check_vma=False,
    )
```

```python
import functools

import jax
import jax.numpy as jnp
from jax import lax
from jax.experimental import pallas as pl
from jax.experimental.pallas import tpu as pltpu
from jax.sharding import PartitionSpec as P

D = 1024
FD = 512
PATCH = 196
CAPLEN = 16
SEQ = 212
NDP = 8
NEX = 32
MAIN = NEX * 8
ROWS = NEX * 9
META = 8
HEIGHT = ROWS + META
CUT = ROWS // 2
LANES = 384
FOLD = D
EXTRA = D + 128
SEND_W = D + 256
BACK_W = D + 384
PT = 2 * NDP * NEX
LOCAL = 2 * NEX

EPS = 1e-06
LOSS_SCALE = 1024.0
BF = jnp.bfloat16
F32 = jnp.float32
I32 = jnp.int32

VM = pl.BlockSpec(memory_space=pltpu.VMEM)
SM = pl.BlockSpec(memory_space=pltpu.SMEM)


def mm(a, b, dims=((1,), (0,))):
    return lax.dot_general(a, b, (dims, ((), ())), preferred_element_type=F32)


def io(shape, axis):
    return lax.broadcasted_iota(I32, shape, axis)


def run(kernel, outs, *args, smem=0, scratch=(), name=None):
    specs = [SM] * smem + [VM] * (len(args) - smem)
    return pl.pallas_call(
        kernel,
        out_shape=outs,
        in_specs=specs,
        out_specs=jax.tree.map(lambda _: VM, outs),
        scratch_shapes=scratch,
        name=name,
        compiler_params=pltpu.CompilerParams(vmem_limit_bytes=32 * 1024 * 1024),
    )(*args)


def shape(*dims, dtype=BF):
    return jax.ShapeDtypeStruct(dims, dtype)


def spread(k):
    return (io((MAIN, NEX), 0) == io((MAIN, NEX), 1) * 8 + k).astype(BF)


def layer_norm(x):
    mean = jnp.mean(x, axis=1, keepdims=True)
    c = x - mean
    rstd = 1.0 / jnp.sqrt(jnp.mean(c * c, axis=1, keepdims=True) + EPS)
    return c * rstd, rstd


def front_kernel(length, tok, ids, gain, send, means, place):
    n = length[0]
    x = tok[...].astype(F32)
    xhat, _ = layer_norm(x)
    xn = (xhat * gain[...]).astype(BF)
    pos = io((1, SEQ), 1)
    real = pos < PATCH + n
    owner = ids[...]
    hit = (io((NEX, SEQ), 0) == owner) & real
    onehot = jnp.where(hit, 1.0, 0.0)
    before = (io((SEQ, SEQ), 0) < io((SEQ, SEQ), 1)).astype(BF)
    slot = jnp.sum(mm(onehot.astype(BF), before) * onehot, axis=0, keepdims=True).astype(I32)
    target = jnp.where(real & (slot < 8), owner * 8 + slot, -1)
    p_main = (io((MAIN, SEQ), 0) == target).astype(BF)
    p_last = jnp.where(slot == 8, onehot, 0.0).astype(BF)
    place[:MAIN] = p_main
    place[MAIN:] = p_last
    send[:, :D] = mm(p_main, xn).astype(BF)
    last = mm(p_last, xn).astype(BF)
    fold = mm(spread(0), last[:, :128])
    for k in range(1, 8):
        fold = fold + mm(spread(k), last[:, 128 * k : 128 * (k + 1)])
    send[:, FOLD:EXTRA] = fold.astype(BF)
    images = jnp.sum(jnp.where(pos < PATCH, onehot, 0.0), axis=1, keepdims=True)
    lane = io((NEX, 128), 1)
    info = jnp.where(lane == 0, images, jnp.where(lane == 1, n.astype(F32), 0.0)).astype(BF)
    send[:, EXTRA:] = mm(spread(0), info).astype(BF)
    at = io((SEQ, 1), 0)
    w_img = jnp.where(at < PATCH, 1.0 / PATCH, 0.0)
    w_cap = jnp.where((at >= PATCH) & (at < PATCH + n), 1.0 / n.astype(F32), 0.0)
    means[0:1] = jnp.sum(x * w_img, axis=0, keepdims=True)
    means[1:2] = jnp.sum(x * w_cap, axis=0, keepdims=True)


def unpack_kernel(got, block):
    block[:MAIN] = got[:, :D]
    info = mm(spread(0), got[:, EXTRA:SEND_W], ((0,), (0,)))
    fold = got[:, FOLD:EXTRA]
    for k in range(8):
        block[MAIN:ROWS, 128 * k : 128 * (k + 1)] = mm(spread(k), fold, ((0,), (0,))).astype(BF)
    r = io((1, LANES), 1)
    ex = jnp.where(r < MAIN, r // 8, r - MAIN)
    slot = jnp.where(r < MAIN, r % 8, 8).astype(F32)
    match = io((NEX, LANES), 0) == ex
    images = jnp.sum(jnp.where(match, info[:, 0:1], 0.0), axis=0, keepdims=True)
    lens = jnp.sum(jnp.where(match, info[:, 1:2], 0.0), axis=0, keepdims=True)
    is_img = slot < images
    pt = jnp.where(r < ROWS, 2 * ex + jnp.where(is_img, 0, 1), LOCAL).astype(F32)
    div = jnp.where(r < ROWS, jnp.where(is_img, float(PATCH), lens), 1.0)
    sub = io((META, LANES), 0)
    block[ROWS:, :LANES] = jnp.where(sub == 0, pt, jnp.where(sub == 1, div, 0.0)).astype(BF)
    block[ROWS:, LANES:] = jnp.zeros((META, D - LANES), BF)


CHUNK = 32


def forward_kernel(x, wu, router, act, slope, cols, pooled, pre, mixed):
    pre[...] = mm(x[:ROWS], wu[...])
    meta = x[ROWS:, :LANES].astype(F32)
    pt_row = meta[0:1]
    div_row = meta[1:2]

    def step(c, _):
        at = pl.ds(pl.multiple_of(c * CHUNK, CHUNK), CHUNK)
        xc = x[at, :].astype(F32)
        gate = jax.nn.sigmoid(jnp.sum(xc * router[...], axis=1, keepdims=True))
        diag = io((CHUNK, LANES), 1) == io((CHUNK, LANES), 0) + c * CHUNK
        div = jnp.sum(jnp.where(diag, div_row, 0.0), axis=1, keepdims=True)
        pt = jnp.sum(jnp.where(diag, pt_row, 0.0), axis=1, keepdims=True)
        scaled = gate / div
        p = pre[at, :]
        phi = 0.5 * (1.0 + lax.erf(p * 0.7071067811865476))
        a = (p * phi).astype(BF)
        act[at, :] = a
        slope[at, :] = (phi + p * jnp.exp(-0.5 * p * p) * 0.3989422804014327).astype(BF)
        mixed[at, :] = (scaled * a.astype(F32)).astype(BF)
        lane = io((CHUNK, 128), 1)
        cols[at, :] = jnp.where(lane == 0, scaled, jnp.where(lane == 1, 1.0 - gate, jnp.where(lane == 2, pt, 0.0)))
        return 0

    lax.fori_loop(0, ROWS // CHUNK, step, 0)
    sel = (io((LOCAL, ROWS), 0).astype(F32) == pt_row[:, :ROWS]).astype(BF)
    pooled[...] = mm(sel, mixed[...]).astype(BF)


def forward_block(x, wu, router):
    return run(
        forward_kernel,
        (shape(ROWS, FD), shape(ROWS, FD), shape(ROWS, 128, dtype=F32), shape(LOCAL, FD)),
        x,
        wu,
        router,
        scratch=[pltpu.VMEM((ROWS, FD), F32), pltpu.VMEM((ROWS, FD), BF)],
        name="expert_forward",
    )


def part_kernel(offsets, me, *refs):
    wd, part, pooled = refs[NDP:]
    total = None
    g = io((PT, LOCAL), 0)
    p = io((PT, LOCAL), 1)
    for ref, off in zip(refs[:NDP], offsets):
        src = (me[0] + off) % NDP
        perm = (g == (p // 2) * (2 * NDP) + src * 2 + p % 2).astype(BF)
        term = mm(perm, ref[...])
        total = term if total is None else total + term
    pooled[...] = total.astype(BF)
    part[...] = mm(pooled[...], wd[...]).astype(BF)


def column_kernel(me, got, means, out):
    s = jnp.sum(got[...].astype(F32), axis=0)
    row = io((2 * NDP, 1), 0)
    own = row // 2 == me[0]
    s = s + jnp.where(own & (row % 2 == 0), means[0:1], 0.0) + jnp.where(own & (row % 2 == 1), means[1:2], 0.0)
    out[...] = jnp.broadcast_to(s.astype(BF)[None], (NDP, 2 * NDP, D))


def share_kernel(got, out):
    s = jnp.sum(got[...].astype(F32), axis=0)
    out[...] = jnp.broadcast_to(s.astype(BF)[None], (NEX, 2 * NDP, D))


def loss_kernel(me, scale, bias, emb, wd, loss, d_emb, dy, q, dots, inv_col, high, low, grads):
    e = emb[...]
    dots[...] = mm(e, e, ((1,), (1,)))
    to_unit = scale[0] / D
    step_rows = 64
    steps = PT // step_rows

    def norms(c, row_sum):
        at = pl.ds(pl.multiple_of(c * step_rows, step_rows), step_rows)
        diag = io((step_rows, PT), 1) == io((step_rows, PT), 0) + c * step_rows
        on = jnp.where(diag, dots[at, :], 0.0)
        inv = 1.0 / jnp.sqrt(jnp.sum(on, axis=1, keepdims=True) / D + EPS)
        inv_col[at, :] = jnp.broadcast_to(inv, (step_rows, 128))
        return row_sum + jnp.sum(on, axis=0, keepdims=True)

    squares = lax.fori_loop(0, steps, norms, jnp.zeros((1, PT), F32))
    inv_row = 1.0 / jnp.sqrt(squares / D + EPS)

    def terms(c, total):
        at = pl.ds(pl.multiple_of(c * step_rows, step_rows), step_rows)
        i = io((step_rows, PT), 0) + c * step_rows
        j = io((step_rows, PT), 1)
        same = i // 2 == j // 2
        sign = jnp.where(same, 1.0, -1.0)
        cross = i % 2 != j % 2
        z = sign * (dots[at, :] * to_unit * inv_col[at, 0:1] * inv_row + bias[0])
        t = jnp.exp(-jnp.abs(z))
        soft = jnp.maximum(-z, 0.0) + jnp.log1p(t)
        sig = jnp.where(z >= 0.0, t, 1.0) / (1.0 + t)
        coef = jnp.where(cross, (-LOSS_SCALE / (PT // 2)) * sign * sig, 0.0) * inv_row * to_unit
        hi = coef.astype(BF)
        high[at, :] = hi
        low[at, :] = (coef - hi.astype(F32)).astype(BF)
        return total + jnp.sum(jnp.where(cross & (i % 2 == 0), soft, 0.0), axis=0, keepdims=True)

    total = lax.fori_loop(0, steps, terms, jnp.zeros((1, PT), F32))
    loss[...] = jnp.sum(total, axis=1, keepdims=True) / (PT // 2)
    grads[...] = mm(high[...], e) + mm(low[...], e)

    def project(c, _):
        at = pl.ds(pl.multiple_of(c * step_rows, step_rows), step_rows)
        inv = inv_col[at, 0:1]
        unit = emb[at, :].astype(F32) * inv
        dw = grads[at, :]
        res = (dw - unit * (jnp.sum(dw * unit, axis=1, keepdims=True) / D)) * inv
        grads[at, :] = res
        d_emb[at, :] = res.astype(BF)
        return 0

    lax.fori_loop(0, steps, project, 0)
    first = (me[1] * NDP + me[0]) * 2
    base = pl.multiple_of((first // 8) * 8, 8)
    near = grads[pl.ds(base, 8), :]
    row = io((8, 1), 0)
    dy[0:1] = jnp.sum(jnp.where(row == first % 8, near, 0.0), axis=0, keepdims=True)
    dy[1:2] = jnp.sum(jnp.where(row == first % 8 + 1, near, 0.0), axis=0, keepdims=True)
    raw = mm(d_emb[...], wd[...], ((1,), (1,))).astype(BF)
    i = io((PT, PT), 0)
    at = (i % LOCAL) // 2 * (2 * NDP) + (i // LOCAL) * 2 + i % 2
    perm = (io((PT, PT), 1) == at).astype(BF)
    q[...] = mm(perm, raw).astype(BF)


def slope_kernel(off, me, q, act, slope, cols, dpre, dgl):
    src = (me[0] + off) % NDP
    qb = q[pl.ds(pl.multiple_of(src * LOCAL, LOCAL), LOCAL), :]

    def step(c, _):
        at = pl.ds(pl.multiple_of(c * CHUNK, CHUNK), CHUNK)
        col = cols[at, :]
        pick = (io((CHUNK, LOCAL), 1).astype(F32) == col[:, 2:3]).astype(BF)
        dact = mm(pick, qb) * col[:, 0:1]
        dpre[at, :] = (dact * slope[at, :].astype(F32)).astype(BF)
        dots = jnp.sum(dact * act[at, :].astype(F32), axis=1, keepdims=True) * col[:, 1:2]
        dgl[at, :] = jnp.broadcast_to(dots, (CHUNK, 128))
        return 0

    lax.fori_loop(0, ROWS // CHUNK, step, 0)


def slope_block(off, me, q, saved):
    _, act, slope, cols, _ = saved
    return run(
        functools.partial(slope_kernel, off),
        (shape(ROWS, FD), shape(ROWS, 128, dtype=F32)),
        me,
        q,
        act,
        slope,
        cols,
        smem=1,
        name="expert_slope",
    )


def back_value(dpre, dgl, wu, router):
    return mm(dpre[...], wu[...], ((1,), (1,))) + dgl[:, 0:1] * router[...]


def back_first_kernel(dpre, dgl, wu, router, top, low):
    v = back_value(dpre, dgl, wu, router)
    top[...] = v[:CUT].astype(BF)
    low[...] = v[CUT:].astype(BF)


def back_half_kernel(upper, dpre, dgl, wu, router, part, out):
    v = back_value(dpre, dgl, wu, router)
    if upper:
        out[:CUT] = (v[:CUT] + part[...].astype(F32)).astype(BF)
        out[CUT:] = v[CUT:].astype(BF)
    else:
        out[:CUT] = v[:CUT].astype(BF)
        out[CUT:] = (v[CUT:] + part[...].astype(F32)).astype(BF)


def back_kernel(dpre, dgl, wu, router, part, out):
    v = back_value(dpre, dgl, wu, router)
    out[...] = (v + part[...].astype(F32)).astype(BF)


def back_last_kernel(own, r, l, small, send):
    v = (own[...] + r[...].astype(F32) + l[...].astype(F32)).astype(BF)
    send[:, :D] = v[:MAIN]
    last = v[MAIN:]
    fold = mm(spread(0), last[:, :128])
    for k in range(1, 8):
        fold = fold + mm(spread(k), last[:, 128 * k : 128 * (k + 1)])
    send[:, FOLD:EXTRA] = fold.astype(BF)
    total = jnp.sum(small[...], axis=0)
    sub = io((MAIN, 128), 0) % 8
    for n in range(2):
        value = jnp.zeros((MAIN, 128), F32)
        for k in range(8):
            value = jnp.where(sub == k, total[n : n + 1, 128 * k : 128 * (k + 1)], value)
        send[:, EXTRA + 128 * n : EXTRA + 128 * (n + 1)] = value.astype(BF)


def back_own_kernel(dpre, dgl, wu, router, out):
    out[...] = back_value(dpre, dgl, wu, router)


def weight_kernel(*refs):
    xs, dpres, dgls = refs[:NDP], refs[NDP : 2 * NDP], refs[2 * NDP : 3 * NDP]
    wu, router, grad_up, small, cat = refs[3 * NDP :]
    for n, (x, dpre) in enumerate(zip(xs, dpres)):
        term = mm(x[:ROWS], dpre[...], ((0,), (0,)))
        if n == 0:
            grad_up[...] = term
        else:
            grad_up[...] += term
    g_router = None
    for x, dgl in zip(xs, dgls):
        term = jnp.sum(x[:ROWS].astype(F32) * dgl[:, 0:1], axis=0, keepdims=True)
        g_router = term if g_router is None else g_router + term
    cat[...] = wu[...].astype(F32) * grad_up[...]
    rows = lax.dot_general(
        jnp.ones((8, FD), F32), cat[...], (((1,), (1,)), ((), ())), precision=lax.Precision.HIGHEST, preferred_element_type=F32
    )
    both = jnp.concatenate([g_router, rows[0:1] + g_router * router[...]], axis=0)
    small[...] = jnp.broadcast_to(both[None], (NDP, 2, D))


def down_kernel(pooled, d_emb, out):
    out[...] = mm(pooled[...], d_emb[...], ((0,), (0,)))


def final_kernel(length, tok, gain, place, got, dy, grad_tokens, grad_router, gain_grad):
    n = length[0]
    xhat, rstd = layer_norm(tok[...].astype(F32))
    fold = got[:, FOLD:EXTRA]
    ones = [mm(spread(k), fold, ((0,), (0,))).astype(BF) for k in range(8)]
    last = jnp.concatenate(ones, axis=1)
    dxn = mm(place[:MAIN], got[:, :D], ((0,), (0,))) + mm(place[MAIN:], last, ((0,), (0,)))
    at = io((SEQ, 1), 0)
    w_img = jnp.where(at < PATCH, 1.0 / PATCH, 0.0)
    w_cap = jnp.where((at >= PATCH) & (at < PATCH + n), 1.0 / n.astype(F32), 0.0)
    g = dxn * gain[...]
    inner = jnp.sum(g * xhat, axis=1, keepdims=True) / D
    dx = (g - jnp.mean(g, axis=1, keepdims=True) - xhat * inner) * rstd
    grad_tokens[...] = (dx + w_img * dy[0:1] + w_cap * dy[1:2]).astype(BF)
    for k in range(8):
        piece = mm(spread(k), got[:, EXTRA:], ((0,), (0,)))
        grad_router[:, 128 * k : 128 * (k + 1)] = piece[:, :128]
        at_k = slice(128 * k, 128 * (k + 1))
        gain_grad[:, at_k] = jnp.sum(piece[:, 128:], axis=0, keepdims=True) / gain[:, at_k]


def exchange(value, axis):
    return lax.all_to_all(value, axis, split_axis=0, concat_axis=0, tiled=True)


def body(tokens, expert_ids, caption_lengths, gain, router, w_up, w_down, logit_scale, logit_bias):
    me_dp = lax.axis_index("dp").astype(I32)
    me_ex = lax.axis_index("expert").astype(I32)
    me = jnp.stack([me_dp, me_ex])
    wu = w_up[0]
    wd = w_down[0]
    tok = tokens[0]
    gain_row = gain.reshape(1, D)
    send, means, place = run(
        front_kernel,
        (shape(MAIN, SEND_W), shape(2, D, dtype=F32), shape(ROWS, SEQ)),
        caption_lengths,
        tok,
        expert_ids.reshape(1, SEQ),
        gain_row,
        smem=1,
        name="front",
    )
    got = exchange(send.reshape(NEX, 8, SEND_W), "expert").reshape(MAIN, SEND_W)
    own = run(unpack_kernel, shape(HEIGHT, D), got, name="unpack")

    right = [(i, (i + 1) % NDP) for i in range(NDP)]
    left = [(i, (i - 1) % NDP) for i in range(NDP)]
    half = NDP // 2
    router_row = jnp.sum(jnp.where(jnp.arange(NEX, dtype=I32)[None, :] == me_ex, router, 0.0), axis=1).reshape(1, D)
    r, l = own, own
    xs = {0: own}
    for k in range(1, half):
        r = lax.ppermute(r, "dp", right)
        l = lax.ppermute(l, "dp", left)
        xs[-k], xs[k] = r, l
    r = lax.ppermute(r[:CUT], "dp", right)
    l = lax.ppermute(l[CUT:], "dp", left)
    xs[half] = jnp.concatenate([r, l], axis=0)
    offsets = list(xs)
    saved = {off: (x,) + tuple(forward_block(x, wu, router_row)) for off, x in xs.items()}
    part, pooled = run(
        functools.partial(part_kernel, offsets),
        (shape(PT, D), shape(PT, FD)),
        me,
        *[saved[off][4] for off in offsets],
        wd,
        smem=1,
        name="pooled_down",
    )
    part = exchange(part.reshape(NEX, 2 * NDP, D), "expert")
    column = run(column_kernel, shape(NDP, 2 * NDP, D), me, part, means, smem=1, name="column")
    column = exchange(column, "dp")
    shared = run(share_kernel, shape(NEX, 2 * NDP, D), column, name="share")
    emb = exchange(shared, "expert").reshape(PT, D)
    loss, d_emb, dy, q = run(
        loss_kernel,
        (shape(1, 1, dtype=F32), shape(PT, D), shape(2, D, dtype=F32), shape(PT, FD)),
        me,
        logit_scale,
        logit_bias,
        emb,
        wd,
        smem=3,
        scratch=[
            pltpu.VMEM((PT, PT), F32),
            pltpu.VMEM((PT, 128), F32),
            pltpu.VMEM((PT, PT), BF),
            pltpu.VMEM((PT, PT), BF),
            pltpu.VMEM((PT, D), F32),
        ],
        name="pair_loss",
    )

    slopes = {half: slope_block(half, me, q, saved[half])}
    r, l = run(back_first_kernel, (shape(CUT, D), shape(CUT, D)), *slopes[half], wu, router_row, name="back_first")
    for off in (half - 1, 1 - half, 2, -2, 1, -1, 0):
        slopes[off] = slope_block(off, me, q, saved[off])
    for k in range(half - 1, -1, -1):
        r = lax.ppermute(r, "dp", right)
        l = lax.ppermute(l, "dp", left)
        if k == half - 1:
            r = run(functools.partial(back_half_kernel, True), shape(ROWS, D), *slopes[k], wu, router_row, r, name="back_half")
            l = run(functools.partial(back_half_kernel, False), shape(ROWS, D), *slopes[-k], wu, router_row, l, name="back_half")
        elif k > 0:
            r = run(back_kernel, shape(ROWS, D), *slopes[k], wu, router_row, r, name="back")
            l = run(back_kernel, shape(ROWS, D), *slopes[-k], wu, router_row, l, name="back")
    grad_up, small = run(
        weight_kernel,
        (shape(D, FD, dtype=F32), shape(NDP, 2, D, dtype=F32)),
        *[xs[off] for off in offsets],
        *[slopes[off][0] for off in offsets],
        *[slopes[off][1] for off in offsets],
        wu,
        router_row,
        scratch=[pltpu.VMEM((D, FD), F32)],
        name="weight_grads",
    )
    grad_down = run(down_kernel, shape(FD, D, dtype=F32), pooled, d_emb, name="down_grad")
    small = exchange(small, "dp")
    own_back = run(back_own_kernel, shape(ROWS, D, dtype=F32), *slopes[0], wu, router_row, name="back_own")
    send = run(back_last_kernel, shape(MAIN, BACK_W), own_back, r, l, small, name="back_last")
    got = exchange(send.reshape(NEX, 8, BACK_W), "expert").reshape(MAIN, BACK_W)
    grad_tokens, grad_router, gain_grad = run(
        final_kernel,
        (shape(SEQ, D), shape(NEX, D, dtype=F32), shape(1, D, dtype=F32)),
        caption_lengths,
        tok,
        gain_row,
        place,
        got,
        dy,
        smem=1,
        name="final",
    )
    return (loss.reshape(1), grad_tokens[None], grad_up[None], grad_down[None], grad_router.T, gain_grad.reshape(D))


def solution(mesh):
    return jax.shard_map(
        body,
        mesh=mesh,
        in_specs=(
            P(("dp", "expert"), None, None),
            P(("dp", "expert"), None, None),
            P(("dp", "expert")),
            P(),
            P(),
            P("expert", None, "dp"),
            P("expert", "dp", None),
            P(),
            P(),
        ),
        out_specs=(
            P(),
            P(("dp", "expert"), None, None),
            P("expert", None, "dp"),
            P("expert", "dp", None),
            P(),
            P(),
        ),
        check_vma=False,
    )
```

```python
import functools

import jax
import jax.numpy as jnp
from jax import lax
from jax.experimental import pallas as pl
from jax.experimental.pallas import tpu as pltpu
from jax.sharding import PartitionSpec as P

D = 1024
FD = 512
PATCH = 196
CAPLEN = 16
SEQ = 212
NDP = 8
NEX = 32
MAIN = NEX * 8
ROWS = NEX * 9
META = 8
HEIGHT = ROWS + META
CUT = ROWS // 2
LANES = 384
FOLD = D
EXTRA = D + 128
SEND_W = D + 256
BACK_W = D + 384
PT = 2 * NDP * NEX
LOCAL = 2 * NEX

EPS = 1e-06
LOSS_SCALE = 1024.0
BF = jnp.bfloat16
F32 = jnp.float32
I32 = jnp.int32

VM = pl.BlockSpec(memory_space=pltpu.VMEM)
SM = pl.BlockSpec(memory_space=pltpu.SMEM)


def mm(a, b, dims=((1,), (0,))):
    return lax.dot_general(a, b, (dims, ((), ())), preferred_element_type=F32)


def io(shape, axis):
    return lax.broadcasted_iota(I32, shape, axis)


def run(kernel, outs, *args, smem=0, scratch=(), name=None, limit=6, stage=False):
    specs = [SM] * smem + [pl.BlockSpec() if stage else VM] * (len(args) - smem)
    return pl.pallas_call(
        kernel,
        out_shape=outs,
        in_specs=specs,
        out_specs=jax.tree.map(lambda _: VM, outs),
        scratch_shapes=scratch,
        name=name,
        compiler_params=pltpu.CompilerParams(vmem_limit_bytes=limit * 1024 * 1024),
    )(*args)


def shape(*dims, dtype=BF):
    return jax.ShapeDtypeStruct(dims, dtype)


def spread(k):
    return (io((MAIN, NEX), 0) == io((MAIN, NEX), 1) * 8 + k).astype(BF)


def layer_norm(x):
    mean = jnp.mean(x, axis=1, keepdims=True)
    c = x - mean
    rstd = 1.0 / jnp.sqrt(jnp.mean(c * c, axis=1, keepdims=True) + EPS)
    return c * rstd, rstd


def front_kernel(length, tok, ids, gain, send, means, place):
    n = length[0]
    x = tok[...].astype(F32)
    xhat, _ = layer_norm(x)
    xn = (xhat * gain[...]).astype(BF)
    pos = io((1, SEQ), 1)
    real = pos < PATCH + n
    owner = ids[...]
    hit = (io((NEX, SEQ), 0) == owner) & real
    onehot = jnp.where(hit, 1.0, 0.0)
    before = (io((SEQ, SEQ), 0) < io((SEQ, SEQ), 1)).astype(BF)
    slot = jnp.sum(mm(onehot.astype(BF), before) * onehot, axis=0, keepdims=True).astype(I32)
    target = jnp.where(real & (slot < 8), owner * 8 + slot, -1)
    p_main = (io((MAIN, SEQ), 0) == target).astype(BF)
    p_last = jnp.where(slot == 8, onehot, 0.0).astype(BF)
    place[:MAIN] = p_main
    place[MAIN:] = p_last
    send[:, :D] = mm(p_main, xn).astype(BF)
    last = mm(p_last, xn).astype(BF)
    fold = mm(spread(0), last[:, :128])
    for k in range(1, 8):
        fold = fold + mm(spread(k), last[:, 128 * k : 128 * (k + 1)])
    send[:, FOLD:EXTRA] = fold.astype(BF)
    images = jnp.sum(jnp.where(pos < PATCH, onehot, 0.0), axis=1, keepdims=True)
    lane = io((NEX, 128), 1)
    info = jnp.where(lane == 0, images, jnp.where(lane == 1, n.astype(F32), 0.0)).astype(BF)
    send[:, EXTRA:] = mm(spread(0), info).astype(BF)
    at = io((SEQ, 1), 0)
    w_img = jnp.where(at < PATCH, 1.0 / PATCH, 0.0)
    w_cap = jnp.where((at >= PATCH) & (at < PATCH + n), 1.0 / n.astype(F32), 0.0)
    means[0:1] = jnp.sum(x * w_img, axis=0, keepdims=True)
    means[1:2] = jnp.sum(x * w_cap, axis=0, keepdims=True)


def unpack_kernel(got, block):
    block[:MAIN] = got[:, :D]
    info = mm(spread(0), got[:, EXTRA:SEND_W], ((0,), (0,)))
    fold = got[:, FOLD:EXTRA]
    for k in range(8):
        block[MAIN:ROWS, 128 * k : 128 * (k + 1)] = mm(spread(k), fold, ((0,), (0,))).astype(BF)
    r = io((1, LANES), 1)
    ex = jnp.where(r < MAIN, r // 8, r - MAIN)
    slot = jnp.where(r < MAIN, r % 8, 8).astype(F32)
    match = io((NEX, LANES), 0) == ex
    images = jnp.sum(jnp.where(match, info[:, 0:1], 0.0), axis=0, keepdims=True)
    lens = jnp.sum(jnp.where(match, info[:, 1:2], 0.0), axis=0, keepdims=True)
    is_img = slot < images
    pt = jnp.where(r < ROWS, 2 * ex + jnp.where(is_img, 0, 1), LOCAL).astype(F32)
    div = jnp.where(r < ROWS, jnp.where(is_img, float(PATCH), lens), 1.0)
    sub = io((META, LANES), 0)
    block[ROWS:, :LANES] = jnp.where(sub == 0, pt, jnp.where(sub == 1, div, 0.0)).astype(BF)
    block[ROWS:, LANES:] = jnp.zeros((META, D - LANES), BF)


CHUNK = 32


def forward_math(x, wu, router, act, slope, cols, pooled, pre, mixed):
    pre[...] = mm(x[:ROWS], wu[...])
    meta = x[ROWS:, :LANES].astype(F32)
    pt_row = meta[0:1]

    def gates(c, _):
        at = pl.ds(pl.multiple_of(c * CHUNK, CHUNK), CHUNK)
        prod = x[at, :].astype(F32) * router[...]
        t = prod[:, :128]
        for k in range(1, 8):
            t = t + prod[:, 128 * k : 128 * (k + 1)]
        cols[at, :] = t
        return 0

    lax.fori_loop(0, ROWS // CHUNK, gates, 0)
    gate = jax.nn.sigmoid(jnp.sum(cols[...], axis=1, keepdims=True))
    diag = io((ROWS, LANES), 1) == io((ROWS, LANES), 0)
    div = jnp.sum(jnp.where(diag, meta[1:2], 0.0), axis=1, keepdims=True)
    pt = jnp.sum(jnp.where(diag, pt_row, 0.0), axis=1, keepdims=True)
    lane = io((ROWS, 128), 1)
    cols[...] = jnp.where(lane == 0, gate / div, jnp.where(lane == 1, 1.0 - gate, jnp.where(lane == 2, pt, 0.0)))

    def step(c, _):
        at = pl.ds(pl.multiple_of(c * CHUNK, CHUNK), CHUNK)
        p = pre[at, :]
        phi = 0.5 * (1.0 + lax.erf(p * 0.7071067811865476))
        a = (p * phi).astype(BF)
        act[at, :] = a
        slope[at, :] = (phi + p * jnp.exp(-0.5 * p * p) * 0.3989422804014327).astype(BF)
        mixed[at, :] = (cols[at, 0:1] * a.astype(F32)).astype(BF)
        return 0

    lax.fori_loop(0, ROWS // CHUNK, step, 0)
    sel = (io((LOCAL, ROWS), 0).astype(F32) == pt_row[:, :ROWS]).astype(BF)
    pooled[...] = mm(sel, mixed[...]).astype(BF)


def forward_kernel(x, wu, router, act, slope, cols, pooled, pre, mixed):
    forward_math(x, wu, router, act, slope, cols, pooled, pre, mixed)


def forward_join_kernel(top, low, wu, router, act, slope, cols, pooled, x, pre, mixed):
    x[:CUT] = top[...]
    x[CUT:] = low[...]
    forward_math(x, wu, router, act, slope, cols, pooled, pre, mixed)


FORWARD_OUT = (shape(ROWS, FD), shape(ROWS, FD), shape(ROWS, 128, dtype=F32), shape(LOCAL, FD))
FORWARD_SCRATCH = [pltpu.VMEM((ROWS, FD), F32), pltpu.VMEM((ROWS, FD), BF)]


def forward_block(x, wu, router):
    return (x,) + tuple(run(forward_kernel, FORWARD_OUT, x, wu, router, scratch=FORWARD_SCRATCH, name="expert_forward"))


def forward_join(top, low, wu, router):
    out = run(
        forward_join_kernel,
        FORWARD_OUT + (shape(HEIGHT, D),),
        top,
        low,
        wu,
        router,
        scratch=FORWARD_SCRATCH,
        name="expert_forward_join",
    )
    return (out[4],) + tuple(out[:4])


def part_kernel(offsets, me, *refs):
    wd, part, pooled = refs[NDP:]
    total = None
    g = io((PT, LOCAL), 0)
    p = io((PT, LOCAL), 1)
    for ref, off in zip(refs[:NDP], offsets):
        src = (me[0] + off) % NDP
        perm = (g == (p // 2) * (2 * NDP) + (p % 2) * NDP + src).astype(BF)
        term = mm(perm, ref[...])
        total = term if total is None else total + term
    pooled[...] = total.astype(BF)
    part[...] = mm(pooled[...], wd[...]).astype(BF)


def column_kernel(me, got, means, out):
    s = jnp.sum(got[...].astype(F32), axis=0)
    row = io((2 * NDP, 1), 0)
    s = s + jnp.where(row == me[0], means[0:1], 0.0) + jnp.where(row == me[0] + NDP, means[1:2], 0.0)
    out[...] = jnp.broadcast_to(s.astype(BF)[None], (NDP, 2 * NDP, D))


def share_kernel(got, out):
    s = jnp.sum(got[...].astype(F32), axis=0)
    out[...] = jnp.broadcast_to(s.astype(BF)[None], (NEX, 2 * NDP, D))


def loss_kernel(me, scale, bias, emb, wd, loss, d_emb, dy, q, grads):
    n = PT // 2
    u = emb[:, :NDP].reshape(n, D)
    v = emb[:, NDP:].reshape(n, D)
    dots = mm(u, v, ((1,), (1,)))
    i = io((n, n), 0)
    j = io((n, n), 1)
    same = i == j

    def norms(a):
        on = jnp.where(same, mm(a, a, ((1,), (1,))), 0.0)
        col = 1.0 / jnp.sqrt(jnp.sum(on, axis=1, keepdims=True) / D + EPS)
        row = 1.0 / jnp.sqrt(jnp.sum(on, axis=0, keepdims=True) / D + EPS)
        return col, row

    iu, iu_row = norms(u)
    iv, iv_row = norms(v)
    to_unit = scale[0] / D
    sign = jnp.where(same, 1.0, -1.0)
    z = sign * (dots * to_unit * iu * iv_row + bias[0])
    t = jnp.exp(-jnp.abs(z))
    soft = jnp.maximum(-z, 0.0) + jnp.log1p(t)
    loss[...] = jnp.sum(jnp.sum(soft, axis=0, keepdims=True), axis=1, keepdims=True) / n
    coef = (-LOSS_SCALE / n) * sign * (jnp.where(z >= 0.0, t, 1.0) / (1.0 + t)) * to_unit
    for_u = coef * iv_row
    for_v = coef * iu

    def halves(c):
        hi = c.astype(BF)
        return hi, (c - hi.astype(F32)).astype(BF)

    u_hi, u_lo = halves(for_u)
    v_hi, v_lo = halves(for_v)
    u_dot = jnp.sum(for_u * dots, axis=1, keepdims=True)
    v_dot_row = jnp.sum(for_v * dots, axis=0, keepdims=True)
    v_dot = jnp.sum(jnp.where(same, v_dot_row, 0.0), axis=1, keepdims=True)
    grads[0] = (mm(u_hi, v) + mm(u_lo, v)) * iu - u.astype(F32) * (iu * iu * iu * u_dot / D)
    first = ((0,), (0,))
    grads[1] = (mm(v_hi, u, first) + mm(v_lo, u, first)) * iv - v.astype(F32) * (iv * iv * iv * v_dot / D)
    d_emb[:, :NDP] = grads[0].astype(BF).reshape(NEX, NDP, D)
    d_emb[:, NDP:] = grads[1].astype(BF).reshape(NEX, NDP, D)
    raw = mm(d_emb[...].reshape(PT, D), wd[...], ((1,), (1,))).astype(BF)
    r = io((PT, PT), 0)
    at = (r % LOCAL) // 2 * (2 * NDP) + (r % 2) * NDP + r // LOCAL
    perm = (io((PT, PT), 1) == at).astype(BF)
    q[...] = mm(perm, raw).astype(BF)
    row = io((NDP, 1), 0)
    near = pl.ds(pl.multiple_of(me[1] * NDP, NDP), NDP)
    for kind in range(2):
        dy[kind : kind + 1] = jnp.sum(jnp.where(row == me[0], grads[kind, near, :], 0.0), axis=0, keepdims=True)


def slope_kernel(off, me, q, act, slope, cols, dpre, dgl, dact, partial):
    src = (me[0] + off) % NDP
    qb = q[pl.ds(pl.multiple_of(src * LOCAL, LOCAL), LOCAL), :]
    pick = (io((ROWS, LOCAL), 1).astype(F32) == cols[:, 2:3]).astype(BF)
    dact[...] = mm(pick, qb)

    def step(c, _):
        at = pl.ds(pl.multiple_of(c * CHUNK, CHUNK), CHUNK)
        da = dact[at, :] * cols[at, 0:1]
        dpre[at, :] = (da * slope[at, :].astype(F32)).astype(BF)
        prod = da * act[at, :].astype(F32)
        partial[at, :] = prod[:, :128] + prod[:, 128:256] + prod[:, 256:384] + prod[:, 384:]
        return 0

    lax.fori_loop(0, ROWS // CHUNK, step, 0)
    dgl[...] = jnp.broadcast_to(jnp.sum(partial[...], axis=1, keepdims=True) * cols[:, 1:2], (ROWS, 128))


def slope_block(off, me, q, saved):
    _, act, slope, cols, _ = saved
    return run(
        functools.partial(slope_kernel, off),
        (shape(ROWS, FD), shape(ROWS, 128, dtype=F32)),
        me,
        q,
        act,
        slope,
        cols,
        smem=1,
        scratch=[pltpu.VMEM((ROWS, FD), F32), pltpu.VMEM((ROWS, 128), F32)],
        name="expert_slope",
    )


def back_value(dpre, dgl, wu, router):
    return mm(dpre[...], wu[...], ((1,), (1,))) + dgl[:, 0:1] * router[...]


def back_first_kernel(dpre, dgl, wu, router, top, low):
    v = back_value(dpre, dgl, wu, router)
    top[...] = v[:CUT].astype(BF)
    low[...] = v[CUT:].astype(BF)


def back_half_kernel(upper, dpre, dgl, wu, router, part, out):
    v = back_value(dpre, dgl, wu, router)
    if upper:
        out[:CUT] = (v[:CUT] + part[...].astype(F32)).astype(BF)
        out[CUT:] = v[CUT:].astype(BF)
    else:
        out[:CUT] = v[:CUT].astype(BF)
        out[CUT:] = (v[CUT:] + part[...].astype(F32)).astype(BF)


def back_kernel(dpre, dgl, wu, router, part, out):
    v = back_value(dpre, dgl, wu, router)
    out[...] = (v + part[...].astype(F32)).astype(BF)


def back_last_kernel(own, r, l, small, send):
    v = (own[...] + r[...].astype(F32) + l[...].astype(F32)).astype(BF)
    send[:, :D] = v[:MAIN]
    last = v[MAIN:]
    fold = mm(spread(0), last[:, :128])
    for k in range(1, 8):
        fold = fold + mm(spread(k), last[:, 128 * k : 128 * (k + 1)])
    send[:, FOLD:EXTRA] = fold.astype(BF)
    total = jnp.sum(small[...], axis=0)
    sub = io((MAIN, 128), 0) % 8
    for n in range(2):
        value = jnp.zeros((MAIN, 128), F32)
        for k in range(8):
            value = jnp.where(sub == k, total[n : n + 1, 128 * k : 128 * (k + 1)], value)
        send[:, EXTRA + 128 * n : EXTRA + 128 * (n + 1)] = value.astype(BF)


def back_own_kernel(dpre, dgl, wu, router, out):
    out[...] = back_value(dpre, dgl, wu, router)


def weight_kernel(*refs):
    xs, dpres, dgls = refs[:NDP], refs[NDP : 2 * NDP], refs[2 * NDP : 3 * NDP]
    wu, router, grad_up, small, cat = refs[3 * NDP :]
    for n, (x, dpre) in enumerate(zip(xs, dpres)):
        term = mm(x[:ROWS], dpre[...], ((0,), (0,)))
        if n == 0:
            grad_up[...] = term
        else:
            grad_up[...] += term
    g_router = None
    for x, dgl in zip(xs, dgls):
        term = jnp.sum(x[:ROWS].astype(F32) * dgl[:, 0:1], axis=0, keepdims=True)
        g_router = term if g_router is None else g_router + term
    cat[...] = wu[...].astype(F32) * grad_up[...]
    rows = lax.dot_general(
        jnp.ones((8, FD), F32), cat[...], (((1,), (1,)), ((), ())), precision=lax.Precision.HIGHEST, preferred_element_type=F32
    )
    both = jnp.concatenate([g_router, rows[0:1] + g_router * router[...]], axis=0)
    small[...] = jnp.broadcast_to(both[None], (NDP, 2, D))


def down_kernel(pooled, d_emb, out):
    out[...] = mm(pooled[...], d_emb[...].reshape(PT, D), ((0,), (0,)))


def final_kernel(length, tok, gain, place, got, dy, grad_tokens, grad_router, gain_grad):
    n = length[0]
    xhat, rstd = layer_norm(tok[...].astype(F32))
    fold = got[:, FOLD:EXTRA]
    ones = [mm(spread(k), fold, ((0,), (0,))).astype(BF) for k in range(8)]
    last = jnp.concatenate(ones, axis=1)
    dxn = mm(place[:MAIN], got[:, :D], ((0,), (0,))) + mm(place[MAIN:], last, ((0,), (0,)))
    at = io((SEQ, 1), 0)
    w_img = jnp.where(at < PATCH, 1.0 / PATCH, 0.0)
    w_cap = jnp.where((at >= PATCH) & (at < PATCH + n), 1.0 / n.astype(F32), 0.0)
    g = dxn * gain[...]
    inner = jnp.sum(g * xhat, axis=1, keepdims=True) / D
    dx = (g - jnp.mean(g, axis=1, keepdims=True) - xhat * inner) * rstd
    grad_tokens[...] = (dx + w_img * dy[0:1] + w_cap * dy[1:2]).astype(BF)
    for k in range(8):
        piece = mm(spread(k), got[:, EXTRA:], ((0,), (0,)))
        grad_router[:, 128 * k : 128 * (k + 1)] = piece[:, :128]
        at_k = slice(128 * k, 128 * (k + 1))
        gain_grad[:, at_k] = jnp.sum(piece[:, 128:], axis=0, keepdims=True) / gain[:, at_k]


def weight_grads(xs, slopes, offsets, wu, router_row):
    return run(
        weight_kernel,
        (shape(D, FD, dtype=F32), shape(NDP, 2, D, dtype=F32)),
        *[xs[off] for off in offsets],
        *[slopes[off][0] for off in offsets],
        *[slopes[off][1] for off in offsets],
        wu,
        router_row,
        scratch=[pltpu.VMEM((D, FD), F32)],
        name="weight_grads",
        limit=12,
    )


def exchange(value, axis):
    return lax.all_to_all(value, axis, split_axis=0, concat_axis=0, tiled=True)


def body(tokens, expert_ids, caption_lengths, gain, router, w_up, w_down, logit_scale, logit_bias):
    me_dp = lax.axis_index("dp").astype(I32)
    me_ex = lax.axis_index("expert").astype(I32)
    me = jnp.stack([me_dp, me_ex])
    wu = w_up[0]
    wd = w_down[0]
    tok = tokens[0]
    gain_row = gain.reshape(1, D)
    send, means, place = run(
        front_kernel,
        (shape(MAIN, SEND_W), shape(2, D, dtype=F32), shape(ROWS, SEQ)),
        caption_lengths,
        tok,
        expert_ids.reshape(1, SEQ),
        gain_row,
        smem=1,
        name="front",
        stage=True,
    )
    got = exchange(send.reshape(NEX, 8, SEND_W), "expert").reshape(MAIN, SEND_W)
    own = run(unpack_kernel, shape(HEIGHT, D), got, name="unpack")

    right = [(i, (i + 1) % NDP) for i in range(NDP)]
    left = [(i, (i - 1) % NDP) for i in range(NDP)]
    half = NDP // 2
    router_row = jnp.sum(jnp.where(jnp.arange(NEX, dtype=I32)[None, :] == me_ex, router, 0.0), axis=1).reshape(1, D)
    r, l = own, own
    saved = {}
    ready = [(0, own)]
    for k in range(1, half):
        nr = lax.ppermute(r, "dp", right)
        nl = lax.ppermute(l, "dp", left)
        for off, x in ready:
            saved[off] = forward_block(x, wu, router_row)
        flat = [saved[off] for off, _ in ready]
        r, l, flat = lax.optimization_barrier((nr, nl, flat))
        for (off, _), value in zip(ready, flat):
            saved[off] = value
        ready = [(-k, r), (k, l)]
    top = lax.ppermute(r[:CUT], "dp", right)
    low = lax.ppermute(l[CUT:], "dp", left)
    for off, x in ready:
        saved[off] = forward_block(x, wu, router_row)
    saved[half] = forward_join(top, low, wu, router_row)
    offsets = list(saved)
    xs = {off: saved[off][0] for off in offsets}
    part, pooled = run(
        functools.partial(part_kernel, offsets),
        (shape(PT, D), shape(PT, FD)),
        me,
        *[saved[off][4] for off in offsets],
        wd,
        smem=1,
        name="pooled_down",
    )
    part = exchange(part.reshape(NEX, 2 * NDP, D), "expert")
    column = run(column_kernel, shape(NDP, 2 * NDP, D), me, part, means, smem=1, name="column")
    column = exchange(column, "dp")
    shared = run(share_kernel, shape(NEX, 2 * NDP, D), column, name="share")
    emb = exchange(shared, "expert")
    loss, d_emb, dy, q = run(
        loss_kernel,
        (shape(1, 1, dtype=F32), shape(NEX, 2 * NDP, D), shape(2, D, dtype=F32), shape(PT, FD)),
        me,
        logit_scale,
        logit_bias,
        emb,
        wd,
        smem=3,
        scratch=[pltpu.VMEM((2, PT // 2, D), F32)],
        limit=16,
        name="pair_loss",
    )

    slopes = {half: slope_block(half, me, q, saved[half])}
    r, l = run(back_first_kernel, (shape(CUT, D), shape(CUT, D)), *slopes[half], wu, router_row, name="back_first")
    for off in (half - 1, 1 - half, 2, -2, 1, -1, 0):
        slopes[off] = slope_block(off, me, q, saved[off])
    small = None
    for k in range(half - 1, -1, -1):
        r = lax.ppermute(r, "dp", right)
        l = lax.ppermute(l, "dp", left)
        if k == half - 1:
            r, l, slopes = lax.optimization_barrier((r, l, slopes))
            r = run(functools.partial(back_half_kernel, True), shape(ROWS, D), *slopes[k], wu, router_row, r, name="back_half")
            l = run(functools.partial(back_half_kernel, False), shape(ROWS, D), *slopes[-k], wu, router_row, l, name="back_half")
        elif k > 0:
            if k == half - 2:
                grad_up, small = weight_grads(xs, slopes, offsets, wu, router_row)
                r, l, small = lax.optimization_barrier((r, l, small))
            else:
                small = exchange(small, "dp")
                r, l, small = lax.optimization_barrier((r, l, small))
            r = run(back_kernel, shape(ROWS, D), *slopes[k], wu, router_row, r, name="back")
            l = run(back_kernel, shape(ROWS, D), *slopes[-k], wu, router_row, l, name="back")
    grad_down = run(down_kernel, shape(FD, D, dtype=F32), pooled, d_emb, name="down_grad")
    own_back = run(back_own_kernel, shape(ROWS, D, dtype=F32), *slopes[0], wu, router_row, name="back_own")
    send = run(back_last_kernel, shape(MAIN, BACK_W), own_back, r, l, small, name="back_last")
    got = exchange(send.reshape(NEX, 8, BACK_W), "expert").reshape(MAIN, BACK_W)
    grad_tokens, grad_router, gain_grad = run(
        final_kernel,
        (shape(SEQ, D), shape(NEX, D, dtype=F32), shape(1, D, dtype=F32)),
        caption_lengths,
        tok,
        gain_row,
        place,
        got,
        dy,
        smem=1,
        name="final",
    )
    return (loss.reshape(1), grad_tokens[None], grad_up[None], grad_down[None], grad_router.T, gain_grad.reshape(D))


def solution(mesh):
    return jax.shard_map(
        body,
        mesh=mesh,
        in_specs=(
            P(("dp", "expert"), None, None),
            P(("dp", "expert"), None, None),
            P(("dp", "expert")),
            P(),
            P(),
            P("expert", None, "dp"),
            P("expert", "dp", None),
            P(),
            P(),
        ),
        out_specs=(
            P(),
            P(("dp", "expert"), None, None),
            P("expert", None, "dp"),
            P("expert", "dp", None),
            P(),
            P(),
        ),
        check_vma=False,
    )
```

```python
import functools

import jax
import jax.numpy as jnp
from jax import lax
from jax.experimental import pallas as pl
from jax.experimental.pallas import tpu as pltpu
from jax.sharding import PartitionSpec as P

D = 1024
FD = 512
PATCH = 196
CAPLEN = 16
SEQ = 212
NDP = 8
NEX = 32
MAIN = NEX * 8
ROWS = NEX * 9
META = 8
HEIGHT = ROWS + META
CUT = ROWS // 2
LANES = 384
FOLD = D
EXTRA = D + 128
SEND_W = D + 256
BACK_W = D + 384
PT = 2 * NDP * NEX
LOCAL = 2 * NEX

EPS = 1e-06
LOSS_SCALE = 1024.0
BF = jnp.bfloat16
F32 = jnp.float32
I32 = jnp.int32

VM = pl.BlockSpec(memory_space=pltpu.VMEM)
SM = pl.BlockSpec(memory_space=pltpu.SMEM)


def mm(a, b, dims=((1,), (0,))):
    return lax.dot_general(a, b, (dims, ((), ())), preferred_element_type=F32)


def io(shape, axis):
    return lax.broadcasted_iota(I32, shape, axis)


HB = pl.BlockSpec(memory_space=pltpu.HBM)


def run(kernel, outs, *args, smem=0, scratch=(), name=None, limit=6, hbm=0, spill=()):
    specs = [SM] * smem + [HB] * hbm + [VM] * (len(args) - smem - hbm)
    many = isinstance(outs, tuple)
    kinds = [n in spill for n in range(len(outs) if many else 1)]
    out_specs = tuple(HB if k else VM for k in kinds) if many else VM
    if many:
        outs = tuple(pltpu.HBM(o.shape, o.dtype) if k else o for o, k in zip(outs, kinds))
    args = tuple(pltpu.with_memory_space_constraint(a, pltpu.HBM) if smem <= n < smem + hbm else a for n, a in enumerate(args))
    return pl.pallas_call(
        kernel,
        out_shape=outs,
        in_specs=specs,
        out_specs=out_specs,
        scratch_shapes=scratch,
        name=name,
        cost_estimate=pl.CostEstimate(flops=1024, transcendentals=0, bytes_accessed=1024),
        compiler_params=pltpu.CompilerParams(vmem_limit_bytes=limit * 1024 * 1024),
    )(*args)


def shape(*dims, dtype=BF):
    return jax.ShapeDtypeStruct(dims, dtype)


def spread(k):
    return (io((MAIN, NEX), 0) == io((MAIN, NEX), 1) * 8 + k).astype(BF)


def layer_norm(x):
    mean = jnp.mean(x, axis=1, keepdims=True)
    c = x - mean
    rstd = 1.0 / jnp.sqrt(jnp.mean(c * c, axis=1, keepdims=True) + EPS)
    return c * rstd, rstd


def front_kernel(length, tok_hbm, ids_hbm, gain_hbm, send, means, place, tok, ids, gain, sems):
    copies = [
        pltpu.make_async_copy(src, dst, sems.at[k])
        for k, (src, dst) in enumerate(((tok_hbm, tok), (ids_hbm, ids), (gain_hbm, gain)))
    ]
    for copy in copies:
        copy.start()
    for copy in copies:
        copy.wait()
    n = length[0]
    x = tok[...].astype(F32)
    xhat, _ = layer_norm(x)
    xn = (xhat * gain[...]).astype(BF)
    pos = io((1, SEQ), 1)
    real = pos < PATCH + n
    owner = ids[...]
    hit = (io((NEX, SEQ), 0) == owner) & real
    onehot = jnp.where(hit, 1.0, 0.0)
    before = (io((SEQ, SEQ), 0) < io((SEQ, SEQ), 1)).astype(BF)
    slot = jnp.sum(mm(onehot.astype(BF), before) * onehot, axis=0, keepdims=True).astype(I32)
    target = jnp.where(real & (slot < 8), owner * 8 + slot, -1)
    p_main = (io((MAIN, SEQ), 0) == target).astype(BF)
    p_last = jnp.where(slot == 8, onehot, 0.0).astype(BF)
    place[:MAIN] = p_main
    place[MAIN:] = p_last
    send[:, :D] = mm(p_main, xn).astype(BF)
    last = mm(p_last, xn).astype(BF)
    fold = mm(spread(0), last[:, :128])
    for k in range(1, 8):
        fold = fold + mm(spread(k), last[:, 128 * k : 128 * (k + 1)])
    send[:, FOLD:EXTRA] = fold.astype(BF)
    images = jnp.sum(jnp.where(pos < PATCH, onehot, 0.0), axis=1, keepdims=True)
    lane = io((NEX, 128), 1)
    info = jnp.where(lane == 0, images, jnp.where(lane == 1, n.astype(F32), 0.0)).astype(BF)
    send[:, EXTRA:] = mm(spread(0), info).astype(BF)
    at = io((SEQ, 1), 0)
    w_img = jnp.where(at < PATCH, 1.0 / PATCH, 0.0)
    w_cap = jnp.where((at >= PATCH) & (at < PATCH + n), 1.0 / n.astype(F32), 0.0)
    means[0:1] = jnp.sum(x * w_img, axis=0, keepdims=True)
    means[1:2] = jnp.sum(x * w_cap, axis=0, keepdims=True)


def unpack_kernel(got, top, low):
    top[:CUT] = got[:CUT, :D]
    low[: MAIN - CUT] = got[CUT:, :D]
    info = mm(spread(0), got[:, EXTRA:SEND_W], ((0,), (0,)))
    fold = got[:, FOLD:EXTRA]
    for k in range(8):
        low[MAIN - CUT : CUT, 128 * k : 128 * (k + 1)] = mm(spread(k), fold, ((0,), (0,))).astype(BF)
    r = io((1, LANES), 1)
    ex = jnp.where(r < MAIN, r // 8, r - MAIN)
    slot = jnp.where(r < MAIN, r % 8, 8).astype(F32)
    match = io((NEX, LANES), 0) == ex
    images = jnp.sum(jnp.where(match, info[:, 0:1], 0.0), axis=0, keepdims=True)
    lens = jnp.sum(jnp.where(match, info[:, 1:2], 0.0), axis=0, keepdims=True)
    is_img = slot < images
    pt = jnp.where(r < ROWS, 2 * ex + jnp.where(is_img, 0, 1), LOCAL).astype(F32)
    div = jnp.where(r < ROWS, jnp.where(is_img, float(PATCH), lens), 1.0)
    for ref, info_row in ((top, pt), (low, div)):
        ref[CUT:, :LANES] = jnp.broadcast_to(info_row, (META, LANES)).astype(BF)
        ref[CUT:, LANES:] = jnp.zeros((META, D - LANES), BF)


CHUNK = 96


def forward_core(top, low, wu, router, act, slope, cols, pre, mixed):
    pre[:CUT] = mm(top[:CUT], wu[...])
    pre[CUT:] = mm(low[:CUT], wu[...])
    pt_row = top[CUT:, :LANES].astype(F32)[0:1]
    div_row = low[CUT:, :LANES].astype(F32)[0:1]

    def gates(c, _):
        at = pl.ds(pl.multiple_of(c * 48, 48), 48)
        for ref, base in ((top, 0), (low, CUT)):
            prod = ref[at, :].astype(F32) * router[...]
            t = prod[:, :128]
            for k in range(1, 8):
                t = t + prod[:, 128 * k : 128 * (k + 1)]
            cols[pl.ds(pl.multiple_of(c * 48 + base, 48), 48), :] = t
        return 0

    lax.fori_loop(0, CUT // 48, gates, 0)
    gate = jax.nn.sigmoid(jnp.sum(cols[...], axis=1, keepdims=True))
    diag = io((ROWS, LANES), 1) == io((ROWS, LANES), 0)
    div = jnp.sum(jnp.where(diag, div_row, 0.0), axis=1, keepdims=True)
    pt = jnp.sum(jnp.where(diag, pt_row, 0.0), axis=1, keepdims=True)
    lane = io((ROWS, 128), 1)
    cols[...] = jnp.where(lane == 0, gate / div, jnp.where(lane == 1, 1.0 - gate, jnp.where(lane == 2, pt, 0.0)))

    def step(c, _):
        at = pl.ds(pl.multiple_of(c * CHUNK, CHUNK), CHUNK)
        p = pre[at, :]
        phi = 0.5 * (1.0 + lax.erf(p * 0.7071067811865476))
        a = (p * phi).astype(BF)
        act[at, :] = a
        slope[at, :] = (phi + p * jnp.exp(-0.5 * p * p) * 0.3989422804014327).astype(BF)
        mixed[at, :] = (cols[at, 0:1] * a.astype(F32)).astype(BF)
        return 0

    lax.fori_loop(0, ROWS // CHUNK, step, 0)
    return (io((LOCAL, ROWS), 0).astype(F32) == pt_row[:, :ROWS]).astype(BF)


def forward_kernel(top, low, wu, router, act_out, slope_out, cols_out, pooled_out, act, slope, cols, pooled, pre, mixed, sems):
    sel = forward_core(top, low, wu, router, act, slope, cols, pre, mixed)
    outs = ((act, act_out), (slope, slope_out), (cols, cols_out), (pooled, pooled_out))
    copies = [pltpu.make_async_copy(src, dst, sems.at[k]) for k, (src, dst) in enumerate(outs)]
    for copy in copies[:3]:
        copy.start()
    pooled[...] = mm(sel, mixed[...]).astype(BF)
    copies[3].start()
    for copy in copies:
        copy.wait()


def keep_shapes():
    return (shape(ROWS, FD), shape(ROWS, FD), shape(ROWS, 128, dtype=F32))


def keep_scratch():
    return [pltpu.VMEM((ROWS, FD), BF), pltpu.VMEM((ROWS, FD), BF), pltpu.VMEM((ROWS, 128), F32)]


def forward_block(top, low, wu, router):
    out = run(
        forward_kernel,
        keep_shapes() + (shape(LOCAL, FD),),
        top,
        low,
        wu,
        router,
        scratch=keep_scratch()
        + [
            pltpu.VMEM((LOCAL, FD), BF),
            pltpu.VMEM((ROWS, FD), F32),
            pltpu.VMEM((ROWS, FD), BF),
            pltpu.SemaphoreType.DMA((4,)),
        ],
        name="expert_forward",
        spill=(0, 1, 2, 3),
    )
    return (top, low) + tuple(out)


def forward_last_kernel(offsets, late, me, *refs):
    n_late = len(late)
    early = refs[: NDP - n_late]
    refs = refs[NDP - n_late :]
    xs, refs = refs[: 2 * n_late], refs[2 * n_late :]
    wu, wd, router = refs[:3]
    outs, refs = refs[3 : 3 + 3 * n_late], refs[3 + 3 * n_late :]
    part, pooled_out = refs[:2]
    held, refs = refs[2 : 2 + 3 * n_late], refs[2 + 3 * n_late :]
    near, pooled, pre, mixed, total, sems = refs
    copies = []
    loads = [pltpu.make_async_copy(ref, near.at[n], sems.at[3 * n_late + 1 + n]) for n, ref in enumerate(early)]
    for copy in loads:
        copy.start()
    g = io((PT, LOCAL), 0)
    p = io((PT, LOCAL), 1)
    for n in list(range(len(early), NDP)) + list(range(len(early))):
        if n < len(early):
            loads[n].wait()
            value = near[n]
        else:
            m = n - len(early)
            keep = held[3 * m : 3 * m + 3]
            sel = forward_core(xs[2 * m], xs[2 * m + 1], wu, router, *keep, pre, mixed)
            for k in range(3):
                copies.append(pltpu.make_async_copy(keep[k], outs[3 * m + k], sems.at[3 * m + k]))
                copies[-1].start()
            value = mm(sel, mixed[...]).astype(BF)
        src = (me[0] + offsets[n]) % NDP
        perm = (g == (p // 2) * (2 * NDP) + (p % 2) * NDP + src).astype(BF)
        if n == len(early):
            total[...] = mm(perm, value)
        else:
            total[...] += mm(perm, value)
    pooled[...] = total[...].astype(BF)
    copies.append(pltpu.make_async_copy(pooled, pooled_out, sems.at[3 * n_late]))
    copies[-1].start()
    part[...] = mm(pooled[...], wd[...]).astype(BF)
    for copy in copies:
        copy.wait()


def forward_last(me, early, late, wu, wd, router):
    offsets = list(early) + list(late)
    n_late = len(late)
    out = run(
        functools.partial(forward_last_kernel, offsets, list(late)),
        keep_shapes() * n_late + (shape(PT, D), shape(PT, FD)),
        me,
        *[value[5] for value in early.values()],
        *[half for pair in late.values() for half in pair],
        wu,
        wd,
        router,
        smem=1,
        scratch=keep_scratch() * n_late
        + [
            pltpu.VMEM((len(early), LOCAL, FD), BF),
            pltpu.VMEM((PT, FD), BF),
            pltpu.VMEM((ROWS, FD), F32),
            pltpu.VMEM((ROWS, FD), BF),
            pltpu.VMEM((PT, FD), F32),
            pltpu.SemaphoreType.DMA((3 * n_late + 1 + len(early),)),
        ],
        name="forward_last",
        hbm=len(early),
        limit=10,
        spill=tuple(range(3 * n_late)) + (3 * n_late + 1,),
    )
    saved = dict(early)
    for n, off in enumerate(late):
        saved[off] = tuple(late[off]) + tuple(out[3 * n : 3 * n + 3]) + (None,)
    return saved, out[3 * n_late], out[3 * n_late + 1]


def column_kernel(me, got, means, out):
    s = jnp.sum(got[...].astype(F32), axis=0)
    row = io((2 * NDP, 1), 0)
    s = s + jnp.where(row == me[0], means[0:1], 0.0) + jnp.where(row == me[0] + NDP, means[1:2], 0.0)
    out[...] = jnp.broadcast_to(s.astype(BF)[None], (NDP, 2 * NDP, D))


def share_kernel(got, out):
    s = jnp.sum(got[...].astype(F32), axis=0)
    out[...] = jnp.broadcast_to(s.astype(BF)[None], (NEX, 2 * NDP, D))


def loss_kernel(me, scale, bias, emb, wd, loss, d_emb, dy, q, grads):
    n = PT // 2
    u = emb[:, :NDP].reshape(n, D)
    v = emb[:, NDP:].reshape(n, D)
    dots = mm(u, v, ((1,), (1,)))
    i = io((n, n), 0)
    j = io((n, n), 1)
    same = i == j

    def norms(a):
        on = jnp.where(same, mm(a, a, ((1,), (1,))), 0.0)
        col = 1.0 / jnp.sqrt(jnp.sum(on, axis=1, keepdims=True) / D + EPS)
        row = 1.0 / jnp.sqrt(jnp.sum(on, axis=0, keepdims=True) / D + EPS)
        return col, row

    iu, iu_row = norms(u)
    iv, iv_row = norms(v)
    to_unit = scale[0] / D
    sign = jnp.where(same, 1.0, -1.0)
    z = sign * (dots * to_unit * iu * iv_row + bias[0])
    t = jnp.exp(-jnp.abs(z))
    soft = jnp.maximum(-z, 0.0) + jnp.log1p(t)
    loss[...] = jnp.sum(jnp.sum(soft, axis=0, keepdims=True), axis=1, keepdims=True) / n
    coef = (-LOSS_SCALE / n) * sign * (jnp.where(z >= 0.0, t, 1.0) / (1.0 + t)) * to_unit
    for_u = coef * iv_row
    for_v = coef * iu

    def halves(c):
        hi = c.astype(BF)
        return hi, (c - hi.astype(F32)).astype(BF)

    u_hi, u_lo = halves(for_u)
    v_hi, v_lo = halves(for_v)
    u_dot = jnp.sum(for_u * dots, axis=1, keepdims=True)
    v_dot_row = jnp.sum(for_v * dots, axis=0, keepdims=True)
    v_dot = jnp.sum(jnp.where(same, v_dot_row, 0.0), axis=1, keepdims=True)
    grads[0] = (mm(u_hi, v) + mm(u_lo, v)) * iu - u.astype(F32) * (iu * iu * iu * u_dot / D)
    first = ((0,), (0,))
    grads[1] = (mm(v_hi, u, first) + mm(v_lo, u, first)) * iv - v.astype(F32) * (iv * iv * iv * v_dot / D)
    d_emb[:, :NDP] = grads[0].astype(BF).reshape(NEX, NDP, D)
    d_emb[:, NDP:] = grads[1].astype(BF).reshape(NEX, NDP, D)
    raw = mm(d_emb[...].reshape(PT, D), wd[...], ((1,), (1,))).astype(BF)
    r = io((PT, PT), 0)
    at = (r % LOCAL) // 2 * (2 * NDP) + (r % 2) * NDP + r // LOCAL
    perm = (io((PT, PT), 1) == at).astype(BF)
    q[...] = mm(perm, raw).astype(BF)
    row = io((NDP, 1), 0)
    near = pl.ds(pl.multiple_of(me[1] * NDP, NDP), NDP)
    for kind in range(2):
        dy[kind : kind + 1] = jnp.sum(jnp.where(row == me[0], grads[kind, near, :], 0.0), axis=0, keepdims=True)


def slope_kernel(off, me, q, act, slope, cols, dpre, dgl, dact, partial):
    src = (me[0] + off) % NDP
    qb = q[pl.ds(pl.multiple_of(src * LOCAL, LOCAL), LOCAL), :]
    pick = (io((ROWS, LOCAL), 1).astype(F32) == cols[:, 2:3]).astype(BF)
    dact[...] = mm(pick, qb)

    for c in range(0, ROWS, CHUNK):
        at = pl.ds(c, CHUNK)
        da = dact[at, :] * cols[at, 0:1]
        dpre[at, :] = (da * slope[at, :].astype(F32)).astype(BF)
        prod = da * act[at, :].astype(F32)
        partial[at, :] = prod[:, :128] + prod[:, 128:256] + prod[:, 256:384] + prod[:, 384:]
    dgl[...] = jnp.broadcast_to(jnp.sum(partial[...], axis=1, keepdims=True) * cols[:, 1:2], (ROWS, 128))


def slope_block(off, me, q, saved):
    _, _, act, slope, cols, _ = saved
    return run(
        functools.partial(slope_kernel, off),
        (shape(ROWS, FD), shape(ROWS, 128, dtype=F32)),
        me,
        q,
        act,
        slope,
        cols,
        smem=1,
        scratch=[pltpu.VMEM((ROWS, FD), F32), pltpu.VMEM((ROWS, 128), F32)],
        name="expert_slope",
    )


def half_value(upper, x, dpre, dgl, wu, router):
    rows = slice(0, CUT) if upper else slice(CUT, ROWS)
    col = dgl[rows, 0:1]
    v = mm(dpre[rows], wu[...], ((1,), (1,))) + col * router[...]
    xf = x[:CUT].astype(F32)
    return v, jnp.sum(xf * col, axis=0, keepdims=True), jnp.sum(xf * v, axis=0, keepdims=True)


def back_first_kernel(x_a, dpre_a, dgl_a, x_b, dpre_b, dgl_b, wu, router, out_a, out_b, sums):
    v_a, r_a, g_a = half_value(True, x_a, dpre_a, dgl_a, wu, router)
    v_b, r_b, g_b = half_value(False, x_b, dpre_b, dgl_b, wu, router)
    out_a[...] = v_a.astype(BF)
    out_b[...] = v_b.astype(BF)
    sums[0:1] = r_a + r_b
    sums[1:2] = g_a + g_b


def back_add_kernel(x_a, dpre_a, dgl_a, x_b, dpre_b, dgl_b, wu, router, got_a, got_b, out_a, out_b, sums):
    v_a, r_a, g_a = half_value(True, x_a, dpre_a, dgl_a, wu, router)
    v_b, r_b, g_b = half_value(False, x_b, dpre_b, dgl_b, wu, router)
    out_a[...] = (v_a + got_a[...].astype(F32)).astype(BF)
    out_b[...] = (v_b + got_b[...].astype(F32)).astype(BF)
    sums[0:1] = r_a + r_b
    sums[1:2] = g_a + g_b


def back_near_kernel(top, low, dpre, dgl, wu, router, out, sums):
    v_a, r_a, g_a = half_value(True, top, dpre, dgl, wu, router)
    v_b, r_b, g_b = half_value(False, low, dpre, dgl, wu, router)
    out[:CUT] = v_a
    out[CUT:] = v_b
    sums[0:1] = r_a + r_b
    sums[1:2] = g_a + g_b


def back_sums_kernel(top, low, dpre, dgl, wu, router, sums):
    _, r_a, g_a = half_value(True, top, dpre, dgl, wu, router)
    _, r_b, g_b = half_value(False, low, dpre, dgl, wu, router)
    sums[0:1] = r_a + r_b
    sums[1:2] = g_a + g_b


def add_kernel(near_a, near_b, got_a, got_b, out_a, out_b):
    out_a[...] = (near_a[:CUT] + got_a[...].astype(F32)).astype(BF)
    out_b[...] = (near_b[CUT:] + got_b[...].astype(F32)).astype(BF)


def total_kernel(*refs):
    out = refs[-1]
    total = refs[0][...]
    for ref in refs[1:-1]:
        total = total + ref[...]
    out[...] = jnp.broadcast_to(total[None], (NDP, 2, D))


SUMS = shape(2, D, dtype=F32)


def back_pair(block_a, slope_a, block_b, slope_b, wu, router, got=()):
    return run(
        back_add_kernel if got else back_first_kernel,
        (shape(CUT, D), shape(CUT, D), SUMS),
        block_a[0],
        *slope_a,
        block_b[1],
        *slope_b,
        wu,
        router,
        *got,
        name="back_pair",
    )


def back_last_kernel(dpre, dgl, wu, router, ra, la, rb, lb, small, send):
    own = mm(dpre[...], wu[...], ((1,), (1,))) + dgl[:, 0:1] * router[...]
    v_a = own[:CUT] + ra[...].astype(F32) + la[...].astype(F32)
    v_b = own[CUT:] + rb[...].astype(F32) + lb[...].astype(F32)
    v = jnp.concatenate([v_a, v_b], axis=0).astype(BF)
    send[:, :D] = v[:MAIN]
    last = v[MAIN:]
    fold = mm(spread(0), last[:, :128])
    for k in range(1, 8):
        fold = fold + mm(spread(k), last[:, 128 * k : 128 * (k + 1)])
    send[:, FOLD:EXTRA] = fold.astype(BF)
    total = jnp.sum(small[...], axis=0)
    sub = io((MAIN, 128), 0) % 8
    for n in range(2):
        value = jnp.zeros((MAIN, 128), F32)
        for k in range(8):
            value = jnp.where(sub == k, total[n : n + 1, 128 * k : 128 * (k + 1)], value)
        send[:, EXTRA + 128 * n : EXTRA + 128 * (n + 1)] = value.astype(BF)


def weight_kernel(*refs):
    tops, lows, dpres = (refs[NDP * k : NDP * (k + 1)] for k in range(3))
    grad_up = refs[3 * NDP]
    step_cols = 256

    def step(c, _):
        at = pl.ds(pl.multiple_of(c * step_cols, step_cols), step_cols)
        total = None
        for n in range(NDP):
            x = jnp.concatenate([tops[n][:CUT, at], lows[n][:CUT, at]], axis=0)
            term = mm(x, dpres[n][...], ((0,), (0,)))
            total = term if total is None else total + term
        grad_up[at, :] = total
        return 0

    lax.fori_loop(0, D // step_cols, step, 0)


def down_kernel(pooled, d_emb, out):
    out[...] = mm(pooled[...], d_emb[...].reshape(PT, D), ((0,), (0,)))


def final_kernel(length, tok, gain, place, got, dy, grad_tokens, grad_router, gain_grad):
    n = length[0]
    xhat, rstd = layer_norm(tok[...].astype(F32))
    fold = got[:, FOLD:EXTRA]
    ones = [mm(spread(k), fold, ((0,), (0,))).astype(BF) for k in range(8)]
    last = jnp.concatenate(ones, axis=1)
    dxn = mm(place[:MAIN], got[:, :D], ((0,), (0,))) + mm(place[MAIN:], last, ((0,), (0,)))
    at = io((SEQ, 1), 0)
    w_img = jnp.where(at < PATCH, 1.0 / PATCH, 0.0)
    w_cap = jnp.where((at >= PATCH) & (at < PATCH + n), 1.0 / n.astype(F32), 0.0)
    g = dxn * gain[...]
    inner = jnp.sum(g * xhat, axis=1, keepdims=True) / D
    dx = (g - jnp.mean(g, axis=1, keepdims=True) - xhat * inner) * rstd
    grad_tokens[...] = (dx + w_img * dy[0:1] + w_cap * dy[1:2]).astype(BF)
    for k in range(8):
        piece = mm(spread(k), got[:, EXTRA:], ((0,), (0,)))
        grad_router[:, 128 * k : 128 * (k + 1)] = piece[:, :128]
        at_k = slice(128 * k, 128 * (k + 1))
        gain_grad[:, at_k] = jnp.sum(piece[:, 128:], axis=0, keepdims=True) / gain[:, at_k]


def weight_grads(saved, dpres, offsets):
    return run(
        weight_kernel,
        shape(D, FD, dtype=F32),
        *[saved[off][0] for off in offsets],
        *[saved[off][1] for off in offsets],
        *dpres,
        name="weight_grads",
        limit=12,
    )


def exchange(value, axis):
    return lax.all_to_all(value, axis, split_axis=0, concat_axis=0, tiled=True)


def body(tokens, expert_ids, caption_lengths, gain, router, w_up, w_down, logit_scale, logit_bias):
    me_dp = lax.axis_index("dp").astype(I32)
    me_ex = lax.axis_index("expert").astype(I32)
    me = jnp.stack([me_dp, me_ex])
    wu = w_up[0]
    wd = w_down[0]
    tok = tokens[0]
    gain_row = gain.reshape(1, D)
    send, means, place = run(
        front_kernel,
        (shape(MAIN, SEND_W), shape(2, D, dtype=F32), shape(ROWS, SEQ)),
        caption_lengths,
        tok,
        expert_ids.reshape(1, SEQ),
        gain_row,
        smem=1,
        name="front",
        hbm=3,
        scratch=[
            pltpu.VMEM((SEQ, D), BF),
            pltpu.VMEM((1, SEQ), I32),
            pltpu.VMEM((1, D), F32),
            pltpu.SemaphoreType.DMA((3,)),
        ],
    )
    got = exchange(send.reshape(NEX, 8, SEND_W), "expert").reshape(MAIN, SEND_W)
    top, low = run(unpack_kernel, (shape(CUT + META, D), shape(CUT + META, D)), got, name="unpack")

    right = [(i, (i + 1) % NDP) for i in range(NDP)]
    left = [(i, (i - 1) % NDP) for i in range(NDP)]
    half = NDP // 2
    router_row = jnp.sum(jnp.where(jnp.arange(NEX, dtype=I32)[None, :] == me_ex, router, 0.0), axis=1).reshape(1, D)
    to_right = functools.partial(lax.ppermute, axis_name="dp", perm=right)
    to_left = functools.partial(lax.ppermute, axis_name="dp", perm=left)
    ra, la, rb, lb = top, top, low, low
    saved = {}
    pin = lax.optimization_barrier
    blocks = {0: (top, low)}

    def forward(off):
        saved[off] = forward_block(*blocks[off], wu, router_row)
        return saved[off]

    pinned_first = {2: 0, 3: -1, 4: -2}
    pinned_second = {3: 1}
    for k in range(1, half + 1):
        if k in pinned_first:
            off = pinned_first[k]
            ra, lb, saved[off] = pin((ra, lb, forward(off)))
        ra, lb = pin((to_right(ra), to_left(lb)))
        if k < half:
            if k in pinned_second:
                off = pinned_second[k]
                rb, la, saved[off] = pin((rb, la, forward(off)))
            rb, la = pin((to_right(rb), to_left(la)))
            blocks[-k] = (ra, rb)
            blocks[k] = (la, lb)
    forward(2)
    blocks[half] = (ra, lb)
    late = {off: blocks[off] for off in (1 - half, half - 1, half)}
    saved, part, pooled = forward_last(me, saved, late, wu, wd, router_row)
    offsets = list(saved)
    part = exchange(part.reshape(NEX, 2 * NDP, D), "expert")
    column = run(column_kernel, shape(NDP, 2 * NDP, D), me, part, means, smem=1, name="column")
    column = exchange(column, "dp")
    shared = run(share_kernel, shape(NEX, 2 * NDP, D), column, name="share")
    emb = exchange(shared, "expert")
    loss, d_emb, dy, q = run(
        loss_kernel,
        (shape(1, 1, dtype=F32), shape(NEX, 2 * NDP, D), shape(2, D, dtype=F32), shape(PT, FD)),
        me,
        logit_scale,
        logit_bias,
        emb,
        wd,
        smem=3,
        scratch=[pltpu.VMEM((2, PT // 2, D), F32)],
        limit=16,
        name="pair_loss",
    )

    slopes = {off: slope_block(off, me, q, saved[off]) for off in (half, half - 1, 1 - half, 2, -2, 1, -1, 0)}
    sums = []

    def pair(a, b, got=()):
        out = back_pair(saved[a], slopes[a], saved[b], slopes[b], wu, router_row, got)
        sums.append(out[2])
        return out[:2]

    def near(off):
        v, part_sums = run(
            back_near_kernel, (shape(ROWS, D, dtype=F32), SUMS), *saved[off][:2], *slopes[off], wu, router_row, name="back_near"
        )
        sums.append(part_sums)
        return v

    ra, lb = pair(half, half)
    la, rb = pair(1 - half, half - 1)
    nears = {}
    for k in range(half - 1, -1, -1):
        ra, lb = pin((to_right(ra), to_left(lb)))
        if k > 0:
            rb, la = pin((to_right(rb), to_left(la)))
        if k == 1:
            ra, lb, small = pin((ra, lb, small))
        if k > 1:
            ra, lb = pair(k, -k, (ra, lb))
        if k > 2:
            la, rb = pair(1 - k, k - 1, (la, rb))
        elif k == 2:
            nears = {off: near(off) for off in (1, -1)}
            sums.append(run(back_sums_kernel, SUMS, *saved[0][:2], *slopes[0], wu, router_row, name="back_sums"))
            small = run(total_kernel, shape(NDP, 2, D, dtype=F32), *sums, name="total")
            la, rb = run(add_kernel, (shape(CUT, D), shape(CUT, D)), nears[-1], nears[1], la, rb, name="back_add")
        elif k == 1:
            small = exchange(small, "dp")
            ra, lb = run(add_kernel, (shape(CUT, D), shape(CUT, D)), nears[1], nears[-1], ra, lb, name="back_add")
    send = run(back_last_kernel, shape(MAIN, BACK_W), *slopes[0], wu, router_row, ra, la, rb, lb, small, name="back_last")
    send, dpres = pin((send, [slopes[off][0] for off in offsets]))
    grad_up = weight_grads(saved, dpres, offsets)
    grad_down = run(down_kernel, shape(FD, D, dtype=F32), pooled, d_emb, name="down_grad")
    got = exchange(send.reshape(NEX, 8, BACK_W), "expert").reshape(MAIN, BACK_W)
    grad_tokens, grad_router, gain_grad = run(
        final_kernel,
        (shape(SEQ, D), shape(NEX, D, dtype=F32), shape(1, D, dtype=F32)),
        caption_lengths,
        tok,
        gain_row,
        place,
        got,
        dy,
        smem=1,
        name="final",
    )
    return (loss.reshape(1), grad_tokens[None], grad_up[None], grad_down[None], grad_router.T, gain_grad.reshape(D))


def solution(mesh):
    return jax.shard_map(
        body,
        mesh=mesh,
        in_specs=(
            P(("dp", "expert"), None, None),
            P(("dp", "expert"), None, None),
            P(("dp", "expert")),
            P(),
            P(),
            P("expert", None, "dp"),
            P("expert", "dp", None),
            P(),
            P(),
        ),
        out_specs=(
            P(),
            P(("dp", "expert"), None, None),
            P("expert", None, "dp"),
            P("expert", "dp", None),
            P(),
            P(),
        ),
        check_vma=False,
    )
```

```python
import functools

import jax
import jax.numpy as jnp
from jax import lax
from jax.experimental import pallas as pl
from jax.experimental.pallas import tpu as pltpu
from jax.sharding import PartitionSpec as P

D = 1024
FD = 512
PATCH = 196
CAPLEN = 16
SEQ = 212
NDP = 8
NEX = 32
MAIN = NEX * 8
ROWS = NEX * 9
META = 8
HEIGHT = ROWS + META
CUT = ROWS // 2
LANES = 384
FOLD = D
EXTRA = D + 128
SEND_W = D + 256
BACK_W = D + 384
PT = 2 * NDP * NEX
LOCAL = 2 * NEX

EPS = 1e-06
LOSS_SCALE = 1024.0
BF = jnp.bfloat16
F32 = jnp.float32
I32 = jnp.int32

VM = pl.BlockSpec(memory_space=pltpu.VMEM)
SM = pl.BlockSpec(memory_space=pltpu.SMEM)


def mm(a, b, dims=((1,), (0,))):
    return lax.dot_general(a, b, (dims, ((), ())), preferred_element_type=F32)


def io(shape, axis):
    return lax.broadcasted_iota(I32, shape, axis)


HB = pl.BlockSpec(memory_space=pltpu.HBM)


def run(kernel, outs, *args, smem=0, scratch=(), name=None, limit=6, hbm=0, spill=()):
    specs = [SM] * smem + [HB] * hbm + [VM] * (len(args) - smem - hbm)
    many = isinstance(outs, tuple)
    kinds = [n in spill for n in range(len(outs) if many else 1)]
    out_specs = tuple(HB if k else VM for k in kinds) if many else VM
    if many:
        outs = tuple(pltpu.HBM(o.shape, o.dtype) if k else o for o, k in zip(outs, kinds))
    args = tuple(pltpu.with_memory_space_constraint(a, pltpu.HBM) if smem <= n < smem + hbm else a for n, a in enumerate(args))
    return pl.pallas_call(
        kernel,
        out_shape=outs,
        in_specs=specs,
        out_specs=out_specs,
        scratch_shapes=scratch,
        name=name,
        cost_estimate=pl.CostEstimate(flops=1024, transcendentals=0, bytes_accessed=1024),
        compiler_params=pltpu.CompilerParams(vmem_limit_bytes=limit * 1024 * 1024),
    )(*args)


def shape(*dims, dtype=BF):
    return jax.ShapeDtypeStruct(dims, dtype)


def spread(k):
    return (io((MAIN, NEX), 0) == io((MAIN, NEX), 1) * 8 + k).astype(BF)


def layer_norm(x):
    mean = jnp.mean(x, axis=1, keepdims=True)
    c = x - mean
    rstd = 1.0 / jnp.sqrt(jnp.mean(c * c, axis=1, keepdims=True) + EPS)
    return c * rstd, rstd


def front_kernel(length, tok_hbm, ids_hbm, gain_hbm, send, means, place, tok, ids, gain, sems):
    copies = [
        pltpu.make_async_copy(src, dst, sems.at[k])
        for k, (src, dst) in enumerate(((tok_hbm, tok), (ids_hbm, ids), (gain_hbm, gain)))
    ]
    for copy in copies:
        copy.start()
    for copy in copies:
        copy.wait()
    n = length[0]
    x = tok[...].astype(F32)
    xhat, _ = layer_norm(x)
    xn = (xhat * gain[...]).astype(BF)
    pos = io((1, SEQ), 1)
    real = pos < PATCH + n
    owner = ids[...]
    hit = (io((NEX, SEQ), 0) == owner) & real
    onehot = jnp.where(hit, 1.0, 0.0)
    before = (io((SEQ, SEQ), 0) < io((SEQ, SEQ), 1)).astype(BF)
    slot = jnp.sum(mm(onehot.astype(BF), before) * onehot, axis=0, keepdims=True).astype(I32)
    target = jnp.where(real & (slot < 8), owner * 8 + slot, -1)
    p_main = (io((MAIN, SEQ), 0) == target).astype(BF)
    p_last = jnp.where(slot == 8, onehot, 0.0).astype(BF)
    place[:MAIN] = p_main
    place[MAIN:] = p_last
    send[:, :D] = mm(p_main, xn).astype(BF)
    last = mm(p_last, xn).astype(BF)
    fold = mm(spread(0), last[:, :128])
    for k in range(1, 8):
        fold = fold + mm(spread(k), last[:, 128 * k : 128 * (k + 1)])
    send[:, FOLD:EXTRA] = fold.astype(BF)
    images = jnp.sum(jnp.where(pos < PATCH, onehot, 0.0), axis=1, keepdims=True)
    lane = io((NEX, 128), 1)
    info = jnp.where(lane == 0, images, jnp.where(lane == 1, n.astype(F32), 0.0)).astype(BF)
    send[:, EXTRA:] = mm(spread(0), info).astype(BF)
    at = io((SEQ, 1), 0)
    w_img = jnp.where(at < PATCH, 1.0 / PATCH, 0.0)
    w_cap = jnp.where((at >= PATCH) & (at < PATCH + n), 1.0 / n.astype(F32), 0.0)
    means[0:1] = jnp.sum(x * w_img, axis=0, keepdims=True)
    means[1:2] = jnp.sum(x * w_cap, axis=0, keepdims=True)


def unpack_kernel(got, top, low):
    top[:CUT] = got[:CUT, :D]
    low[: MAIN - CUT] = got[CUT:, :D]
    info = mm(spread(0), got[:, EXTRA:SEND_W], ((0,), (0,)))
    fold = got[:, FOLD:EXTRA]
    for k in range(8):
        low[MAIN - CUT : CUT, 128 * k : 128 * (k + 1)] = mm(spread(k), fold, ((0,), (0,))).astype(BF)
    r = io((1, LANES), 1)
    ex = jnp.where(r < MAIN, r // 8, r - MAIN)
    slot = jnp.where(r < MAIN, r % 8, 8).astype(F32)
    match = io((NEX, LANES), 0) == ex
    images = jnp.sum(jnp.where(match, info[:, 0:1], 0.0), axis=0, keepdims=True)
    lens = jnp.sum(jnp.where(match, info[:, 1:2], 0.0), axis=0, keepdims=True)
    is_img = slot < images
    pt = jnp.where(r < ROWS, 2 * ex + jnp.where(is_img, 0, 1), LOCAL).astype(F32)
    div = jnp.where(r < ROWS, jnp.where(is_img, float(PATCH), lens), 1.0)
    for ref, info_row in ((top, pt), (low, div)):
        ref[CUT:, :LANES] = jnp.broadcast_to(info_row, (META, LANES)).astype(BF)
        ref[CUT:, LANES:] = jnp.zeros((META, D - LANES), BF)


CHUNK = 96


def phi_of(p):
    return 0.5 * (1.0 + lax.erf(p * 0.7071067811865476))


def slope_of(p, phi):
    return (phi + p * jnp.exp(-0.5 * p * p) * 0.3989422804014327).astype(BF)


def late_slope_kernel(*refs):
    n = len(refs) // 2
    for pre, slope in zip(refs[:n], refs[n:]):

        def step(c, _, pre=pre, slope=slope):
            at = pl.ds(pl.multiple_of(c * CHUNK, CHUNK), CHUNK)
            p = pre[at, :]
            slope[at, :] = slope_of(p, phi_of(p))
            return 0

        lax.fori_loop(0, ROWS // CHUNK, step, 0)


def forward_core(top, low, wu, router, act, slope, cols, pre, mixed):
    pre[:CUT] = mm(top[:CUT], wu[...])
    pre[CUT:] = mm(low[:CUT], wu[...])
    pt_row = top[CUT:, :LANES].astype(F32)[0:1]
    div_row = low[CUT:, :LANES].astype(F32)[0:1]

    def gates(c, _):
        at = pl.ds(pl.multiple_of(c * 48, 48), 48)
        for ref, base in ((top, 0), (low, CUT)):
            prod = ref[at, :].astype(F32) * router[...]
            t = prod[:, :128]
            for k in range(1, 8):
                t = t + prod[:, 128 * k : 128 * (k + 1)]
            cols[pl.ds(pl.multiple_of(c * 48 + base, 48), 48), :] = t
        return 0

    lax.fori_loop(0, CUT // 48, gates, 0)
    gate = jax.nn.sigmoid(jnp.sum(cols[...], axis=1, keepdims=True))
    diag = io((ROWS, LANES), 1) == io((ROWS, LANES), 0)
    div = jnp.sum(jnp.where(diag, div_row, 0.0), axis=1, keepdims=True)
    pt = jnp.sum(jnp.where(diag, pt_row, 0.0), axis=1, keepdims=True)
    lane = io((ROWS, 128), 1)
    cols[...] = jnp.where(lane == 0, gate / div, jnp.where(lane == 1, 1.0 - gate, jnp.where(lane == 2, pt, 0.0)))

    def step(c, _):
        at = pl.ds(pl.multiple_of(c * CHUNK, CHUNK), CHUNK)
        p = pre[at, :]
        phi = phi_of(p)
        a = (p * phi).astype(BF)
        act[at, :] = a
        if slope is not None:
            slope[at, :] = slope_of(p, phi)
        mixed[at, :] = (cols[at, 0:1] * a.astype(F32)).astype(BF)
        return 0

    lax.fori_loop(0, ROWS // CHUNK, step, 0)
    return (io((LOCAL, ROWS), 0).astype(F32) == pt_row[:, :ROWS]).astype(BF)


def forward_kernel(top, low, wu, router, act_out, slope_out, cols_out, pooled_out, act, slope, cols, pooled, pre, mixed, sems):
    sel = forward_core(top, low, wu, router, act, slope, cols, pre, mixed)
    outs = ((act, act_out), (slope, slope_out), (cols, cols_out), (pooled, pooled_out))
    copies = [pltpu.make_async_copy(src, dst, sems.at[k]) for k, (src, dst) in enumerate(outs)]
    for copy in copies[:3]:
        copy.start()
    pooled[...] = mm(sel, mixed[...]).astype(BF)
    copies[3].start()
    for copy in copies:
        copy.wait()


def keep_shapes():
    return (shape(ROWS, FD), shape(ROWS, FD), shape(ROWS, 128, dtype=F32))


def keep_scratch():
    return [pltpu.VMEM((ROWS, FD), BF), pltpu.VMEM((ROWS, FD), BF), pltpu.VMEM((ROWS, 128), F32)]


def forward_block(top, low, wu, router):
    out = run(
        forward_kernel,
        keep_shapes() + (shape(LOCAL, FD),),
        top,
        low,
        wu,
        router,
        scratch=keep_scratch()
        + [
            pltpu.VMEM((LOCAL, FD), BF),
            pltpu.VMEM((ROWS, FD), F32),
            pltpu.VMEM((ROWS, FD), BF),
            pltpu.SemaphoreType.DMA((4,)),
        ],
        name="expert_forward",
        spill=(0, 1, 2, 3),
    )
    return (top, low) + tuple(out)


def forward_last_kernel(offsets, late, me, *refs):
    n_late = len(late)
    early = refs[: NDP - n_late]
    refs = refs[NDP - n_late :]
    xs, refs = refs[: 2 * n_late], refs[2 * n_late :]
    wu, wd, router = refs[:3]
    outs, refs = refs[3 : 3 + 3 * n_late], refs[3 + 3 * n_late :]
    part, pooled_out = refs[:2]
    held, refs = refs[2 : 2 + 3 * n_late], refs[2 + 3 * n_late :]
    near, pooled, mixed, total, sems = refs
    copies = []
    loads = [pltpu.make_async_copy(ref, near.at[n], sems.at[3 * n_late + 1 + n]) for n, ref in enumerate(early)]
    for copy in loads:
        copy.start()
    g = io((PT, LOCAL), 0)
    p = io((PT, LOCAL), 1)
    for n in list(range(len(early), NDP)) + list(range(len(early))):
        if n < len(early):
            loads[n].wait()
            value = near[n]
        else:
            m = n - len(early)
            keep = held[3 * m : 3 * m + 3]
            act, pre, cols = keep
            sel = forward_core(xs[2 * m], xs[2 * m + 1], wu, router, act, None, cols, pre, mixed)
            for k in range(3):
                copies.append(pltpu.make_async_copy(keep[k], outs[3 * m + k], sems.at[3 * m + k]))
                copies[-1].start()
            value = mm(sel, mixed[...]).astype(BF)
        src = (me[0] + offsets[n]) % NDP
        perm = (g == (p // 2) * (2 * NDP) + (p % 2) * NDP + src).astype(BF)
        if n == len(early):
            total[...] = mm(perm, value)
        else:
            total[...] += mm(perm, value)
    pooled[...] = total[...].astype(BF)
    copies.append(pltpu.make_async_copy(pooled, pooled_out, sems.at[3 * n_late]))
    copies[-1].start()
    part[...] = mm(pooled[...], wd[...]).astype(BF)
    for copy in copies:
        copy.wait()


def forward_last(me, early, late, wu, wd, router):
    offsets = list(early) + list(late)
    n_late = len(late)
    out = run(
        functools.partial(forward_last_kernel, offsets, list(late)),
        (shape(ROWS, FD), shape(ROWS, FD, dtype=F32), shape(ROWS, 128, dtype=F32)) * n_late + (shape(PT, D), shape(PT, FD)),
        me,
        *[value[5] for value in early.values()],
        *[half for pair in late.values() for half in pair],
        wu,
        wd,
        router,
        smem=1,
        scratch=[pltpu.VMEM((ROWS, FD), BF), pltpu.VMEM((ROWS, FD), F32), pltpu.VMEM((ROWS, 128), F32)] * n_late
        + [
            pltpu.VMEM((len(early), LOCAL, FD), BF),
            pltpu.VMEM((PT, FD), BF),
            pltpu.VMEM((ROWS, FD), BF),
            pltpu.VMEM((PT, FD), F32),
            pltpu.SemaphoreType.DMA((3 * n_late + 1 + len(early),)),
        ],
        name="forward_last",
        hbm=len(early),
        limit=10,
        spill=tuple(range(3 * n_late)) + (3 * n_late + 1,),
    )
    saved = dict(early)
    slopes = run(late_slope_kernel, (shape(ROWS, FD),) * n_late, *out[1 : 3 * n_late : 3], name="late_slope")
    for n, off in enumerate(late):
        saved[off] = tuple(late[off]) + (out[3 * n], slopes[n], out[3 * n + 2], None)
    return saved, out[3 * n_late], out[3 * n_late + 1]


def column_kernel(me, got, means, out):
    s = jnp.sum(got[...].astype(F32), axis=0)
    row = io((2 * NDP, 1), 0)
    s = s + jnp.where(row == me[0], means[0:1], 0.0) + jnp.where(row == me[0] + NDP, means[1:2], 0.0)
    out[...] = jnp.broadcast_to(s.astype(BF)[None], (NDP, 2 * NDP, D))


def share_kernel(got, out):
    s = jnp.sum(got[...].astype(F32), axis=0)
    out[...] = jnp.broadcast_to(s.astype(BF)[None], (NEX, 2 * NDP, D))


def loss_kernel(me, scale, bias, emb, wd, loss, d_emb, dy, q, grads):
    n = PT // 2
    u = emb[:, :NDP].reshape(n, D)
    v = emb[:, NDP:].reshape(n, D)
    dots = mm(u, v, ((1,), (1,)))
    i = io((n, n), 0)
    j = io((n, n), 1)
    same = i == j

    def norms(a):
        on = jnp.where(same, mm(a, a, ((1,), (1,))), 0.0)
        col = 1.0 / jnp.sqrt(jnp.sum(on, axis=1, keepdims=True) / D + EPS)
        row = 1.0 / jnp.sqrt(jnp.sum(on, axis=0, keepdims=True) / D + EPS)
        return col, row

    iu, iu_row = norms(u)
    iv, iv_row = norms(v)
    to_unit = scale[0] / D
    sign = jnp.where(same, 1.0, -1.0)
    z = sign * (dots * to_unit * iu * iv_row + bias[0])
    t = jnp.exp(-jnp.abs(z))
    soft = jnp.maximum(-z, 0.0) + jnp.log1p(t)
    loss[...] = jnp.sum(jnp.sum(soft, axis=0, keepdims=True), axis=1, keepdims=True) / n
    coef = (-LOSS_SCALE / n) * sign * (jnp.where(z >= 0.0, t, 1.0) / (1.0 + t)) * to_unit
    for_u = coef * iv_row
    for_v = coef * iu

    def halves(c):
        hi = c.astype(BF)
        return hi, (c - hi.astype(F32)).astype(BF)

    u_hi, u_lo = halves(for_u)
    v_hi, v_lo = halves(for_v)
    u_dot = jnp.sum(for_u * dots, axis=1, keepdims=True)
    v_dot_row = jnp.sum(for_v * dots, axis=0, keepdims=True)
    v_dot = jnp.sum(jnp.where(same, v_dot_row, 0.0), axis=1, keepdims=True)
    grads[0] = (mm(u_hi, v) + mm(u_lo, v)) * iu - u.astype(F32) * (iu * iu * iu * u_dot / D)
    first = ((0,), (0,))
    grads[1] = (mm(v_hi, u, first) + mm(v_lo, u, first)) * iv - v.astype(F32) * (iv * iv * iv * v_dot / D)
    d_emb[:, :NDP] = grads[0].astype(BF).reshape(NEX, NDP, D)
    d_emb[:, NDP:] = grads[1].astype(BF).reshape(NEX, NDP, D)
    raw = mm(d_emb[...].reshape(PT, D), wd[...], ((1,), (1,))).astype(BF)
    r = io((PT, PT), 0)
    at = (r % LOCAL) // 2 * (2 * NDP) + (r % 2) * NDP + r // LOCAL
    perm = (io((PT, PT), 1) == at).astype(BF)
    q[...] = mm(perm, raw).astype(BF)
    row = io((NDP, 1), 0)
    near = pl.ds(pl.multiple_of(me[1] * NDP, NDP), NDP)
    for kind in range(2):
        dy[kind : kind + 1] = jnp.sum(jnp.where(row == me[0], grads[kind, near, :], 0.0), axis=0, keepdims=True)


def slope_kernel(off, me, q, act, slope, cols, dpre, dgl, dact, partial):
    src = (me[0] + off) % NDP
    qb = q[pl.ds(pl.multiple_of(src * LOCAL, LOCAL), LOCAL), :]
    pick = (io((ROWS, LOCAL), 1).astype(F32) == cols[:, 2:3]).astype(BF)
    dact[...] = mm(pick, qb)

    for c in range(0, ROWS, CHUNK):
        at = pl.ds(c, CHUNK)
        da = dact[at, :] * cols[at, 0:1]
        dpre[at, :] = (da * slope[at, :].astype(F32)).astype(BF)
        prod = da * act[at, :].astype(F32)
        partial[at, :] = prod[:, :128] + prod[:, 128:256] + prod[:, 256:384] + prod[:, 384:]
    dgl[...] = jnp.broadcast_to(jnp.sum(partial[...], axis=1, keepdims=True) * cols[:, 1:2], (ROWS, 128))


def slope_block(off, me, q, saved):
    _, _, act, slope, cols, _ = saved
    return run(
        functools.partial(slope_kernel, off),
        (shape(ROWS, FD), shape(ROWS, 128, dtype=F32)),
        me,
        q,
        act,
        slope,
        cols,
        smem=1,
        scratch=[pltpu.VMEM((ROWS, FD), F32), pltpu.VMEM((ROWS, 128), F32)],
        name="expert_slope",
    )


def half_value(upper, x, dpre, dgl, wu, router):
    rows = slice(0, CUT) if upper else slice(CUT, ROWS)
    col = dgl[rows, 0:1]
    v = mm(dpre[rows], wu[...], ((1,), (1,))) + col * router[...]
    xf = x[:CUT].astype(F32)
    return v, jnp.sum(xf * col, axis=0, keepdims=True), jnp.sum(xf * v, axis=0, keepdims=True)


def back_far_kernel(added, x_a_hbm, x_b_hbm, dpre_a, dgl_a, dpre_b, dgl_b, wu, router, *refs):
    got_a, got_b = refs[:2] if added else (None, None)
    out_a, out_b, sums, x_a, x_b, sems = refs[2 if added else 0 :]
    loads = [pltpu.make_async_copy(x_a_hbm, x_a, sems.at[0]), pltpu.make_async_copy(x_b_hbm, x_b, sems.at[1])]
    for copy in loads:
        copy.start()
    col_a = dgl_a[:CUT, 0:1]
    col_b = dgl_b[CUT:, 0:1]
    v_a = mm(dpre_a[:CUT], wu[...], ((1,), (1,))) + col_a * router[...]
    v_b = mm(dpre_b[CUT:], wu[...], ((1,), (1,))) + col_b * router[...]
    out_a[...] = (v_a + got_a[...].astype(F32) if added else v_a).astype(BF)
    out_b[...] = (v_b + got_b[...].astype(F32) if added else v_b).astype(BF)
    for copy in loads:
        copy.wait()
    xf_a = x_a[:CUT].astype(F32)
    xf_b = x_b[:CUT].astype(F32)
    sums[0:1] = jnp.sum(xf_a * col_a, axis=0, keepdims=True) + jnp.sum(xf_b * col_b, axis=0, keepdims=True)
    sums[1:2] = jnp.sum(xf_a * v_a, axis=0, keepdims=True) + jnp.sum(xf_b * v_b, axis=0, keepdims=True)


def back_add_kernel(x_a, dpre_a, dgl_a, x_b, dpre_b, dgl_b, wu, router, got_a, got_b, out_a, out_b, sums):
    v_a, r_a, g_a = half_value(True, x_a, dpre_a, dgl_a, wu, router)
    v_b, r_b, g_b = half_value(False, x_b, dpre_b, dgl_b, wu, router)
    out_a[...] = (v_a + got_a[...].astype(F32)).astype(BF)
    out_b[...] = (v_b + got_b[...].astype(F32)).astype(BF)
    sums[0:1] = r_a + r_b
    sums[1:2] = g_a + g_b


def back_near_kernel(top, low, dpre, dgl, wu, router, out, sums):
    v_a, r_a, g_a = half_value(True, top, dpre, dgl, wu, router)
    v_b, r_b, g_b = half_value(False, low, dpre, dgl, wu, router)
    out[:CUT] = v_a
    out[CUT:] = v_b
    sums[0:1] = r_a + r_b
    sums[1:2] = g_a + g_b


def back_sums_kernel(top, low, dpre, dgl, wu, router, sums):
    _, r_a, g_a = half_value(True, top, dpre, dgl, wu, router)
    _, r_b, g_b = half_value(False, low, dpre, dgl, wu, router)
    sums[0:1] = r_a + r_b
    sums[1:2] = g_a + g_b


def add_kernel(near, got_a, got_b, out):
    out[:CUT] = (near[:CUT] + got_a[...].astype(F32)).astype(BF)
    out[CUT:] = (near[CUT:] + got_b[...].astype(F32)).astype(BF)


def total_kernel(*refs):
    out = refs[-1]
    total = refs[0][...]
    for ref in refs[1:-1]:
        total = total + ref[...]
    out[...] = jnp.broadcast_to(total[None], (NDP, 2, D))


SUMS = shape(2, D, dtype=F32)


def back_pair(far, block_a, slope_a, block_b, slope_b, wu, router, got=()):
    outs = (shape(CUT, D), shape(CUT, D), SUMS)
    if far:
        return run(
            functools.partial(back_far_kernel, bool(got)),
            outs,
            block_a[0],
            block_b[1],
            *slope_a,
            *slope_b,
            wu,
            router,
            *got,
            hbm=2,
            scratch=[pltpu.VMEM((CUT + META, D), BF), pltpu.VMEM((CUT + META, D), BF), pltpu.SemaphoreType.DMA((2,))],
            name="back_far",
        )
    return run(back_add_kernel, outs, block_a[0], *slope_a, block_b[1], *slope_b, wu, router, *got, name="back_pair")


def back_own_kernel(dpre, dgl, wu, router, out):
    out[...] = mm(dpre[...], wu[...], ((1,), (1,))) + dgl[:, 0:1] * router[...]


def back_last_kernel(r_hbm, l_hbm, own, small, send, r, l, sems):
    loads = [pltpu.make_async_copy(r_hbm, r, sems.at[0]), pltpu.make_async_copy(l_hbm, l, sems.at[1])]
    for copy in loads:
        copy.start()
    total = jnp.sum(small[...], axis=0)
    sub = io((MAIN, 128), 0) % 8
    for n in range(2):
        value = jnp.zeros((MAIN, 128), F32)
        for k in range(8):
            value = jnp.where(sub == k, total[n : n + 1, 128 * k : 128 * (k + 1)], value)
        send[:, EXTRA + 128 * n : EXTRA + 128 * (n + 1)] = value.astype(BF)
    for copy in loads:
        copy.wait()
    v = (own[...] + r[...].astype(F32) + l[...].astype(F32)).astype(BF)
    send[:, :D] = v[:MAIN]
    last = v[MAIN:]
    fold = mm(spread(0), last[:, :128])
    for k in range(1, 8):
        fold = fold + mm(spread(k), last[:, 128 * k : 128 * (k + 1)])
    send[:, FOLD:EXTRA] = fold.astype(BF)


def weight_kernel(*refs):
    tops, lows, dpres = (refs[NDP * k : NDP * (k + 1)] for k in range(3))
    grad_up = refs[3 * NDP]
    step_cols = 256

    def step(c, _):
        at = pl.ds(pl.multiple_of(c * step_cols, step_cols), step_cols)
        total = None
        for n in range(NDP):
            x = jnp.concatenate([tops[n][:CUT, at], lows[n][:CUT, at]], axis=0)
            term = mm(x, dpres[n][...], ((0,), (0,)))
            total = term if total is None else total + term
        grad_up[at, :] = total
        return 0

    lax.fori_loop(0, D // step_cols, step, 0)


def down_kernel(pooled, d_emb, out):
    out[...] = mm(pooled[...], d_emb[...].reshape(PT, D), ((0,), (0,)))


def final_kernel(length, tok_hbm, place_hbm, gain, got, dy, grad_tokens, grad_router, gain_grad, tok, place, sems):
    n = length[0]
    load_place = pltpu.make_async_copy(place_hbm, place, sems.at[0])
    load_tok = pltpu.make_async_copy(tok_hbm, tok, sems.at[1])
    load_place.start()
    load_tok.start()
    fold = got[:, FOLD:EXTRA]
    ones = [mm(spread(k), fold, ((0,), (0,))).astype(BF) for k in range(8)]
    last = jnp.concatenate(ones, axis=1)
    for k in range(8):
        at_k = slice(128 * k, 128 * (k + 1))
        piece = mm(spread(k), got[:, EXTRA:], ((0,), (0,)))
        grad_router[:, at_k] = piece[:, :128]
        gain_grad[:, at_k] = jnp.sum(piece[:, 128:], axis=0, keepdims=True) / gain[:, at_k]
    load_place.wait()
    dxn = mm(place[:MAIN], got[:, :D], ((0,), (0,))) + mm(place[MAIN:], last, ((0,), (0,)))
    load_tok.wait()
    xhat, rstd = layer_norm(tok[...].astype(F32))
    at = io((SEQ, 1), 0)
    w_img = jnp.where(at < PATCH, 1.0 / PATCH, 0.0)
    w_cap = jnp.where((at >= PATCH) & (at < PATCH + n), 1.0 / n.astype(F32), 0.0)
    g = dxn * gain[...]
    inner = jnp.sum(g * xhat, axis=1, keepdims=True) / D
    dx = (g - jnp.mean(g, axis=1, keepdims=True) - xhat * inner) * rstd
    grad_tokens[...] = (dx + w_img * dy[0:1] + w_cap * dy[1:2]).astype(BF)


def weight_grads(saved, dpres, offsets):
    return run(
        weight_kernel,
        shape(D, FD, dtype=F32),
        *[saved[off][0] for off in offsets],
        *[saved[off][1] for off in offsets],
        *dpres,
        name="weight_grads",
        limit=12,
    )


def exchange(value, axis):
    return lax.all_to_all(value, axis, split_axis=0, concat_axis=0, tiled=True)


def body(tokens, expert_ids, caption_lengths, gain, router, w_up, w_down, logit_scale, logit_bias):
    me_dp = lax.axis_index("dp").astype(I32)
    me_ex = lax.axis_index("expert").astype(I32)
    me = jnp.stack([me_dp, me_ex])
    wu = w_up[0]
    wd = w_down[0]
    tok = tokens[0]
    gain_row = gain.reshape(1, D)
    send, means, place = run(
        front_kernel,
        (shape(MAIN, SEND_W), shape(2, D, dtype=F32), shape(ROWS, SEQ)),
        caption_lengths,
        tok,
        expert_ids.reshape(1, SEQ),
        gain_row,
        smem=1,
        name="front",
        hbm=3,
        scratch=[
            pltpu.VMEM((SEQ, D), BF),
            pltpu.VMEM((1, SEQ), I32),
            pltpu.VMEM((1, D), F32),
            pltpu.SemaphoreType.DMA((3,)),
        ],
    )
    got = exchange(send.reshape(NEX, 8, SEND_W), "expert").reshape(MAIN, SEND_W)
    top, low = run(unpack_kernel, (shape(CUT + META, D), shape(CUT + META, D)), got, name="unpack")

    right = [(i, (i + 1) % NDP) for i in range(NDP)]
    left = [(i, (i - 1) % NDP) for i in range(NDP)]
    half = NDP // 2
    router_row = jnp.sum(jnp.where(jnp.arange(NEX, dtype=I32)[None, :] == me_ex, router, 0.0), axis=1).reshape(1, D)
    to_right = functools.partial(lax.ppermute, axis_name="dp", perm=right)
    to_left = functools.partial(lax.ppermute, axis_name="dp", perm=left)
    ra, la, rb, lb = top, top, low, low
    saved = {}
    pin = lax.optimization_barrier
    blocks = {0: (top, low)}

    def forward(off):
        saved[off] = forward_block(*blocks[off], wu, router_row)
        return saved[off]

    pinned_first = {2: 0, 3: -1, 4: -2}
    pinned_second = {3: 1}
    for k in range(1, half + 1):
        if k in pinned_first:
            off = pinned_first[k]
            ra, lb, saved[off] = pin((ra, lb, forward(off)))
        ra, lb = pin((to_right(ra), to_left(lb)))
        if k < half:
            if k in pinned_second:
                off = pinned_second[k]
                rb, la, saved[off] = pin((rb, la, forward(off)))
            rb, la = pin((to_right(rb), to_left(la)))
            blocks[-k] = (ra, rb)
            blocks[k] = (la, lb)
    forward(2)
    blocks[half] = (ra, lb)
    late = {off: blocks[off] for off in (1 - half, half - 1, half)}
    saved, part, pooled = forward_last(me, saved, late, wu, wd, router_row)
    offsets = list(saved)
    part = exchange(part.reshape(NEX, 2 * NDP, D), "expert")
    column = run(column_kernel, shape(NDP, 2 * NDP, D), me, part, means, smem=1, name="column")
    column = exchange(column, "dp")
    shared = run(share_kernel, shape(NEX, 2 * NDP, D), column, name="share")
    emb = exchange(shared, "expert")
    loss, d_emb, dy, q = run(
        loss_kernel,
        (shape(1, 1, dtype=F32), shape(NEX, 2 * NDP, D), shape(2, D, dtype=F32), shape(PT, FD)),
        me,
        logit_scale,
        logit_bias,
        emb,
        wd,
        smem=3,
        scratch=[pltpu.VMEM((2, PT // 2, D), F32)],
        limit=16,
        name="pair_loss",
    )

    slopes = {off: slope_block(off, me, q, saved[off]) for off in (half, half - 1, 1 - half, 2, -2, 1, -1, 0)}
    sums = []

    def pair(a, b, got=()):
        out = back_pair(a in late, saved[a], slopes[a], saved[b], slopes[b], wu, router_row, got)
        sums.append(out[2])
        return out[:2]

    def near(off):
        v, part_sums = run(
            back_near_kernel, (shape(ROWS, D, dtype=F32), SUMS), *saved[off][:2], *slopes[off], wu, router_row, name="back_near"
        )
        sums.append(part_sums)
        return v

    ra, lb = pair(half, half)
    la, rb = pair(1 - half, half - 1)
    for k in range(half - 1, 0, -1):
        ra, lb = pin((to_right(ra), to_left(lb)))
        if k > 1:
            rb, la = pin((to_right(rb), to_left(la)))
            ra, lb = pair(k, -k, (ra, lb))
        if k > 2:
            la, rb = pair(1 - k, k - 1, (la, rb))
    nears = {off: near(off) for off in (1, -1)}
    sums.append(run(back_sums_kernel, SUMS, *saved[0][:2], *slopes[0], wu, router_row, name="back_sums"))
    small = run(total_kernel, shape(NDP, 2, D, dtype=F32), *sums, name="total")
    r = run(add_kernel, shape(ROWS, D), nears[1], ra, rb, name="back_add")
    l = run(add_kernel, shape(ROWS, D), nears[-1], la, lb, name="back_add")
    r, l, small = pin((r, l, small))
    r, l = pin((to_right(r), to_left(l)))
    small = exchange(small, "dp")
    own_back = run(back_own_kernel, shape(ROWS, D, dtype=F32), *slopes[0], wu, router_row, name="back_own")
    send = run(back_last_kernel, shape(MAIN, BACK_W), r, l, own_back, small, hbm=2, scratch=[pltpu.VMEM((ROWS, D), BF), pltpu.VMEM((ROWS, D), BF), pltpu.SemaphoreType.DMA((2,))], name="back_last")
    send, dpres = pin((send, [slopes[off][0] for off in offsets]))
    grad_up = weight_grads(saved, dpres, offsets)
    grad_down = run(down_kernel, shape(FD, D, dtype=F32), pooled, d_emb, name="down_grad")
    got = exchange(send.reshape(NEX, 8, BACK_W), "expert").reshape(MAIN, BACK_W)
    grad_tokens, grad_router, gain_grad = run(
        final_kernel,
        (shape(SEQ, D), shape(NEX, D, dtype=F32), shape(1, D, dtype=F32)),
        caption_lengths,
        tok,
        place,
        gain_row,
        got,
        dy,
        smem=1,
        hbm=2,
        scratch=[pltpu.VMEM((SEQ, D), BF), pltpu.VMEM((ROWS, SEQ), BF), pltpu.SemaphoreType.DMA((2,))],
        name="final",
    )
    return (loss.reshape(1), grad_tokens[None], grad_up[None], grad_down[None], grad_router.T, gain_grad.reshape(D))


def solution(mesh):
    return jax.shard_map(
        body,
        mesh=mesh,
        in_specs=(
            P(("dp", "expert"), None, None),
            P(("dp", "expert"), None, None),
            P(("dp", "expert")),
            P(),
            P(),
            P("expert", None, "dp"),
            P("expert", "dp", None),
            P(),
            P(),
        ),
        out_specs=(
            P(),
            P(("dp", "expert"), None, None),
            P("expert", None, "dp"),
            P("expert", "dp", None),
            P(),
            P(),
        ),
        check_vma=False,
    )
```

```python
import functools

import jax
import jax.numpy as jnp
from jax import lax
from jax.experimental import pallas as pl
from jax.experimental.pallas import tpu as pltpu
from jax.sharding import PartitionSpec as P

D = 1024
FD = 512
PATCH = 196
CAPLEN = 16
SEQ = 212
NDP = 8
NEX = 32
MAIN = NEX * 8
ROWS = NEX * 9
META = 8
HEIGHT = ROWS + META
CUT = ROWS // 2
LANES = 384
FOLD = D
EXTRA = D + 128
SEND_W = D + 256
BACK_W = D + 384
PT = 2 * NDP * NEX
LOCAL = 2 * NEX

EPS = 1e-06
LOSS_SCALE = 1024.0
BF = jnp.bfloat16
F32 = jnp.float32
I32 = jnp.int32

VM = pl.BlockSpec(memory_space=pltpu.VMEM)
SM = pl.BlockSpec(memory_space=pltpu.SMEM)


def mm(a, b, dims=((1,), (0,))):
    return lax.dot_general(a, b, (dims, ((), ())), preferred_element_type=F32)


def io(shape, axis):
    return lax.broadcasted_iota(I32, shape, axis)


HB = pl.BlockSpec(memory_space=pltpu.HBM)


def run(kernel, outs, *args, smem=0, scratch=(), name=None, limit=6, hbm=0, spill=()):
    specs = [SM] * smem + [HB] * hbm + [VM] * (len(args) - smem - hbm)
    many = isinstance(outs, tuple)
    kinds = [n in spill for n in range(len(outs) if many else 1)]
    out_specs = tuple(HB if k else VM for k in kinds) if many else VM
    if many:
        outs = tuple(pltpu.HBM(o.shape, o.dtype) if k else o for o, k in zip(outs, kinds))
    args = tuple(pltpu.with_memory_space_constraint(a, pltpu.HBM) if smem <= n < smem + hbm else a for n, a in enumerate(args))
    return pl.pallas_call(
        kernel,
        out_shape=outs,
        in_specs=specs,
        out_specs=out_specs,
        scratch_shapes=scratch,
        name=name,
        cost_estimate=pl.CostEstimate(flops=1024, transcendentals=0, bytes_accessed=1024),
        compiler_params=pltpu.CompilerParams(vmem_limit_bytes=limit * 1024 * 1024),
    )(*args)


def shape(*dims, dtype=BF):
    return jax.ShapeDtypeStruct(dims, dtype)


def spread(k):
    return (io((MAIN, NEX), 0) == io((MAIN, NEX), 1) * 8 + k).astype(BF)


def layer_norm(x):
    mean = jnp.mean(x, axis=1, keepdims=True)
    c = x - mean
    rstd = 1.0 / jnp.sqrt(jnp.mean(c * c, axis=1, keepdims=True) + EPS)
    return c * rstd, rstd


def front_kernel(length, tok_hbm, ids_hbm, gain_hbm, send, means, place, tok, ids, gain, sems):
    copies = [
        pltpu.make_async_copy(src, dst, sems.at[k])
        for k, (src, dst) in enumerate(((tok_hbm, tok), (ids_hbm, ids), (gain_hbm, gain)))
    ]
    for copy in copies:
        copy.start()
    for copy in copies:
        copy.wait()
    n = length[0]
    x = tok[...].astype(F32)
    xhat, _ = layer_norm(x)
    xn = (xhat * gain[...]).astype(BF)
    pos = io((1, SEQ), 1)
    real = pos < PATCH + n
    owner = ids[...]
    hit = (io((NEX, SEQ), 0) == owner) & real
    onehot = jnp.where(hit, 1.0, 0.0)
    before = (io((SEQ, SEQ), 0) < io((SEQ, SEQ), 1)).astype(BF)
    slot = jnp.sum(mm(onehot.astype(BF), before) * onehot, axis=0, keepdims=True).astype(I32)
    target = jnp.where(real & (slot < 8), owner * 8 + slot, -1)
    p_main = (io((MAIN, SEQ), 0) == target).astype(BF)
    p_last = jnp.where(slot == 8, onehot, 0.0).astype(BF)
    place[:MAIN] = p_main
    place[MAIN:] = p_last
    send[:, :D] = mm(p_main, xn).astype(BF)
    last = mm(p_last, xn).astype(BF)
    fold = mm(spread(0), last[:, :128])
    for k in range(1, 8):
        fold = fold + mm(spread(k), last[:, 128 * k : 128 * (k + 1)])
    send[:, FOLD:EXTRA] = fold.astype(BF)
    images = jnp.sum(jnp.where(pos < PATCH, onehot, 0.0), axis=1, keepdims=True)
    lane = io((NEX, 128), 1)
    info = jnp.where(lane == 0, images, jnp.where(lane == 1, n.astype(F32), 0.0)).astype(BF)
    send[:, EXTRA:] = mm(spread(0), info).astype(BF)
    at = io((SEQ, 1), 0)
    w_img = jnp.where(at < PATCH, 1.0 / PATCH, 0.0)
    w_cap = jnp.where((at >= PATCH) & (at < PATCH + n), 1.0 / n.astype(F32), 0.0)
    means[0:1] = jnp.sum(x * w_img, axis=0, keepdims=True)
    means[1:2] = jnp.sum(x * w_cap, axis=0, keepdims=True)


def unpack_kernel(got, top, low):
    top[:CUT] = got[:CUT, :D]
    low[: MAIN - CUT] = got[CUT:, :D]
    info = mm(spread(0), got[:, EXTRA:SEND_W], ((0,), (0,)))
    fold = got[:, FOLD:EXTRA]
    for k in range(8):
        low[MAIN - CUT : CUT, 128 * k : 128 * (k + 1)] = mm(spread(k), fold, ((0,), (0,))).astype(BF)
    r = io((1, LANES), 1)
    ex = jnp.where(r < MAIN, r // 8, r - MAIN)
    slot = jnp.where(r < MAIN, r % 8, 8).astype(F32)
    match = io((NEX, LANES), 0) == ex
    images = jnp.sum(jnp.where(match, info[:, 0:1], 0.0), axis=0, keepdims=True)
    lens = jnp.sum(jnp.where(match, info[:, 1:2], 0.0), axis=0, keepdims=True)
    is_img = slot < images
    pt = jnp.where(r < ROWS, 2 * ex + jnp.where(is_img, 0, 1), LOCAL).astype(F32)
    div = jnp.where(r < ROWS, jnp.where(is_img, float(PATCH), lens), 1.0)
    for ref, info_row in ((top, pt), (low, div)):
        ref[CUT:, :LANES] = jnp.broadcast_to(info_row, (META, LANES)).astype(BF)
        ref[CUT:, LANES:] = jnp.zeros((META, D - LANES), BF)


CHUNK = 96


def phi_of(p):
    return 0.5 * (1.0 + lax.erf(p * 0.7071067811865476))


def slope_of(p, phi):
    return (phi + p * jnp.exp(-0.5 * p * p) * 0.3989422804014327).astype(BF)


def late_slope_kernel(*refs):
    n = len(refs) // 2
    for pre, slope in zip(refs[:n], refs[n:]):

        def step(c, _, pre=pre, slope=slope):
            at = pl.ds(pl.multiple_of(c * CHUNK, CHUNK), CHUNK)
            p = pre[at, :]
            slope[at, :] = slope_of(p, phi_of(p))
            return 0

        lax.fori_loop(0, ROWS // CHUNK, step, 0)


def forward_core(top, low, wu, router, act, slope, cols, pre, mixed):
    pre[:CUT] = mm(top[:CUT], wu[...])
    pre[CUT:] = mm(low[:CUT], wu[...])
    pt_row = top[CUT:, :LANES].astype(F32)[0:1]
    div_row = low[CUT:, :LANES].astype(F32)[0:1]

    def gates(c, _):
        at = pl.ds(pl.multiple_of(c * 48, 48), 48)
        for ref, base in ((top, 0), (low, CUT)):
            prod = ref[at, :].astype(F32) * router[...]
            t = prod[:, :128]
            for k in range(1, 8):
                t = t + prod[:, 128 * k : 128 * (k + 1)]
            cols[pl.ds(pl.multiple_of(c * 48 + base, 48), 48), :] = t
        return 0

    lax.fori_loop(0, CUT // 48, gates, 0)
    gate = jax.nn.sigmoid(jnp.sum(cols[...], axis=1, keepdims=True))
    diag = io((ROWS, LANES), 1) == io((ROWS, LANES), 0)
    div = jnp.sum(jnp.where(diag, div_row, 0.0), axis=1, keepdims=True)
    pt = jnp.sum(jnp.where(diag, pt_row, 0.0), axis=1, keepdims=True)
    lane = io((ROWS, 128), 1)
    cols[...] = jnp.where(lane == 0, gate / div, jnp.where(lane == 1, 1.0 - gate, jnp.where(lane == 2, pt, 0.0)))

    def step(c, _):
        at = pl.ds(pl.multiple_of(c * CHUNK, CHUNK), CHUNK)
        p = pre[at, :]
        phi = phi_of(p)
        a = (p * phi).astype(BF)
        act[at, :] = a
        if slope is not None:
            slope[at, :] = slope_of(p, phi)
        mixed[at, :] = (cols[at, 0:1] * a.astype(F32)).astype(BF)
        return 0

    lax.fori_loop(0, ROWS // CHUNK, step, 0)
    return (io((LOCAL, ROWS), 0).astype(F32) == pt_row[:, :ROWS]).astype(BF)


def forward_kernel(top, low, wu, router, act_out, slope_out, cols_out, pooled_out, act, slope, cols, pooled, pre, mixed, sems):
    sel = forward_core(top, low, wu, router, act, slope, cols, pre, mixed)
    outs = ((act, act_out), (slope, slope_out), (cols, cols_out), (pooled, pooled_out))
    copies = [pltpu.make_async_copy(src, dst, sems.at[k]) for k, (src, dst) in enumerate(outs)]
    for copy in copies[:3]:
        copy.start()
    pooled[...] = mm(sel, mixed[...]).astype(BF)
    copies[3].start()
    for copy in copies:
        copy.wait()


def keep_shapes():
    return (shape(ROWS, FD), shape(ROWS, FD), shape(ROWS, 128, dtype=F32))


def keep_scratch():
    return [pltpu.VMEM((ROWS, FD), BF), pltpu.VMEM((ROWS, FD), BF), pltpu.VMEM((ROWS, 128), F32)]


def forward_block(top, low, wu, router):
    out = run(
        forward_kernel,
        keep_shapes() + (shape(LOCAL, FD),),
        top,
        low,
        wu,
        router,
        scratch=keep_scratch()
        + [
            pltpu.VMEM((LOCAL, FD), BF),
            pltpu.VMEM((ROWS, FD), F32),
            pltpu.VMEM((ROWS, FD), BF),
            pltpu.SemaphoreType.DMA((4,)),
        ],
        name="expert_forward",
        spill=(0, 1, 2, 3),
    )
    return (top, low) + tuple(out)


def forward_last_kernel(offsets, late, me, *refs):
    n_late = len(late)
    early = refs[: NDP - n_late]
    refs = refs[NDP - n_late :]
    xs, refs = refs[: 2 * n_late], refs[2 * n_late :]
    wu, wd, router = refs[:3]
    outs, refs = refs[3 : 3 + 3 * n_late], refs[3 + 3 * n_late :]
    part, pooled_out = refs[:2]
    held, refs = refs[2 : 2 + 3 * n_late], refs[2 + 3 * n_late :]
    near, pooled, mixed, total, sems = refs
    copies = []
    loads = [pltpu.make_async_copy(ref, near.at[n], sems.at[3 * n_late + 1 + n]) for n, ref in enumerate(early)]
    for copy in loads:
        copy.start()
    for n in list(range(len(early), NDP)) + list(range(len(early))):
        if n < len(early):
            loads[n].wait()
            value = near[n]
        else:
            m = n - len(early)
            keep = held[3 * m : 3 * m + 3]
            act, pre, cols = keep
            sel = forward_core(xs[2 * m], xs[2 * m + 1], wu, router, act, None, cols, pre, mixed)
            for k in range(3):
                copies.append(pltpu.make_async_copy(keep[k], outs[3 * m + k], sems.at[3 * m + k]))
                copies[-1].start()
            value = mm(sel, mixed[...])
        src = (me[0] + offsets[n]) % NDP
        value = value.astype(F32)
        for k in range(FD // 128):
            total[k, pl.ds(src, LOCAL, stride=NDP), :] = value[:, 128 * k : 128 * (k + 1)]
    for k in range(FD // 128):
        pooled[:, 128 * k : 128 * (k + 1)] = total[k].astype(BF)
    copies.append(pltpu.make_async_copy(pooled, pooled_out, sems.at[3 * n_late]))
    copies[-1].start()
    part[...] = mm(pooled[...], wd[...]).astype(BF)
    for copy in copies:
        copy.wait()


def forward_last(me, early, late, wu, wd, router):
    offsets = list(early) + list(late)
    n_late = len(late)
    out = run(
        functools.partial(forward_last_kernel, offsets, list(late)),
        (shape(ROWS, FD), shape(ROWS, FD, dtype=F32), shape(ROWS, 128, dtype=F32)) * n_late + (shape(PT, D), shape(PT, FD)),
        me,
        *[value[5] for value in early.values()],
        *[half for pair in late.values() for half in pair],
        wu,
        wd,
        router,
        smem=1,
        scratch=[pltpu.VMEM((ROWS, FD), BF), pltpu.VMEM((ROWS, FD), F32), pltpu.VMEM((ROWS, 128), F32)] * n_late
        + [
            pltpu.VMEM((len(early), LOCAL, FD), BF),
            pltpu.VMEM((PT, FD), BF),
            pltpu.VMEM((ROWS, FD), BF),
            pltpu.VMEM((FD // 128, PT, 128), F32),
            pltpu.SemaphoreType.DMA((3 * n_late + 1 + len(early),)),
        ],
        name="forward_last",
        hbm=len(early),
        limit=10,
        spill=tuple(range(3 * n_late)) + (3 * n_late + 1,),
    )
    saved = dict(early)
    slopes = run(late_slope_kernel, (shape(ROWS, FD),) * n_late, *out[1 : 3 * n_late : 3], name="late_slope")
    for n, off in enumerate(late):
        saved[off] = tuple(late[off]) + (out[3 * n], slopes[n], out[3 * n + 2], None)
    return saved, out[3 * n_late], out[3 * n_late + 1]


def column_kernel(me, got, means, out):
    s = jnp.sum(got[...].astype(F32), axis=0)
    row = io((2 * NDP, 1), 0)
    s = s + jnp.where(row == me[0], means[0:1], 0.0) + jnp.where(row == me[0] + NDP, means[1:2], 0.0)
    out[...] = jnp.broadcast_to(s.astype(BF)[None], (NDP, 2 * NDP, D))


def share_kernel(got, out):
    s = jnp.sum(got[...].astype(F32), axis=0)
    out[...] = jnp.broadcast_to(s.astype(BF)[None], (NEX, 2 * NDP, D))


def loss_kernel(me, scale, bias, emb, wd, loss, d_emb, dy, q, grads):
    n = PT // 2
    u = emb[:, :NDP].reshape(n, D)
    v = emb[:, NDP:].reshape(n, D)
    dots = mm(u, v, ((1,), (1,)))
    i = io((n, n), 0)
    j = io((n, n), 1)
    same = i == j

    def norms(a):
        on = jnp.where(same, mm(a, a, ((1,), (1,))), 0.0)
        col = 1.0 / jnp.sqrt(jnp.sum(on, axis=1, keepdims=True) / D + EPS)
        row = 1.0 / jnp.sqrt(jnp.sum(on, axis=0, keepdims=True) / D + EPS)
        return col, row

    iu, iu_row = norms(u)
    iv, iv_row = norms(v)
    to_unit = scale[0] / D
    sign = jnp.where(same, 1.0, -1.0)
    z = sign * (dots * to_unit * iu * iv_row + bias[0])
    t = jnp.exp(-jnp.abs(z))
    soft = jnp.maximum(-z, 0.0) + jnp.log1p(t)
    loss[...] = jnp.sum(jnp.sum(soft, axis=0, keepdims=True), axis=1, keepdims=True) / n
    coef = (-LOSS_SCALE / n) * sign * (jnp.where(z >= 0.0, t, 1.0) / (1.0 + t)) * to_unit
    for_u = coef * iv_row
    for_v = coef * iu

    def halves(c):
        hi = c.astype(BF)
        return hi, (c - hi.astype(F32)).astype(BF)

    u_hi, u_lo = halves(for_u)
    v_hi, v_lo = halves(for_v)
    u_dot = jnp.sum(for_u * dots, axis=1, keepdims=True)
    v_dot_row = jnp.sum(for_v * dots, axis=0, keepdims=True)
    v_dot = jnp.sum(jnp.where(same, v_dot_row, 0.0), axis=1, keepdims=True)
    grads[0] = (mm(u_hi, v) + mm(u_lo, v)) * iu - u.astype(F32) * (iu * iu * iu * u_dot / D)
    first = ((0,), (0,))
    grads[1] = (mm(v_hi, u, first) + mm(v_lo, u, first)) * iv - v.astype(F32) * (iv * iv * iv * v_dot / D)
    d_emb[:, :NDP] = grads[0].astype(BF).reshape(NEX, NDP, D)
    d_emb[:, NDP:] = grads[1].astype(BF).reshape(NEX, NDP, D)
    raw = mm(d_emb[...].reshape(PT, D), wd[...], ((1,), (1,)))
    for k in range(FD // 128):
        q[k] = raw[:, 128 * k : 128 * (k + 1)]
    row = io((NDP, 1), 0)
    near = pl.ds(pl.multiple_of(me[1] * NDP, NDP), NDP)
    for kind in range(2):
        dy[kind : kind + 1] = jnp.sum(jnp.where(row == me[0], grads[kind, near, :], 0.0), axis=0, keepdims=True)


def slope_kernel(off, me, q, act, slope, cols, dpre, dgl, dact, partial):
    src = (me[0] + off) % NDP
    qb = jnp.concatenate([q[k, pl.ds(src, LOCAL, stride=NDP), :] for k in range(FD // 128)], axis=1).astype(BF)
    pick = (io((ROWS, LOCAL), 1).astype(F32) == cols[:, 2:3]).astype(BF)
    dact[...] = mm(pick, qb)

    for c in range(0, ROWS, CHUNK):
        at = pl.ds(c, CHUNK)
        da = dact[at, :] * cols[at, 0:1]
        dpre[at, :] = (da * slope[at, :].astype(F32)).astype(BF)
        prod = da * act[at, :].astype(F32)
        partial[at, :] = prod[:, :128] + prod[:, 128:256] + prod[:, 256:384] + prod[:, 384:]
    dgl[...] = jnp.broadcast_to(jnp.sum(partial[...], axis=1, keepdims=True) * cols[:, 1:2], (ROWS, 128))


def slope_block(off, me, q, saved):
    _, _, act, slope, cols, _ = saved
    return run(
        functools.partial(slope_kernel, off),
        (shape(ROWS, FD), shape(ROWS, 128, dtype=F32)),
        me,
        q,
        act,
        slope,
        cols,
        smem=1,
        scratch=[pltpu.VMEM((ROWS, FD), F32), pltpu.VMEM((ROWS, 128), F32)],
        name="expert_slope",
    )


def half_value(upper, x, dpre, dgl, wu, router):
    rows = slice(0, CUT) if upper else slice(CUT, ROWS)
    col = dgl[rows, 0:1]
    v = mm(dpre[rows], wu[...], ((1,), (1,))) + col * router[...]
    xf = x[:CUT].astype(F32)
    return v, jnp.sum(xf * col, axis=0, keepdims=True), jnp.sum(xf * v, axis=0, keepdims=True)


def back_far_kernel(added, x_a_hbm, x_b_hbm, dpre_a, dgl_a, dpre_b, dgl_b, wu, router, *refs):
    got_a, got_b = refs[:2] if added else (None, None)
    out_a, out_b, sums, x_a, x_b, sems = refs[2 if added else 0 :]
    loads = [pltpu.make_async_copy(x_a_hbm, x_a, sems.at[0]), pltpu.make_async_copy(x_b_hbm, x_b, sems.at[1])]
    for copy in loads:
        copy.start()
    col_a = dgl_a[:CUT, 0:1]
    col_b = dgl_b[CUT:, 0:1]
    v_a = mm(dpre_a[:CUT], wu[...], ((1,), (1,))) + col_a * router[...]
    v_b = mm(dpre_b[CUT:], wu[...], ((1,), (1,))) + col_b * router[...]
    out_a[...] = (v_a + got_a[...].astype(F32) if added else v_a).astype(BF)
    out_b[...] = (v_b + got_b[...].astype(F32) if added else v_b).astype(BF)
    for copy in loads:
        copy.wait()
    xf_a = x_a[:CUT].astype(F32)
    xf_b = x_b[:CUT].astype(F32)
    sums[0:1] = jnp.sum(xf_a * col_a, axis=0, keepdims=True) + jnp.sum(xf_b * col_b, axis=0, keepdims=True)
    sums[1:2] = jnp.sum(xf_a * v_a, axis=0, keepdims=True) + jnp.sum(xf_b * v_b, axis=0, keepdims=True)


def back_add_kernel(x_a, dpre_a, dgl_a, x_b, dpre_b, dgl_b, wu, router, got_a, got_b, out_a, out_b, sums):
    v_a, r_a, g_a = half_value(True, x_a, dpre_a, dgl_a, wu, router)
    v_b, r_b, g_b = half_value(False, x_b, dpre_b, dgl_b, wu, router)
    out_a[...] = (v_a + got_a[...].astype(F32)).astype(BF)
    out_b[...] = (v_b + got_b[...].astype(F32)).astype(BF)
    sums[0:1] = r_a + r_b
    sums[1:2] = g_a + g_b


def back_near_kernel(top, low, dpre, dgl, wu, router, out, sums):
    v_a, r_a, g_a = half_value(True, top, dpre, dgl, wu, router)
    v_b, r_b, g_b = half_value(False, low, dpre, dgl, wu, router)
    out[:CUT] = v_a
    out[CUT:] = v_b
    sums[0:1] = r_a + r_b
    sums[1:2] = g_a + g_b


def add_kernel(near_r, near_l, ra, rb, la, lb, r, l):
    for near, got_a, got_b, out in ((near_r, ra, rb, r), (near_l, la, lb, l)):
        out[:CUT] = (near[:CUT] + got_a[...].astype(F32)).astype(BF)
        out[CUT:] = (near[CUT:] + got_b[...].astype(F32)).astype(BF)


def back_sums_kernel(top, low, dpre, dgl, wu, router, sums):
    _, r_a, g_a = half_value(True, top, dpre, dgl, wu, router)
    _, r_b, g_b = half_value(False, low, dpre, dgl, wu, router)
    sums[0:1] = r_a + r_b
    sums[1:2] = g_a + g_b


def total_kernel(*refs):
    out = refs[-1]
    total = refs[0][...]
    for ref in refs[1:-1]:
        total = total + ref[...]
    out[...] = jnp.broadcast_to(total[None], (NDP, 2, D))


SUMS = shape(2, D, dtype=F32)


def back_pair(far, block_a, slope_a, block_b, slope_b, wu, router, got=()):
    outs = (shape(CUT, D), shape(CUT, D), SUMS)
    if far:
        return run(
            functools.partial(back_far_kernel, bool(got)),
            outs,
            block_a[0],
            block_b[1],
            *slope_a,
            *slope_b,
            wu,
            router,
            *got,
            hbm=2,
            scratch=[pltpu.VMEM((CUT + META, D), BF), pltpu.VMEM((CUT + META, D), BF), pltpu.SemaphoreType.DMA((2,))],
            name="back_far",
        )
    return run(back_add_kernel, outs, block_a[0], *slope_a, block_b[1], *slope_b, wu, router, *got, name="back_pair")


def back_own_kernel(dpre, dgl, wu, router, out):
    out[...] = mm(dpre[...], wu[...], ((1,), (1,))) + dgl[:, 0:1] * router[...]


def back_last_kernel(r_hbm, l_hbm, own, small, send, r, l, sems):
    loads = [pltpu.make_async_copy(r_hbm, r, sems.at[0]), pltpu.make_async_copy(l_hbm, l, sems.at[1])]
    for copy in loads:
        copy.start()
    total = jnp.sum(small[...], axis=0)
    sub = io((MAIN, 128), 0) % 8
    for n in range(2):
        value = jnp.zeros((MAIN, 128), F32)
        for k in range(8):
            value = jnp.where(sub == k, total[n : n + 1, 128 * k : 128 * (k + 1)], value)
        send[:, EXTRA + 128 * n : EXTRA + 128 * (n + 1)] = value.astype(BF)
    for copy in loads:
        copy.wait()
    v = (own[...] + r[...].astype(F32) + l[...].astype(F32)).astype(BF)
    send[:, :D] = v[:MAIN]
    last = v[MAIN:]
    fold = mm(spread(0), last[:, :128])
    for k in range(1, 8):
        fold = fold + mm(spread(k), last[:, 128 * k : 128 * (k + 1)])
    send[:, FOLD:EXTRA] = fold.astype(BF)


def weight_kernel(*refs):
    tops, lows, dpres = (refs[NDP * k : NDP * (k + 1)] for k in range(3))
    grad_up = refs[3 * NDP]
    step_cols = 256

    def step(c, _):
        at = pl.ds(pl.multiple_of(c * step_cols, step_cols), step_cols)
        total = None
        for n in range(NDP):
            x = jnp.concatenate([tops[n][:CUT, at], lows[n][:CUT, at]], axis=0)
            term = mm(x, dpres[n][...], ((0,), (0,)))
            total = term if total is None else total + term
        grad_up[at, :] = total
        return 0

    lax.fori_loop(0, D // step_cols, step, 0)


def down_kernel(pooled, d_emb, out):
    out[...] = mm(pooled[...], d_emb[...].reshape(PT, D), ((0,), (0,)))


def final_kernel(length, tok_hbm, place_hbm, gain, got, dy, grad_tokens, grad_router, gain_grad, tok, place, sems):
    n = length[0]
    load_place = pltpu.make_async_copy(place_hbm, place, sems.at[0])
    load_tok = pltpu.make_async_copy(tok_hbm, tok, sems.at[1])
    load_place.start()
    load_tok.start()
    fold = got[:, FOLD:EXTRA]
    ones = [mm(spread(k), fold, ((0,), (0,))).astype(BF) for k in range(8)]
    last = jnp.concatenate(ones, axis=1)
    for k in range(8):
        at_k = slice(128 * k, 128 * (k + 1))
        piece = mm(spread(k), got[:, EXTRA:], ((0,), (0,)))
        grad_router[:, at_k] = piece[:, :128]
        gain_grad[:, at_k] = jnp.sum(piece[:, 128:], axis=0, keepdims=True) / gain[:, at_k]
    load_place.wait()
    dxn = mm(place[:MAIN], got[:, :D], ((0,), (0,))) + mm(place[MAIN:], last, ((0,), (0,)))
    load_tok.wait()
    xhat, rstd = layer_norm(tok[...].astype(F32))
    at = io((SEQ, 1), 0)
    w_img = jnp.where(at < PATCH, 1.0 / PATCH, 0.0)
    w_cap = jnp.where((at >= PATCH) & (at < PATCH + n), 1.0 / n.astype(F32), 0.0)
    g = dxn * gain[...]
    inner = jnp.sum(g * xhat, axis=1, keepdims=True) / D
    dx = (g - jnp.mean(g, axis=1, keepdims=True) - xhat * inner) * rstd
    grad_tokens[...] = (dx + w_img * dy[0:1] + w_cap * dy[1:2]).astype(BF)


def weight_grads(saved, dpres, offsets):
    return run(
        weight_kernel,
        shape(D, FD, dtype=F32),
        *[saved[off][0] for off in offsets],
        *[saved[off][1] for off in offsets],
        *dpres,
        name="weight_grads",
        limit=12,
    )


def exchange(value, axis):
    return lax.all_to_all(value, axis, split_axis=0, concat_axis=0, tiled=True)


def body(tokens, expert_ids, caption_lengths, gain, router, w_up, w_down, logit_scale, logit_bias):
    me_dp = lax.axis_index("dp").astype(I32)
    me_ex = lax.axis_index("expert").astype(I32)
    me = jnp.stack([me_dp, me_ex])
    wu = w_up[0]
    wd = w_down[0]
    tok = tokens[0]
    gain_row = gain.reshape(1, D)
    send, means, place = run(
        front_kernel,
        (shape(MAIN, SEND_W), shape(2, D, dtype=F32), shape(ROWS, SEQ)),
        caption_lengths,
        tok,
        expert_ids.reshape(1, SEQ),
        gain_row,
        smem=1,
        name="front",
        hbm=3,
        scratch=[
            pltpu.VMEM((SEQ, D), BF),
            pltpu.VMEM((1, SEQ), I32),
            pltpu.VMEM((1, D), F32),
            pltpu.SemaphoreType.DMA((3,)),
        ],
    )
    got = exchange(send.reshape(NEX, 8, SEND_W), "expert").reshape(MAIN, SEND_W)
    top, low = run(unpack_kernel, (shape(CUT + META, D), shape(CUT + META, D)), got, name="unpack")

    right = [(i, (i + 1) % NDP) for i in range(NDP)]
    left = [(i, (i - 1) % NDP) for i in range(NDP)]
    half = NDP // 2
    router_row = jnp.sum(jnp.where(jnp.arange(NEX, dtype=I32)[None, :] == me_ex, router, 0.0), axis=1).reshape(1, D)
    to_right = functools.partial(lax.ppermute, axis_name="dp", perm=right)
    to_left = functools.partial(lax.ppermute, axis_name="dp", perm=left)
    ra, la, rb, lb = top, top, low, low
    saved = {}
    pin = lax.optimization_barrier
    blocks = {0: (top, low)}

    def forward(off):
        saved[off] = forward_block(*blocks[off], wu, router_row)
        return saved[off]

    pinned_first = {2: 0, 3: -1, 4: -2}
    pinned_second = {3: 1}
    for k in range(1, half + 1):
        if k in pinned_first:
            off = pinned_first[k]
            ra, lb, saved[off] = pin((ra, lb, forward(off)))
        ra, lb = pin((to_right(ra), to_left(lb)))
        if k < half:
            if k in pinned_second:
                off = pinned_second[k]
                rb, la, saved[off] = pin((rb, la, forward(off)))
            rb, la = pin((to_right(rb), to_left(la)))
            blocks[-k] = (ra, rb)
            blocks[k] = (la, lb)
    forward(2)
    blocks[half] = (ra, lb)
    late = {off: blocks[off] for off in (1 - half, half - 1, half)}
    saved, part, pooled = forward_last(me, saved, late, wu, wd, router_row)
    offsets = list(saved)
    part = exchange(part.reshape(NEX, 2 * NDP, D), "expert")
    column = run(column_kernel, shape(NDP, 2 * NDP, D), me, part, means, smem=1, name="column")
    column = exchange(column, "dp")
    shared = run(share_kernel, shape(NEX, 2 * NDP, D), column, name="share")
    emb = exchange(shared, "expert")
    loss, d_emb, dy, q = run(
        loss_kernel,
        (shape(1, 1, dtype=F32), shape(NEX, 2 * NDP, D), shape(2, D, dtype=F32), shape(FD // 128, PT, 128, dtype=F32)),
        me,
        logit_scale,
        logit_bias,
        emb,
        wd,
        smem=3,
        scratch=[pltpu.VMEM((2, PT // 2, D), F32)],
        limit=16,
        name="pair_loss",
    )

    slopes = {off: slope_block(off, me, q, saved[off]) for off in (half, half - 1, 1 - half, 2, -2, 1, -1, 0)}
    sums = []

    def pair(a, b, got=()):
        out = back_pair(a in late, saved[a], slopes[a], saved[b], slopes[b], wu, router_row, got)
        sums.append(out[2])
        return out[:2]

    def near(off):
        v, part_sums = run(
            back_near_kernel, (shape(ROWS, D, dtype=F32), SUMS), *saved[off][:2], *slopes[off], wu, router_row, name="back_near"
        )
        sums.append(part_sums)
        return v

    ra, lb = pair(half, half)
    la, rb = pair(1 - half, half - 1)
    for k in range(half - 1, 0, -1):
        ra, lb = pin((to_right(ra), to_left(lb)))
        if k > 1:
            rb, la = pin((to_right(rb), to_left(la)))
            ra, lb = pair(k, -k, (ra, lb))
        if k > 2:
            la, rb = pair(1 - k, k - 1, (la, rb))
    nears = {off: near(off) for off in (1, -1)}
    sums.append(run(back_sums_kernel, SUMS, *saved[0][:2], *slopes[0], wu, router_row, name="back_sums"))
    small = run(total_kernel, shape(NDP, 2, D, dtype=F32), *sums, name="total")
    r, l = run(add_kernel, (shape(ROWS, D), shape(ROWS, D)), nears[1], nears[-1], ra, rb, la, lb, name="back_add")
    r, l, small = pin((r, l, small))
    r, l = pin((to_right(r), to_left(l)))
    small = exchange(small, "dp")
    own_back = run(back_own_kernel, shape(ROWS, D, dtype=F32), *slopes[0], wu, router_row, name="back_own")
    send = run(back_last_kernel, shape(MAIN, BACK_W), r, l, own_back, small, hbm=2, scratch=[pltpu.VMEM((ROWS, D), BF), pltpu.VMEM((ROWS, D), BF), pltpu.SemaphoreType.DMA((2,))], name="back_last")
    send, dpres = pin((send, [slopes[off][0] for off in offsets]))
    grad_up = weight_grads(saved, dpres, offsets)
    grad_down = run(down_kernel, shape(FD, D, dtype=F32), pooled, d_emb, name="down_grad")
    got = exchange(send.reshape(NEX, 8, BACK_W), "expert").reshape(MAIN, BACK_W)
    grad_tokens, grad_router, gain_grad = run(
        final_kernel,
        (shape(SEQ, D), shape(NEX, D, dtype=F32), shape(1, D, dtype=F32)),
        caption_lengths,
        tok,
        place,
        gain_row,
        got,
        dy,
        smem=1,
        hbm=2,
        scratch=[pltpu.VMEM((SEQ, D), BF), pltpu.VMEM((ROWS, SEQ), BF), pltpu.SemaphoreType.DMA((2,))],
        name="final",
    )
    return (loss.reshape(1), grad_tokens[None], grad_up[None], grad_down[None], grad_router.T, gain_grad.reshape(D))


def solution(mesh):
    return jax.shard_map(
        body,
        mesh=mesh,
        in_specs=(
            P(("dp", "expert"), None, None),
            P(("dp", "expert"), None, None),
            P(("dp", "expert")),
            P(),
            P(),
            P("expert", None, "dp"),
            P("expert", "dp", None),
            P(),
            P(),
        ),
        out_specs=(
            P(),
            P(("dp", "expert"), None, None),
            P("expert", None, "dp"),
            P("expert", "dp", None),
            P(),
            P(),
        ),
        check_vma=False,
    )
```

```python
import functools

import jax
import jax.numpy as jnp
from jax import lax
from jax.experimental import pallas as pl
from jax.experimental.pallas import tpu as pltpu
from jax.sharding import PartitionSpec as P

D = 1024
FD = 512
PATCH = 196
CAPLEN = 16
SEQ = 212
NDP = 8
NEX = 32
MAIN = NEX * 8
ROWS = NEX * 9
META = 8
HEIGHT = ROWS + META
CUT = ROWS // 2
LANES = 384
FOLD = D
EXTRA = D + 128
SEND_W = D + 256
BACK_W = D + 384
PT = 2 * NDP * NEX
LOCAL = 2 * NEX

EPS = 1e-06
LOSS_SCALE = 1024.0
BF = jnp.bfloat16
F32 = jnp.float32
I32 = jnp.int32

VM = pl.BlockSpec(memory_space=pltpu.VMEM)
SM = pl.BlockSpec(memory_space=pltpu.SMEM)


def mm(a, b, dims=((1,), (0,))):
    return lax.dot_general(a, b, (dims, ((), ())), preferred_element_type=F32)


def io(shape, axis):
    return lax.broadcasted_iota(I32, shape, axis)


HB = pl.BlockSpec(memory_space=pltpu.HBM)


def run(kernel, outs, *args, smem=0, scratch=(), name=None, limit=6, hbm=0, spill=()):
    specs = [SM] * smem + [HB] * hbm + [VM] * (len(args) - smem - hbm)
    many = isinstance(outs, tuple)
    kinds = [n in spill for n in range(len(outs) if many else 1)]
    out_specs = tuple(HB if k else VM for k in kinds) if many else VM
    if many:
        outs = tuple(pltpu.HBM(o.shape, o.dtype) if k else o for o, k in zip(outs, kinds))
    args = tuple(pltpu.with_memory_space_constraint(a, pltpu.HBM) if smem <= n < smem + hbm else a for n, a in enumerate(args))
    return pl.pallas_call(
        kernel,
        out_shape=outs,
        in_specs=specs,
        out_specs=out_specs,
        scratch_shapes=scratch,
        name=name,
        cost_estimate=pl.CostEstimate(flops=1024, transcendentals=0, bytes_accessed=1024),
        compiler_params=pltpu.CompilerParams(vmem_limit_bytes=limit * 1024 * 1024),
    )(*args)


def shape(*dims, dtype=BF):
    return jax.ShapeDtypeStruct(dims, dtype)


def spread(k):
    return (io((MAIN, NEX), 0) == io((MAIN, NEX), 1) * 8 + k).astype(BF)


def layer_norm(x):
    mean = jnp.mean(x, axis=1, keepdims=True)
    c = x - mean
    rstd = 1.0 / jnp.sqrt(jnp.mean(c * c, axis=1, keepdims=True) + EPS)
    return c * rstd, rstd


def front_kernel(length, tok_hbm, ids_hbm, gain_hbm, send, means, place, tok, ids, gain, sems):
    copies = [
        pltpu.make_async_copy(src, dst, sems.at[k])
        for k, (src, dst) in enumerate(((tok_hbm, tok), (ids_hbm, ids), (gain_hbm, gain)))
    ]
    for copy in copies:
        copy.start()
    for copy in copies:
        copy.wait()
    n = length[0]
    x = tok[...].astype(F32)
    xhat, _ = layer_norm(x)
    xn = (xhat * gain[...]).astype(BF)
    pos = io((1, SEQ), 1)
    real = pos < PATCH + n
    owner = ids[...]
    hit = (io((NEX, SEQ), 0) == owner) & real
    onehot = jnp.where(hit, 1.0, 0.0)
    before = (io((SEQ, SEQ), 0) < io((SEQ, SEQ), 1)).astype(BF)
    slot = jnp.sum(mm(onehot.astype(BF), before) * onehot, axis=0, keepdims=True).astype(I32)
    target = jnp.where(real & (slot < 8), owner * 8 + slot, -1)
    p_main = (io((MAIN, SEQ), 0) == target).astype(BF)
    p_last = jnp.where(slot == 8, onehot, 0.0).astype(BF)
    place[:MAIN] = p_main
    place[MAIN:] = p_last
    send[:, :D] = mm(p_main, xn).astype(BF)
    last = mm(p_last, xn).astype(BF)
    fold = mm(spread(0), last[:, :128])
    for k in range(1, 8):
        fold = fold + mm(spread(k), last[:, 128 * k : 128 * (k + 1)])
    send[:, FOLD:EXTRA] = fold.astype(BF)
    images = jnp.sum(jnp.where(pos < PATCH, onehot, 0.0), axis=1, keepdims=True)
    lane = io((NEX, 128), 1)
    info = jnp.where(lane == 0, images, jnp.where(lane == 1, n.astype(F32), 0.0)).astype(BF)
    send[:, EXTRA:] = mm(spread(0), info).astype(BF)
    at = io((SEQ, 1), 0)
    w_img = jnp.where(at < PATCH, 1.0 / PATCH, 0.0)
    w_cap = jnp.where((at >= PATCH) & (at < PATCH + n), 1.0 / n.astype(F32), 0.0)
    means[0:1] = jnp.sum(x * w_img, axis=0, keepdims=True)
    means[1:2] = jnp.sum(x * w_cap, axis=0, keepdims=True)


def unpack_kernel(got, top, low):
    top[:CUT] = got[:CUT, :D]
    low[: MAIN - CUT] = got[CUT:, :D]
    info = mm(spread(0), got[:, EXTRA:SEND_W], ((0,), (0,)))
    fold = got[:, FOLD:EXTRA]
    for k in range(8):
        low[MAIN - CUT : CUT, 128 * k : 128 * (k + 1)] = mm(spread(k), fold, ((0,), (0,))).astype(BF)
    r = io((1, LANES), 1)
    ex = jnp.where(r < MAIN, r // 8, r - MAIN)
    slot = jnp.where(r < MAIN, r % 8, 8).astype(F32)
    match = io((NEX, LANES), 0) == ex
    images = jnp.sum(jnp.where(match, info[:, 0:1], 0.0), axis=0, keepdims=True)
    lens = jnp.sum(jnp.where(match, info[:, 1:2], 0.0), axis=0, keepdims=True)
    is_img = slot < images
    pt = jnp.where(r < ROWS, 2 * ex + jnp.where(is_img, 0, 1), LOCAL).astype(F32)
    div = jnp.where(r < ROWS, jnp.where(is_img, float(PATCH), lens), 1.0)
    for ref, info_row in ((top, pt), (low, div)):
        ref[CUT:, :LANES] = jnp.broadcast_to(info_row, (META, LANES)).astype(BF)
        ref[CUT:, LANES:] = jnp.zeros((META, D - LANES), BF)


CHUNK = 96


def phi_of(p):
    return 0.5 * (1.0 + lax.erf(p * 0.7071067811865476))


def slope_of(p, phi):
    return (phi + p * jnp.exp(-0.5 * p * p) * 0.3989422804014327).astype(BF)


def late_slope_kernel(*refs):
    n = len(refs) // 2
    for pre, slope in zip(refs[:n], refs[n:]):

        def step(c, _, pre=pre, slope=slope):
            at = pl.ds(pl.multiple_of(c * CHUNK, CHUNK), CHUNK)
            p = pre[at, :]
            slope[at, :] = slope_of(p, phi_of(p))
            return 0

        lax.fori_loop(0, ROWS // CHUNK, step, 0)


def forward_core(top, low, wu, router, act, slope, cols, pre, mixed):
    pre[:CUT] = mm(top[:CUT], wu[...])
    pre[CUT:] = mm(low[:CUT], wu[...])
    pt_row = top[CUT:, :LANES].astype(F32)[0:1]
    div_row = low[CUT:, :LANES].astype(F32)[0:1]

    def gates(c, _):
        at = pl.ds(pl.multiple_of(c * 48, 48), 48)
        for ref, base in ((top, 0), (low, CUT)):
            prod = ref[at, :].astype(F32) * router[...]
            t = prod[:, :128]
            for k in range(1, 8):
                t = t + prod[:, 128 * k : 128 * (k + 1)]
            cols[pl.ds(pl.multiple_of(c * 48 + base, 48), 48), :] = t
        return 0

    lax.fori_loop(0, CUT // 48, gates, 0)
    gate = jax.nn.sigmoid(jnp.sum(cols[...], axis=1, keepdims=True))
    diag = io((ROWS, LANES), 1) == io((ROWS, LANES), 0)
    div = jnp.sum(jnp.where(diag, div_row, 0.0), axis=1, keepdims=True)
    pt = jnp.sum(jnp.where(diag, pt_row, 0.0), axis=1, keepdims=True)
    lane = io((ROWS, 128), 1)
    cols[...] = jnp.where(lane == 0, gate / div, jnp.where(lane == 1, 1.0 - gate, jnp.where(lane == 2, pt, 0.0)))

    def step(c, _):
        at = pl.ds(pl.multiple_of(c * CHUNK, CHUNK), CHUNK)
        p = pre[at, :]
        phi = phi_of(p)
        a = (p * phi).astype(BF)
        act[at, :] = a
        if slope is not None:
            slope[at, :] = slope_of(p, phi)
        mixed[at, :] = (cols[at, 0:1] * a.astype(F32)).astype(BF)
        return 0

    lax.fori_loop(0, ROWS // CHUNK, step, 0)
    return (io((LOCAL, ROWS), 0).astype(F32) == pt_row[:, :ROWS]).astype(BF)


def forward_kernel(top, low, wu, router, act_out, slope_out, cols_out, pooled_out, act, slope, cols, pooled, pre, mixed, sems):
    sel = forward_core(top, low, wu, router, act, slope, cols, pre, mixed)
    outs = ((act, act_out), (slope, slope_out), (cols, cols_out), (pooled, pooled_out))
    copies = [pltpu.make_async_copy(src, dst, sems.at[k]) for k, (src, dst) in enumerate(outs)]
    for copy in copies[:3]:
        copy.start()
    pooled[...] = mm(sel, mixed[...]).astype(BF)
    copies[3].start()
    for copy in copies:
        copy.wait()


def keep_shapes():
    return (shape(ROWS, FD), shape(ROWS, FD), shape(ROWS, 128, dtype=F32))


def keep_scratch():
    return [pltpu.VMEM((ROWS, FD), BF), pltpu.VMEM((ROWS, FD), BF), pltpu.VMEM((ROWS, 128), F32)]


def forward_block(top, low, wu, router):
    out = run(
        forward_kernel,
        keep_shapes() + (shape(LOCAL, FD),),
        top,
        low,
        wu,
        router,
        scratch=keep_scratch()
        + [
            pltpu.VMEM((LOCAL, FD), BF),
            pltpu.VMEM((ROWS, FD), F32),
            pltpu.VMEM((ROWS, FD), BF),
            pltpu.SemaphoreType.DMA((4,)),
        ],
        name="expert_forward",
        spill=(0, 1, 2, 3),
    )
    return (top, low) + tuple(out)


def forward_last_kernel(offsets, late, me, *refs):
    n_late = len(late)
    early = refs[: NDP - n_late]
    refs = refs[NDP - n_late :]
    xs, refs = refs[: 2 * n_late], refs[2 * n_late :]
    wu, wd, router = refs[:3]
    outs, refs = refs[3 : 3 + 3 * n_late], refs[3 + 3 * n_late :]
    part, pooled_out = refs[:2]
    held, refs = refs[2 : 2 + 3 * n_late], refs[2 + 3 * n_late :]
    near, pooled, mixed, total, rows, sems = refs
    first = 3 * n_late + 1 + len(early)
    fetch = [pltpu.make_async_copy(ref, rows.at[n], sems.at[first + n]) for n, ref in enumerate(xs)]
    for copy in fetch:
        copy.start()
    copies = []
    loads = [pltpu.make_async_copy(ref, near.at[n], sems.at[3 * n_late + 1 + n]) for n, ref in enumerate(early)]
    for copy in loads:
        copy.start()
    for n in list(range(len(early), NDP)) + list(range(len(early))):
        if n < len(early):
            loads[n].wait()
            value = near[n]
        else:
            m = n - len(early)
            keep = held[3 * m : 3 * m + 3]
            act, pre, cols = keep
            fetch[2 * m].wait()
            fetch[2 * m + 1].wait()
            sel = forward_core(rows.at[2 * m], rows.at[2 * m + 1], wu, router, act, None, cols, pre, mixed)
            for k in range(3):
                copies.append(pltpu.make_async_copy(keep[k], outs[3 * m + k], sems.at[3 * m + k]))
                copies[-1].start()
            value = mm(sel, mixed[...])
        src = (me[0] + offsets[n]) % NDP
        value = value.astype(F32)
        for k in range(FD // 128):
            total[k, pl.ds(src, LOCAL, stride=NDP), :] = value[:, 128 * k : 128 * (k + 1)]
    for k in range(FD // 128):
        pooled[:, 128 * k : 128 * (k + 1)] = total[k].astype(BF)
    copies.append(pltpu.make_async_copy(pooled, pooled_out, sems.at[3 * n_late]))
    copies[-1].start()
    part[...] = mm(pooled[...], wd[...]).astype(BF)
    for copy in copies:
        copy.wait()


def forward_last(me, early, late, wu, wd, router):
    offsets = list(early) + list(late)
    n_late = len(late)
    out = run(
        functools.partial(forward_last_kernel, offsets, list(late)),
        (shape(ROWS, FD), shape(ROWS, FD, dtype=F32), shape(ROWS, 128, dtype=F32)) * n_late + (shape(PT, D), shape(PT, FD)),
        me,
        *[value[5] for value in early.values()],
        *[half for pair in late.values() for half in pair],
        wu,
        wd,
        router,
        smem=1,
        scratch=[pltpu.VMEM((ROWS, FD), BF), pltpu.VMEM((ROWS, FD), F32), pltpu.VMEM((ROWS, 128), F32)] * n_late
        + [
            pltpu.VMEM((len(early), LOCAL, FD), BF),
            pltpu.VMEM((PT, FD), BF),
            pltpu.VMEM((ROWS, FD), BF),
            pltpu.VMEM((FD // 128, PT, 128), F32),
            pltpu.VMEM((2 * n_late, CUT + META, D), BF),
            pltpu.SemaphoreType.DMA((5 * n_late + 1 + len(early),)),
        ],
        name="forward_last",
        hbm=len(early) + 2 * n_late,
        limit=14,
        spill=tuple(range(3 * n_late)) + (3 * n_late + 1,),
    )
    saved = dict(early)
    slopes = run(late_slope_kernel, (shape(ROWS, FD),) * n_late, *out[1 : 3 * n_late : 3], name="late_slope")
    for n, off in enumerate(late):
        saved[off] = tuple(late[off]) + (out[3 * n], slopes[n], out[3 * n + 2], None)
    return saved, out[3 * n_late], out[3 * n_late + 1]


def column_kernel(me, got, means, out):
    s = jnp.sum(got[...].astype(F32), axis=0)
    row = io((2 * NDP, 1), 0)
    s = s + jnp.where(row == me[0], means[0:1], 0.0) + jnp.where(row == me[0] + NDP, means[1:2], 0.0)
    out[...] = jnp.broadcast_to(s.astype(BF)[None], (NDP, 2 * NDP, D))


def share_kernel(got, out):
    s = jnp.sum(got[...].astype(F32), axis=0)
    out[...] = jnp.broadcast_to(s.astype(BF)[None], (NEX, 2 * NDP, D))


def loss_kernel(me, scale, bias, emb, wd, loss, d_emb, dy, q, grads):
    n = PT // 2
    u = emb[:, :NDP].reshape(n, D)
    v = emb[:, NDP:].reshape(n, D)
    dots = mm(u, v, ((1,), (1,)))
    i = io((n, n), 0)
    j = io((n, n), 1)
    same = i == j

    def norms(a):
        on = jnp.where(same, mm(a, a, ((1,), (1,))), 0.0)
        col = 1.0 / jnp.sqrt(jnp.sum(on, axis=1, keepdims=True) / D + EPS)
        row = 1.0 / jnp.sqrt(jnp.sum(on, axis=0, keepdims=True) / D + EPS)
        return col, row

    iu, iu_row = norms(u)
    iv, iv_row = norms(v)
    to_unit = scale[0] / D
    sign = jnp.where(same, 1.0, -1.0)
    z = sign * (dots * to_unit * iu * iv_row + bias[0])
    t = jnp.exp(-jnp.abs(z))
    soft = jnp.maximum(-z, 0.0) + jnp.log1p(t)
    loss[...] = jnp.sum(jnp.sum(soft, axis=0, keepdims=True), axis=1, keepdims=True) / n
    coef = (-LOSS_SCALE / n) * sign * (jnp.where(z >= 0.0, t, 1.0) / (1.0 + t)) * to_unit
    for_u = coef * iv_row
    for_v = coef * iu

    def halves(c):
        hi = c.astype(BF)
        return hi, (c - hi.astype(F32)).astype(BF)

    u_hi, u_lo = halves(for_u)
    v_hi, v_lo = halves(for_v)
    u_dot = jnp.sum(for_u * dots, axis=1, keepdims=True)
    v_dot_row = jnp.sum(for_v * dots, axis=0, keepdims=True)
    v_dot = jnp.sum(jnp.where(same, v_dot_row, 0.0), axis=1, keepdims=True)
    grads[0] = (mm(u_hi, v) + mm(u_lo, v)) * iu - u.astype(F32) * (iu * iu * iu * u_dot / D)
    first = ((0,), (0,))
    grads[1] = (mm(v_hi, u, first) + mm(v_lo, u, first)) * iv - v.astype(F32) * (iv * iv * iv * v_dot / D)
    d_emb[:, :NDP] = grads[0].astype(BF).reshape(NEX, NDP, D)
    d_emb[:, NDP:] = grads[1].astype(BF).reshape(NEX, NDP, D)
    raw = mm(d_emb[...].reshape(PT, D), wd[...], ((1,), (1,)))
    for k in range(FD // 128):
        q[k] = raw[:, 128 * k : 128 * (k + 1)]
    row = io((NDP, 1), 0)
    near = pl.ds(pl.multiple_of(me[1] * NDP, NDP), NDP)
    for kind in range(2):
        dy[kind : kind + 1] = jnp.sum(jnp.where(row == me[0], grads[kind, near, :], 0.0), axis=0, keepdims=True)


def slope_kernel(off, me, q, act, slope, cols, dpre, dgl, dact, partial):
    src = (me[0] + off) % NDP
    qb = jnp.concatenate([q[k, pl.ds(src, LOCAL, stride=NDP), :] for k in range(FD // 128)], axis=1).astype(BF)
    pick = (io((ROWS, LOCAL), 1).astype(F32) == cols[:, 2:3]).astype(BF)
    dact[...] = mm(pick, qb)

    for c in range(0, ROWS, CHUNK):
        at = pl.ds(c, CHUNK)
        da = dact[at, :] * cols[at, 0:1]
        dpre[at, :] = (da * slope[at, :].astype(F32)).astype(BF)
        prod = da * act[at, :].astype(F32)
        partial[at, :] = prod[:, :128] + prod[:, 128:256] + prod[:, 256:384] + prod[:, 384:]
    dgl[...] = jnp.broadcast_to(jnp.sum(partial[...], axis=1, keepdims=True) * cols[:, 1:2], (ROWS, 128))


def slope_block(off, me, q, saved):
    _, _, act, slope, cols, _ = saved
    return run(
        functools.partial(slope_kernel, off),
        (shape(ROWS, FD), shape(ROWS, 128, dtype=F32)),
        me,
        q,
        act,
        slope,
        cols,
        smem=1,
        scratch=[pltpu.VMEM((ROWS, FD), F32), pltpu.VMEM((ROWS, 128), F32)],
        name="expert_slope",
    )


def half_value(upper, x, dpre, dgl, wu, router):
    rows = slice(0, CUT) if upper else slice(CUT, ROWS)
    col = dgl[rows, 0:1]
    v = mm(dpre[rows], wu[...], ((1,), (1,))) + col * router[...]
    xf = x[:CUT].astype(F32)
    return v, jnp.sum(xf * col, axis=0, keepdims=True), jnp.sum(xf * v, axis=0, keepdims=True)


def back_far_kernel(added, x_a_hbm, x_b_hbm, dpre_a, dgl_a, dpre_b, dgl_b, wu, router, *refs):
    got_a, got_b = refs[:2] if added else (None, None)
    out_a, out_b, sums, x_a, x_b, sems = refs[2 if added else 0 :]
    loads = [pltpu.make_async_copy(x_a_hbm, x_a, sems.at[0]), pltpu.make_async_copy(x_b_hbm, x_b, sems.at[1])]
    for copy in loads:
        copy.start()
    col_a = dgl_a[:CUT, 0:1]
    col_b = dgl_b[CUT:, 0:1]
    v_a = mm(dpre_a[:CUT], wu[...], ((1,), (1,))) + col_a * router[...]
    v_b = mm(dpre_b[CUT:], wu[...], ((1,), (1,))) + col_b * router[...]
    out_a[...] = (v_a + got_a[...].astype(F32) if added else v_a).astype(BF)
    out_b[...] = (v_b + got_b[...].astype(F32) if added else v_b).astype(BF)
    for copy in loads:
        copy.wait()
    xf_a = x_a[:CUT].astype(F32)
    xf_b = x_b[:CUT].astype(F32)
    sums[0:1] = jnp.sum(xf_a * col_a, axis=0, keepdims=True) + jnp.sum(xf_b * col_b, axis=0, keepdims=True)
    sums[1:2] = jnp.sum(xf_a * v_a, axis=0, keepdims=True) + jnp.sum(xf_b * v_b, axis=0, keepdims=True)


def back_add_kernel(x_a, dpre_a, dgl_a, x_b, dpre_b, dgl_b, wu, router, got_a, got_b, out_a, out_b, sums):
    v_a, r_a, g_a = half_value(True, x_a, dpre_a, dgl_a, wu, router)
    v_b, r_b, g_b = half_value(False, x_b, dpre_b, dgl_b, wu, router)
    out_a[...] = (v_a + got_a[...].astype(F32)).astype(BF)
    out_b[...] = (v_b + got_b[...].astype(F32)).astype(BF)
    sums[0:1] = r_a + r_b
    sums[1:2] = g_a + g_b


def back_near_kernel(top, low, dpre, dgl, wu, router, out, sums):
    v_a, r_a, g_a = half_value(True, top, dpre, dgl, wu, router)
    v_b, r_b, g_b = half_value(False, low, dpre, dgl, wu, router)
    out[:CUT] = v_a
    out[CUT:] = v_b
    sums[0:1] = r_a + r_b
    sums[1:2] = g_a + g_b


def add_kernel(near_r, near_l, ra, rb, la, lb, r, l):
    for near, got_a, got_b, out in ((near_r, ra, rb, r), (near_l, la, lb, l)):
        out[:CUT] = (near[:CUT] + got_a[...].astype(F32)).astype(BF)
        out[CUT:] = (near[CUT:] + got_b[...].astype(F32)).astype(BF)


def back_sums_kernel(top, low, dpre, dgl, wu, router, sums):
    _, r_a, g_a = half_value(True, top, dpre, dgl, wu, router)
    _, r_b, g_b = half_value(False, low, dpre, dgl, wu, router)
    sums[0:1] = r_a + r_b
    sums[1:2] = g_a + g_b


def total_kernel(*refs):
    out = refs[-1]
    total = refs[0][...]
    for ref in refs[1:-1]:
        total = total + ref[...]
    out[...] = jnp.broadcast_to(total[None], (NDP, 2, D))


SUMS = shape(2, D, dtype=F32)


def back_pair(far, block_a, slope_a, block_b, slope_b, wu, router, got=()):
    outs = (shape(CUT, D), shape(CUT, D), SUMS)
    if far:
        return run(
            functools.partial(back_far_kernel, bool(got)),
            outs,
            block_a[0],
            block_b[1],
            *slope_a,
            *slope_b,
            wu,
            router,
            *got,
            hbm=2,
            scratch=[pltpu.VMEM((CUT + META, D), BF), pltpu.VMEM((CUT + META, D), BF), pltpu.SemaphoreType.DMA((2,))],
            name="back_far",
        )
    return run(back_add_kernel, outs, block_a[0], *slope_a, block_b[1], *slope_b, wu, router, *got, name="back_pair")


def back_own_kernel(dpre, dgl, wu, router, out):
    out[...] = mm(dpre[...], wu[...], ((1,), (1,))) + dgl[:, 0:1] * router[...]


def back_last_kernel(r_hbm, l_hbm, own, small, send, r, l, sems):
    loads = [pltpu.make_async_copy(r_hbm, r, sems.at[0]), pltpu.make_async_copy(l_hbm, l, sems.at[1])]
    for copy in loads:
        copy.start()
    total = jnp.sum(small[...], axis=0)
    sub = io((MAIN, 128), 0) % 8
    for n in range(2):
        value = jnp.zeros((MAIN, 128), F32)
        for k in range(8):
            value = jnp.where(sub == k, total[n : n + 1, 128 * k : 128 * (k + 1)], value)
        send[:, EXTRA + 128 * n : EXTRA + 128 * (n + 1)] = value.astype(BF)
    for copy in loads:
        copy.wait()
    v = (own[...] + r[...].astype(F32) + l[...].astype(F32)).astype(BF)
    send[:, :D] = v[:MAIN]
    last = v[MAIN:]
    fold = mm(spread(0), last[:, :128])
    for k in range(1, 8):
        fold = fold + mm(spread(k), last[:, 128 * k : 128 * (k + 1)])
    send[:, FOLD:EXTRA] = fold.astype(BF)


def weight_kernel(*refs):
    tops, lows, dpres = (refs[NDP * k : NDP * (k + 1)] for k in range(3))
    grad_up = refs[3 * NDP]
    step_cols = 256

    def step(c, _):
        at = pl.ds(pl.multiple_of(c * step_cols, step_cols), step_cols)
        total = None
        for n in range(NDP):
            x = jnp.concatenate([tops[n][:CUT, at], lows[n][:CUT, at]], axis=0)
            term = mm(x, dpres[n][...], ((0,), (0,)))
            total = term if total is None else total + term
        grad_up[at, :] = total
        return 0

    lax.fori_loop(0, D // step_cols, step, 0)


def down_kernel(pooled, d_emb, out):
    out[...] = mm(pooled[...], d_emb[...].reshape(PT, D), ((0,), (0,)))


def final_kernel(length, tok_hbm, place_hbm, gain, got, dy, grad_tokens, grad_router, gain_grad, tok, place, sems):
    n = length[0]
    load_place = pltpu.make_async_copy(place_hbm, place, sems.at[0])
    load_tok = pltpu.make_async_copy(tok_hbm, tok, sems.at[1])
    load_place.start()
    load_tok.start()
    fold = got[:, FOLD:EXTRA]
    ones = [mm(spread(k), fold, ((0,), (0,))).astype(BF) for k in range(8)]
    last = jnp.concatenate(ones, axis=1)
    for k in range(8):
        at_k = slice(128 * k, 128 * (k + 1))
        piece = mm(spread(k), got[:, EXTRA:], ((0,), (0,)))
        grad_router[:, at_k] = piece[:, :128]
        gain_grad[:, at_k] = jnp.sum(piece[:, 128:], axis=0, keepdims=True) / gain[:, at_k]
    load_place.wait()
    dxn = mm(place[:MAIN], got[:, :D], ((0,), (0,))) + mm(place[MAIN:], last, ((0,), (0,)))
    load_tok.wait()
    xhat, rstd = layer_norm(tok[...].astype(F32))
    at = io((SEQ, 1), 0)
    w_img = jnp.where(at < PATCH, 1.0 / PATCH, 0.0)
    w_cap = jnp.where((at >= PATCH) & (at < PATCH + n), 1.0 / n.astype(F32), 0.0)
    g = dxn * gain[...]
    inner = jnp.sum(g * xhat, axis=1, keepdims=True) / D
    dx = (g - jnp.mean(g, axis=1, keepdims=True) - xhat * inner) * rstd
    grad_tokens[...] = (dx + w_img * dy[0:1] + w_cap * dy[1:2]).astype(BF)


def weight_grads(saved, dpres, offsets):
    return run(
        weight_kernel,
        shape(D, FD, dtype=F32),
        *[saved[off][0] for off in offsets],
        *[saved[off][1] for off in offsets],
        *dpres,
        name="weight_grads",
        limit=12,
    )


def exchange(value, axis):
    return lax.all_to_all(value, axis, split_axis=0, concat_axis=0, tiled=True)


def body(tokens, expert_ids, caption_lengths, gain, router, w_up, w_down, logit_scale, logit_bias):
    me_dp = lax.axis_index("dp").astype(I32)
    me_ex = lax.axis_index("expert").astype(I32)
    me = jnp.stack([me_dp, me_ex])
    wu = w_up[0]
    wd = w_down[0]
    tok = tokens[0]
    gain_row = gain.reshape(1, D)
    send, means, place = run(
        front_kernel,
        (shape(MAIN, SEND_W), shape(2, D, dtype=F32), shape(ROWS, SEQ)),
        caption_lengths,
        tok,
        expert_ids.reshape(1, SEQ),
        gain_row,
        smem=1,
        name="front",
        hbm=3,
        scratch=[
            pltpu.VMEM((SEQ, D), BF),
            pltpu.VMEM((1, SEQ), I32),
            pltpu.VMEM((1, D), F32),
            pltpu.SemaphoreType.DMA((3,)),
        ],
    )
    got = exchange(send.reshape(NEX, 8, SEND_W), "expert").reshape(MAIN, SEND_W)
    top, low = run(unpack_kernel, (shape(CUT + META, D), shape(CUT + META, D)), got, name="unpack")

    right = [(i, (i + 1) % NDP) for i in range(NDP)]
    left = [(i, (i - 1) % NDP) for i in range(NDP)]
    half = NDP // 2
    router_row = jnp.sum(jnp.where(jnp.arange(NEX, dtype=I32)[None, :] == me_ex, router, 0.0), axis=1).reshape(1, D)
    to_right = functools.partial(lax.ppermute, axis_name="dp", perm=right)
    to_left = functools.partial(lax.ppermute, axis_name="dp", perm=left)
    ra, la, rb, lb = top, top, low, low
    saved = {}
    pin = lax.optimization_barrier
    blocks = {0: (top, low)}

    def forward(off):
        saved[off] = forward_block(*blocks[off], wu, router_row)
        return saved[off]

    pinned_first = {2: 0, 3: -1, 4: -2}
    pinned_second = {3: 1}
    for k in range(1, half + 1):
        if k in pinned_first:
            off = pinned_first[k]
            ra, lb, saved[off] = pin((ra, lb, forward(off)))
        ra, lb = pin((to_right(ra), to_left(lb)))
        if k < half:
            if k in pinned_second:
                off = pinned_second[k]
                rb, la, saved[off] = pin((rb, la, forward(off)))
            rb, la = pin((to_right(rb), to_left(la)))
            blocks[-k] = (ra, rb)
            blocks[k] = (la, lb)
    forward(2)
    blocks[half] = (ra, lb)
    late = {off: blocks[off] for off in (1 - half, half - 1, half)}
    saved, part, pooled = forward_last(me, saved, late, wu, wd, router_row)
    offsets = list(saved)
    part = exchange(part.reshape(NEX, 2 * NDP, D), "expert")
    column = run(column_kernel, shape(NDP, 2 * NDP, D), me, part, means, smem=1, name="column")
    column = exchange(column, "dp")
    shared = run(share_kernel, shape(NEX, 2 * NDP, D), column, name="share")
    emb = exchange(shared, "expert")
    loss, d_emb, dy, q = run(
        loss_kernel,
        (shape(1, 1, dtype=F32), shape(NEX, 2 * NDP, D), shape(2, D, dtype=F32), shape(FD // 128, PT, 128, dtype=F32)),
        me,
        logit_scale,
        logit_bias,
        emb,
        wd,
        smem=3,
        scratch=[pltpu.VMEM((2, PT // 2, D), F32)],
        limit=16,
        name="pair_loss",
    )

    slopes = {off: slope_block(off, me, q, saved[off]) for off in (half, half - 1, 1 - half, 2, -2, 1, -1, 0)}
    sums = []

    def pair(a, b, got=()):
        out = back_pair(a in late, saved[a], slopes[a], saved[b], slopes[b], wu, router_row, got)
        sums.append(out[2])
        return out[:2]

    def near(off):
        v, part_sums = run(
            back_near_kernel, (shape(ROWS, D, dtype=F32), SUMS), *saved[off][:2], *slopes[off], wu, router_row, name="back_near"
        )
        sums.append(part_sums)
        return v

    ra, lb = pair(half, half)
    la, rb = pair(1 - half, half - 1)
    for k in range(half - 1, 0, -1):
        ra, lb = pin((to_right(ra), to_left(lb)))
        if k > 1:
            rb, la = pin((to_right(rb), to_left(la)))
            ra, lb = pair(k, -k, (ra, lb))
        if k > 2:
            la, rb = pair(1 - k, k - 1, (la, rb))
    nears = {off: near(off) for off in (1, -1)}
    sums.append(run(back_sums_kernel, SUMS, *saved[0][:2], *slopes[0], wu, router_row, name="back_sums"))
    small = run(total_kernel, shape(NDP, 2, D, dtype=F32), *sums, name="total")
    r, l = run(add_kernel, (shape(ROWS, D), shape(ROWS, D)), nears[1], nears[-1], ra, rb, la, lb, name="back_add")
    r, l, small = pin((r, l, small))
    r, l = pin((to_right(r), to_left(l)))
    small = exchange(small, "dp")
    own_back = run(back_own_kernel, shape(ROWS, D, dtype=F32), *slopes[0], wu, router_row, name="back_own")
    send = run(back_last_kernel, shape(MAIN, BACK_W), r, l, own_back, small, hbm=2, scratch=[pltpu.VMEM((ROWS, D), BF), pltpu.VMEM((ROWS, D), BF), pltpu.SemaphoreType.DMA((2,))], name="back_last")
    send, dpres = pin((send, [slopes[off][0] for off in offsets]))
    grad_up = weight_grads(saved, dpres, offsets)
    grad_down = run(down_kernel, shape(FD, D, dtype=F32), pooled, d_emb, name="down_grad")
    got = exchange(send.reshape(NEX, 8, BACK_W), "expert").reshape(MAIN, BACK_W)
    grad_tokens, grad_router, gain_grad = run(
        final_kernel,
        (shape(SEQ, D), shape(NEX, D, dtype=F32), shape(1, D, dtype=F32)),
        caption_lengths,
        tok,
        place,
        gain_row,
        got,
        dy,
        smem=1,
        hbm=2,
        scratch=[pltpu.VMEM((SEQ, D), BF), pltpu.VMEM((ROWS, SEQ), BF), pltpu.SemaphoreType.DMA((2,))],
        name="final",
    )
    return (loss.reshape(1), grad_tokens[None], grad_up[None], grad_down[None], grad_router.T, gain_grad.reshape(D))


def solution(mesh):
    return jax.shard_map(
        body,
        mesh=mesh,
        in_specs=(
            P(("dp", "expert"), None, None),
            P(("dp", "expert"), None, None),
            P(("dp", "expert")),
            P(),
            P(),
            P("expert", None, "dp"),
            P("expert", "dp", None),
            P(),
            P(),
        ),
        out_specs=(
            P(),
            P(("dp", "expert"), None, None),
            P("expert", None, "dp"),
            P("expert", "dp", None),
            P(),
            P(),
        ),
        check_vma=False,
    )
```
